32 devices in a mesh: shard: 2 (over y), context: 4 (over z), tensor: 4 (over x, core).
Axes of the slice: x: 2, y: 2, z: 4, core: 2. Of those that a mesh axis runs over, the one named last changes fastest.
Arguments:
- inputs: bfloat16 [6, 2048, 768], P('shard', 'context'), may hold values from -6 to 6
- w_query: bfloat16 [768, 768], P('shard', 'tensor'), may hold values from -0.21875 to 0.21875
- b_query: float32 [768], P('tensor'), may hold values from -3 to 3
- w_key: bfloat16 [768, 768], P('shard', 'tensor'), may hold values from -0.21875 to 0.21875
- w_value: bfloat16 [768, 768], P('shard', 'tensor'), may hold values from -0.21875 to 0.21875
- b_value: float32 [768], P('tensor'), may hold values from -3 to 3
- w_out: bfloat16 [768, 768], P('tensor', 'shard'), may hold values from -3.5 to 3.5
- b_out: float32 [768], replicated, may hold values from -3 to 3
- first_gain: float32 [768], replicated, may hold values from 0.5 to 1.5
- first_bias: float32 [768], replicated, may hold values from -2 to 2
- w_hidden: bfloat16 [768, 3072], P('shard', 'tensor'), may hold values from -0.21875 to 0.21875
- b_hidden: float32 [3072], P('tensor'), may hold values from -3 to 3
- w_down: bfloat16 [3072, 768], P('tensor', 'shard'), may hold values from -0.109375 to 0.109375
- b_down: float32 [768], replicated, may hold values from -3 to 3
- second_gain: float32 [768], replicated, may hold values from 0.5 to 1.5
- second_bias: float32 [768], replicated, may hold values from -2 to 2
- cotangent: bfloat16 [6, 2048, 768], P('shard', 'context'), may hold values from -6 to 6
Outputs:
- outputs: bfloat16 [6, 2048, 768], P('shard', 'context')
- input_grad: bfloat16 [6, 2048, 768], P('shard', 'context')
- grad_w_query: float32 [768, 768], P('shard', 'tensor')
- grad_b_query: float32 [768], P('tensor')
- grad_w_key: float32 [768, 768], P('shard', 'tensor')
- grad_w_value: float32 [768, 768], P('shard', 'tensor')
- grad_b_value: float32 [768], P('tensor')
- grad_w_out: float32 [768, 768], P('tensor', 'shard')
- grad_b_out: float32 [768], replicated
- grad_first_gain: float32 [768], replicated
- grad_first_bias: float32 [768], replicated
- grad_w_hidden: float32 [768, 3072], P('shard', 'tensor')
- grad_b_hidden: float32 [3072], P('tensor')
- grad_w_down: float32 [3072, 768], P('tensor', 'shard')
- grad_b_down: float32 [768], replicated
- grad_second_gain: float32 [768], replicated
- grad_second_bias: float32 [768], replicated
The draws below stay inside these ranges and needn't reach their ends.
All inputs are finite; a program needn't handle non-finite values.
Results may differ from the reference program's by a relative error of at most 0.018.
Values may be sent and summed in bfloat16 or wider, within the bound.
No kernel may reach another device: no remote copies, remote signals or barrier semaphores. Data moves between devices by JAX's collectives and lax.ppermute only.
A program may use at most 256 MiB of HBM per device.

```python
import jax
import jax.numpy as jnp
from jax import lax

D = 768
HEADS = 12
HEAD_DIM = 64
FF = 3072
LENGTH = 2048
SEQS = 6


def level_of(own_key, shape, split, low, high):
    def one(position, blocks):
        draws = jax.random.uniform(jax.random.fold_in(jax.random.fold_in(own_key, 6), position), (blocks,), jnp.float32, low / len(split), high / len(split))
        return jnp.repeat(jnp.exp(draws), shape[position] // blocks).reshape((-1,) + (1,) * (len(shape) - position - 1))

    loudness = one(*split[0])
    for cut in split[1:]:
        loudness = loudness * one(*cut)
    return loudness


def normal_values(key, shape, scale, bound, pieces=(), dtype=jnp.bfloat16):
    values = scale * jax.random.normal(key, shape, jnp.float32)
    if pieces:
        values = values * level_of(key, shape, pieces, -0.22, 0.18)
    return jnp.clip(values, -bound, bound).astype(dtype)


def setup_inputs(seed: int = 0) -> dict:
    seeds = jax.random.split(jax.random.key(seed), 18)
    inputs = normal_values(seeds[0], (SEQS, LENGTH, D), 1.0, 6.0, ((0, 2), (1, 4)))
    w_query = normal_values(seeds[1], (D, D), D ** -0.5, 0.21875, ((0, 2), (1, 4)))
    b_query = normal_values(seeds[2], (D,), 0.5, 3.0, ((0, 4),), jnp.float32)
    w_key = normal_values(seeds[3], (D, D), D ** -0.5, 0.21875, ((0, 2), (1, 4)))
    w_value = normal_values(seeds[4], (D, D), D ** -0.5, 0.21875, ((0, 2), (1, 4)))
    b_value = normal_values(seeds[5], (D,), 0.5, 3.0, ((0, 4),), jnp.float32)
    w_out = normal_values(seeds[6], (D, D), (max(1, D * 8 // LENGTH)) ** -0.5, 3.5, ((0, 4), (1, 2)))
    b_out = normal_values(seeds[7], (D,), 0.5, 3.0, (), jnp.float32)
    first_gain = jnp.clip(1.0 + 0.1 * jax.random.normal(seeds[8], (D,), jnp.float32), 0.5, 1.5)
    first_bias = normal_values(seeds[9], (D,), 0.3, 2.0, (), jnp.float32)
    w_hidden = normal_values(seeds[10], (D, FF), D ** -0.5, 0.21875, ((0, 2), (1, 4)))
    b_hidden = normal_values(seeds[11], (FF,), 0.5, 3.0, ((0, 4),), jnp.float32)
    w_down = normal_values(seeds[12], (FF, D), FF ** -0.5, 0.109375, ((0, 4), (1, 2)))
    b_down = normal_values(seeds[13], (D,), 0.5, 3.0, (), jnp.float32)
    second_gain = jnp.clip(1.0 + 0.1 * jax.random.normal(seeds[14], (D,), jnp.float32), 0.5, 1.5)
    second_bias = normal_values(seeds[15], (D,), 0.3, 2.0, (), jnp.float32)
    cotangent = normal_values(seeds[16], (SEQS, LENGTH, D), 1.0, 6.0, ((0, 2), (1, 4)))
    return dict(inputs=inputs, w_query=w_query, b_query=b_query, w_key=w_key, w_value=w_value, b_value=b_value, w_out=w_out, b_out=b_out, first_gain=first_gain, first_bias=first_bias, w_hidden=w_hidden, b_hidden=b_hidden, w_down=w_down, b_down=b_down, second_gain=second_gain, second_bias=second_bias, cotangent=cotangent)


@jax.custom_vjp
def low(v):
    return lax.optimization_barrier(v.astype(jnp.bfloat16)).astype(jnp.float32)

@jax.custom_vjp
def low_back(v):
    return v

def low_keep(v):
    return (low(v), None)

def low_pass(kept, grad):
    return (grad,)

def back_keep(v):
    return (v, None)

def back_low(kept, grad):
    return (low(grad),)
low.defvjp(low_keep, low_pass)
low_back.defvjp(back_keep, back_low)
EPSILON = 1e-05

def matmul(left, right):
    return jnp.dot(left, right, precision=lax.Precision.HIGHEST, preferred_element_type=jnp.float32)

def layer_norm(values, gain, bias):
    centre = lax.optimization_barrier(jnp.mean(values, axis=-1, keepdims=True))
    centred = values - centre
    spread = lax.optimization_barrier(jnp.mean(centred * centred, axis=-1, keepdims=True))
    return centred * lax.rsqrt(spread + EPSILON) * gain + bias

def layer(rows_in, w_query, b_query, w_key, w_value, b_value, w_out, b_out, first_gain, first_bias, w_hidden, b_hidden, w_down, b_down, second_gain, second_bias):
    length = rows_in.shape[0]
    query = low_back(low(matmul(rows_in, w_query) + b_query)).reshape(length, HEADS, HEAD_DIM)
    key = low_back(low(matmul(rows_in, w_key))).reshape(length, HEADS, HEAD_DIM)
    value = low_back(low(matmul(rows_in, w_value) + b_value)).reshape(length, HEADS, HEAD_DIM)
    scores = jnp.einsum('qhd,khd->hqk', query, key, precision=lax.Precision.HIGHEST, preferred_element_type=jnp.float32) * HEAD_DIM ** (-0.5)
    scores = low_back(scores)
    probs = low(jax.nn.softmax(scores, axis=-1))
    attended = jnp.einsum('hqk,khd->qhd', probs, value, precision=lax.Precision.HIGHEST, preferred_element_type=jnp.float32).reshape(length, D)
    attended = low_back(low(attended))
    branch = low_back(matmul(attended, w_out))
    first = layer_norm(rows_in + branch + b_out, first_gain, first_bias)
    inner = low_back(matmul(low(first), w_hidden) + b_hidden)
    activated = low(jax.nn.gelu(inner, approximate=False))
    ffn = low_back(matmul(activated, w_down))
    return layer_norm(first + ffn + b_down, second_gain, second_bias)

def reference(inputs, w_query, b_query, w_key, w_value, b_value, w_out, b_out, first_gain, first_bias, w_hidden, b_hidden, w_down, b_down, second_gain, second_bias, cotangent):
    params = tuple((a.astype(jnp.float32) for a in (w_query, b_query, w_key, w_value, b_value, w_out, b_out, first_gain, first_bias, w_hidden, b_hidden, w_down, b_down, second_gain, second_bias)))

    def one_sequence(totals, pair):
        rows_in, grad_out = pair
        result, backward = jax.vjp(layer, rows_in, *params)
        grads = backward(grad_out)
        totals = tuple((t + g for t, g in zip(totals, grads[1:])))
        return (totals, (result.astype(jnp.bfloat16), grads[0].astype(jnp.bfloat16)))
    start = tuple((jnp.zeros(a.shape, jnp.float32) for a in params))
    totals, (results, input_grads) = lax.scan(one_sequence, start, (inputs.astype(jnp.float32), cotangent.astype(jnp.float32)))
    return (results, input_grads, totals[0], totals[1], totals[2], totals[3], totals[4], totals[5], totals[6], totals[7], totals[8], totals[9], totals[10], totals[11], totals[12], totals[13], totals[14])
```

```python
import functools
import jax
import jax.numpy as jnp
from jax import lax
from jax.experimental import pallas as pl
from jax.experimental.pallas import tpu as pltpu
from jax.sharding import PartitionSpec as P

HEAD_DIM = 64
EPSILON = 1e-05
F32 = jnp.float32
BF16 = jnp.bfloat16
VMEM_LIMIT = 56 << 20


def nn(a, b):
    return jnp.dot(a, b, preferred_element_type=F32)


def nt(a, b):
    return lax.dot_general(a, b, (((1,), (1,)), ((), ())), preferred_element_type=F32)


def head_lanes(shape, head):
    lane = lax.broadcasted_iota(jnp.int32, shape, len(shape) - 1)
    return (lane >= head * HEAD_DIM) & (lane < (head + 1) * HEAD_DIM)


def divisor(size, most):
    while size % most:
        most //= 2
    return most


def forward_body(heads, own, near, cross, sib, w_four, b_query, b_value, query, key, value, attended, log_total, keep, send):
    part, width = own.shape
    cols = heads * HEAD_DIM
    factor = HEAD_DIM**-0.5
    w_query, w_key, w_value, w_out = (w_four.at[i] for i in range(4))
    query[...] = ((nn(own[...], w_query[...]) + b_query[...]).astype(BF16).astype(F32) * factor).astype(BF16)
    row = 0
    for piece in (own, near, cross, sib):
        size = piece.shape[0]
        step = divisor(size, 256)

        def project(i, carry, piece=piece, row=row, step=step):
            rows = piece[pl.ds(i * step, step), :]
            out = pl.ds(row + i * step, step)
            key[out, :] = nn(rows, w_key[...]).astype(BF16)
            value[out, :] = (nn(rows, w_value[...]) + b_value[...]).astype(BF16)
            return carry

        lax.fori_loop(0, size // step, project, 0)
        row += size
    block = divisor(part, 128)
    lanes = lax.broadcasted_iota(jnp.int32, (block, 128), 1)

    def attend(i, carry):
        rows = pl.ds(pl.multiple_of(i * block, block), block)
        mine = query[rows, :].astype(F32)
        result = jnp.zeros((block, cols), F32)
        stats = jnp.zeros((block, 128), F32)
        for head in range(heads):
            mask = head_lanes((block, cols), head)
            masked = jnp.where(mask, mine, 0.0).astype(BF16)
            scores = nt(masked, key[...])
            top = jnp.max(scores, axis=-1, keepdims=True)
            powers = jnp.exp(scores - top)
            total = jnp.sum(powers, axis=-1, keepdims=True)
            mixed = nn(powers.astype(BF16), value[...])
            result = jnp.where(mask, mixed / total, result)
            stats = jnp.where(lanes == head, top + jnp.log(total), stats)
        attended[rows, :] = result.astype(BF16)
        turned = stats.T
        log_total[:, rows] = turned[:8, :]
        return carry

    lax.fori_loop(0, part // block, attend, 0)
    half = part // 2
    keep[...] = nt(attended[:half, :], w_out[...]).astype(BF16)
    send[...] = nt(attended[half:, :], w_out[...]).astype(BF16)


def backward_body(heads, nears, g_own, g_cross, g_sib, w_four, query, key, value, attended, log_total,
                  d_query, d_key, d_value, keep, send, d_out, sums, q_heads, g_heads, dq_turned):
    part, cols = query.shape
    width = w_four.shape[1]
    total = key.shape[0]
    quarter = part // 4
    factor = HEAD_DIM**-0.5
    w_query, w_key, w_value, w_out = (w_four.at[i] for i in range(4))
    grad = jnp.concatenate([g_own[...], g_cross[...], g_sib[...]], axis=0)
    grad_heads = nn(grad, w_out[...]).astype(BF16)
    att = attended[...]
    d_out[...] = nn(att.T, grad)
    product = grad_heads.astype(F32) * att.astype(F32)
    picks = jnp.concatenate(
        [jnp.where(head_lanes((1, cols), h), 1.0, 0.0) for h in range(heads)]
        + [jnp.zeros((8 - heads, cols), F32)], axis=0)
    weighted = lax.dot_general(picks, product, (((1,), (1,)), ((), ())), precision=lax.Precision.HIGHEST,
                               preferred_element_type=F32)
    for h in range(heads):
        mask = head_lanes((part, cols), h)
        q_heads[h] = jnp.where(mask, query[...].astype(F32), 0.0).astype(BF16)
        g_heads[h] = jnp.where(mask, grad_heads.astype(F32), 0.0).astype(BF16)
    dq_turned[...] = jnp.zeros_like(dq_turned)
    block = divisor(total, 256)

    def chunk(i, carry):
        rows = pl.ds(pl.multiple_of(i * block, block), block)
        keys = key[rows, :]
        values = value[rows, :]
        keys_turned = keys.T
        dk = jnp.zeros((block, cols), F32)
        dv = jnp.zeros((block, cols), F32)
        for h in range(heads):
            scores = nt(keys, q_heads[h])
            probs = jnp.exp(scores - log_total[h : h + 1, :])
            d_probs = nt(values, g_heads[h])
            d_scores = (probs * (d_probs - weighted[h : h + 1, :])).astype(BF16)
            dv = dv + nn(probs.astype(BF16), g_heads[h])
            dk = dk + nn(d_scores, q_heads[h])
            own = slice(h * HEAD_DIM, (h + 1) * HEAD_DIM)
            dq_turned[own, :] += nn(keys_turned[own, :], d_scores)
        d_key[rows, :] = dk.astype(BF16)
        d_value[rows, :] = dv.astype(BF16)
        return carry + jnp.sum(dv.astype(BF16).astype(F32), axis=0, keepdims=True)

    sum_value = lax.fori_loop(0, total // block, chunk, jnp.zeros((1, cols), F32))
    dq = (dq_turned[...] * factor).T.astype(BF16)
    d_query[...] = dq
    sums[...] = jnp.concatenate(
        [jnp.sum(dq.astype(F32), axis=0, keepdims=True), sum_value, jnp.zeros((6, cols), F32)], axis=0)

    def back(begin, size):
        rows = slice(begin, begin + size)
        return nt(d_key[rows, :], w_key[...]) + nt(d_value[rows, :], w_value[...])

    away = nears
    row = part
    for out, first in ((keep, 0), (send, 2)):
        for j in range(2):
            slot = first + j
            mine = slice(slot * quarter, (slot + 1) * quarter)
            begin = j * (quarter + away)
            out[begin : begin + quarter, :] = (back(slot * quarter, quarter) + nt(dq[mine, :], w_query[...])).astype(BF16)
            out[begin + quarter : begin + quarter + away, :] = back(row, away).astype(BF16)
            row += away


def vmem(n):
    return [pl.BlockSpec(memory_space=pltpu.VMEM)] * n


def attention_forward(own, near, cross, sib, w_four, b_query, b_value):
    part, width = own.shape
    cols = w_four.shape[-1]
    heads = cols // HEAD_DIM
    total = part + near.shape[0] + cross.shape[0] + sib.shape[0]
    shape = jax.ShapeDtypeStruct
    return pl.pallas_call(
        functools.partial(forward_body, heads),
        out_shape=(
            shape((part, cols), BF16),
            shape((total, cols), BF16),
            shape((total, cols), BF16),
            shape((part, cols), BF16),
            shape((8, part), F32),
            shape((part // 2, width), BF16),
            shape((part // 2, width), BF16),
        ),
        in_specs=vmem(7),
        out_specs=vmem(7),
        compiler_params=pltpu.CompilerParams(vmem_limit_bytes=VMEM_LIMIT),
        cost_estimate=pl.CostEstimate(
            flops=2 * total * width * 2 * cols + 4 * heads * 4 * part * total * HEAD_DIM,
            bytes_accessed=2 * (total * width + 3 * total * cols),
            transcendentals=heads * part * total,
        ),
        name="attention_forward",
    )(own, near, cross, sib, w_four, b_query, b_value)


def attention_backward(g_own, g_cross, g_sib, w_four, query, key, value, attended, log_total):
    part, cols = query.shape
    width = w_four.shape[1]
    heads = cols // HEAD_DIM
    total = key.shape[0]
    nears = (total - part) // 4
    shape = jax.ShapeDtypeStruct
    return pl.pallas_call(
        functools.partial(backward_body, heads, nears),
        out_shape=(
            shape((part, cols), BF16),
            shape((total, cols), BF16),
            shape((total, cols), BF16),
            shape((total // 2, width), BF16),
            shape((total // 2, width), BF16),
            shape((cols, width), F32),
            shape((8, cols), F32),
        ),
        in_specs=vmem(9),
        out_specs=vmem(7),
        scratch_shapes=[
            pltpu.VMEM((heads, part, cols), BF16),
            pltpu.VMEM((heads, part, cols), BF16),
            pltpu.VMEM((cols, part), F32),
        ],
        compiler_params=pltpu.CompilerParams(vmem_limit_bytes=VMEM_LIMIT),
        cost_estimate=pl.CostEstimate(
            flops=2 * total * width * 2 * cols + 10 * heads * 4 * part * total * HEAD_DIM,
            bytes_accessed=2 * (total * width + 5 * total * cols),
            transcendentals=heads * part * total,
        ),
        name="attention_backward",
    )(g_own, g_cross, g_sib, w_four, query, key, value, attended, log_total)


def rows_mean(a):
    return jnp.mean(a, axis=-1, keepdims=True)


def norm(values):
    centred = values - rows_mean(values)
    inverse = lax.rsqrt(rows_mean(centred * centred) + EPSILON)
    return centred * inverse, inverse


def norm_back(scaled, normed, inverse):
    return inverse * (scaled - rows_mean(scaled) - normed * rows_mean(scaled * normed))


def col_sum(a):
    return jnp.sum(a, axis=0, keepdims=True)


def feed_body(blocks, pieces, *refs):
    weights = refs[: blocks * pieces]
    inputs, branch_a, branch_b, cotangent, b_hidden, vectors = refs[blocks * pieces : blocks * pieces + 6]
    (result, grad_attn, grad_low, grads_keep, grads_send, sums, sums_hidden,
     up, down, act, slope, turned, sems) = refs[blocks * pieces + 6 :]
    rows, width = inputs.shape
    hidden = up.shape[-1]
    depth = width // pieces
    copies = []
    for b in range(blocks):
        for p in range(pieces):
            source = weights[b * pieces + p]
            spot = pl.ds(p * depth, depth)
            copies.append(pltpu.make_async_copy(source.at[pl.ds(0, depth), :], up.at[b, spot, :], sems.at[b, p, 0]))
            copies.append(pltpu.make_async_copy(source.at[pl.ds(depth, depth), :], down.at[b, spot, :], sems.at[b, p, 1]))
    for copy in copies:
        copy.start()
    b_out, gain_one, bias_one, b_down, gain_two, bias_two = (vectors[i : i + 1, :] for i in range(6))
    pre = inputs[...].astype(F32) + (branch_a[...].astype(F32) + branch_b[...].astype(F32)) + b_out
    normed_one, inverse_one = norm(pre)
    first = normed_one * gain_one + bias_one
    first_low = first.astype(BF16)
    turned[...] = first_low.T
    for copy in copies:
        copy.wait()

    def ahead(b, total):
        inner = nn(first_low, up[b]) + b_hidden[pl.ds(b, 1), :]
        shape = 0.5 * (1.0 + lax.erf(inner * (0.5**0.5)))
        act_low = (inner * shape).astype(BF16)
        act[b] = act_low
        slope[b] = shape + inner * (jnp.exp(-0.5 * inner * inner) * 0.3989422804014327)
        return total + nt(act_low, down[b])

    ffn = lax.fori_loop(0, blocks, ahead, jnp.zeros((rows, width), F32))
    normed_two, inverse_two = norm(first + ffn + b_down)
    result[...] = (normed_two * gain_two + bias_two).astype(BF16)
    grad = cotangent[...].astype(F32)
    grad_second = norm_back(grad * gain_two, normed_two, inverse_two)
    grad_ffn = grad_second.astype(BF16)
    grad_turned = grad_ffn.T

    def astern(offset, grads):
        def step(i, total):
            b = i + offset
            grad_inner = (nn(grad_ffn, down[b]) * slope[b]).astype(BF16)
            sums_hidden[pl.ds(b, 1), :] = col_sum(grad_inner.astype(F32))
            up_grad = nn(turned[...], grad_inner).astype(BF16)
            down_grad = nn(grad_turned, act[b]).astype(BF16)
            for p in range(pieces):
                grads[i, p, :depth, :] = up_grad[p * depth : (p + 1) * depth, :]
                grads[i, p, depth:, :] = down_grad[p * depth : (p + 1) * depth, :]
            return total + nt(grad_inner, up[b])

        return step

    grad_first = lax.fori_loop(0, blocks // 2, astern(blocks // 2, grads_send), grad_second)
    grad_first = lax.fori_loop(0, blocks // 2, astern(0, grads_keep), grad_first)
    grad_pre = norm_back(grad_first * gain_one, normed_one, inverse_one)
    grad_low[...] = grad_pre
    grad_attn[...] = grad_pre.astype(BF16)
    sums[...] = jnp.concatenate(
        [col_sum(grad_pre), col_sum(grad_first * normed_one), col_sum(grad_first), col_sum(grad_second),
         col_sum(grad * normed_two), col_sum(grad), jnp.zeros((2, width), F32)], axis=0)


def feed_forward(weights, inputs, branch_a, branch_b, cotangent, b_hidden, vectors):
    blocks = len(weights)
    pieces = len(weights[0])
    rows, width = inputs.shape
    hidden = weights[0][0].shape[-1]
    depth = width // pieces
    shape = jax.ShapeDtypeStruct
    flat = [w for block in weights for w in block]
    return pl.pallas_call(
        functools.partial(feed_body, blocks, pieces),
        out_shape=(
            shape((rows, width), BF16),
            shape((rows, width), BF16),
            shape((rows, width), F32),
            shape((blocks // 2, pieces, 2 * depth, hidden), BF16),
            shape((blocks // 2, pieces, 2 * depth, hidden), BF16),
            shape((8, width), F32),
            shape((8, hidden), F32),
        ),
        in_specs=[pl.BlockSpec(memory_space=pl.ANY)] * len(flat) + vmem(6),
        out_specs=vmem(7),
        scratch_shapes=[
            pltpu.VMEM((blocks, width, hidden), BF16),
            pltpu.VMEM((blocks, width, hidden), BF16),
            pltpu.VMEM((blocks, rows, hidden), BF16),
            pltpu.VMEM((blocks, rows, hidden), F32),
            pltpu.VMEM((width, rows), BF16),
            pltpu.SemaphoreType.DMA((blocks, pieces, 2)),
        ],
        compiler_params=pltpu.CompilerParams(vmem_limit_bytes=VMEM_LIMIT),
        cost_estimate=pl.CostEstimate(
            flops=12 * rows * width * hidden * blocks,
            bytes_accessed=8 * width * hidden * blocks,
            transcendentals=2 * rows * hidden * blocks,
        ),
        name="feed_forward",
    )(*flat, inputs, branch_a, branch_b, cotangent, b_hidden, vectors)


def gradients_body(own, near, cross, sib, d_query, d_key, d_value, out):
    out[0] = nn(d_query[...].T, own[...])
    row = 0
    for index, piece in enumerate((own, near, cross, sib)):
        rows = slice(row, row + piece.shape[0])
        for slot, grad in ((1, d_key), (2, d_value)):
            part = nn(grad[rows, :].T, piece[...])
            if index == 0:
                out[slot] = part
            else:
                out[slot] += part
        row += piece.shape[0]


def attention_gradients(own, near, cross, sib, d_query, d_key, d_value):
    cols = d_query.shape[1]
    width = own.shape[1]
    total = d_key.shape[0]
    return pl.pallas_call(
        gradients_body,
        out_shape=jax.ShapeDtypeStruct((3, cols, width), F32),
        in_specs=vmem(7),
        out_specs=pl.BlockSpec(memory_space=pltpu.VMEM),
        compiler_params=pltpu.CompilerParams(vmem_limit_bytes=VMEM_LIMIT),
        cost_estimate=pl.CostEstimate(
            flops=4 * total * cols * width, bytes_accessed=2 * total * (width + 2 * cols), transcendentals=0
        ),
        name="attention_gradients",
    )(own, near, cross, sib, d_query, d_key, d_value)


def rotated(value, axis, count, shift):
    return lax.ppermute(value, axis, [(i, (i + shift) % count) for i in range(count)])


def across(value):
    return lax.ppermute(value, "tensor", [(i, i ^ 2) for i in range(4)])


def sibling(value):
    return lax.ppermute(value, "tensor", [(i, i ^ 1) for i in range(4)])


def roll_columns(value, place, count):
    if count == 2:
        half = value.shape[-1] // 2
        turned = jnp.concatenate([value[..., half:], value[..., :half]], axis=-1)
        return jnp.where(place == 1, turned, value)
    size = value.shape[-1] // count
    twice = jnp.concatenate([value, value], axis=-1)
    return lax.dynamic_slice_in_dim(twice, place * size, value.shape[-1], axis=-1)


def on_device(shards, contexts, inputs, w_query, b_query, w_key, w_value, b_value, w_out, b_out,
              first_gain, first_bias, w_hidden, b_hidden, w_down, b_down, second_gain, second_bias, cotangent):
    seqs, part, width = inputs.shape
    cols = w_query.shape[1]
    hidden = w_hidden.shape[1]
    quarter = part // 4
    depth = width // shards
    shard = lax.axis_index("shard")
    tensor = lax.axis_index("tensor")
    places = [tensor ^ flip for flip in (0, 2, 1, 3)]
    unplace = (shards - shard) % shards

    def to_rel(value):
        return roll_columns(value, shard, shards)

    def from_rel(value):
        return roll_columns(value, unplace, shards)

    def block_of(value, axis, index, size):
        return lax.dynamic_slice_in_dim(value, index * size, size, axis=axis)

    four = jnp.stack([w_query, w_key, w_value, w_out.T])
    two = jnp.concatenate([w_hidden, w_down.T], axis=0)
    own = to_rel(jnp.concatenate([block_of(inputs, 1, p, quarter) for p in places], axis=1))

    nears = []
    for s in range(seqs):
        mine = own[s, :quarter]
        nears.append([rotated(mine, "context", contexts, -r) for r in range(1, contexts)])
    four_all = jnp.concatenate(
        [four] + [rotated(four, "shard", shards, -r) for r in range(1, shards)], axis=1)
    two_cross = across(two)
    two_pieces = [two] + [rotated(two, "shard", shards, -r) for r in range(1, shards)]
    cross_pieces = [two_cross] + [rotated(two_cross, "shard", shards, -r) for r in range(1, shards)]
    b_hidden_all = lax.all_gather(b_hidden, "tensor", axis=0)
    b_hidden_rel = jnp.concatenate([block_of(b_hidden_all, 0, p, 1) for p in places], axis=0)
    vectors = to_rel(jnp.stack([b_out, first_gain, first_bias, b_down, second_gain, second_bias, b_out, b_out]))
    cot_own = to_rel(block_of(cotangent, 1, tensor, quarter)).reshape(seqs * quarter, width)

    kept = []
    sums_a = []
    sums_b = []
    for s in range(seqs):
        near = jnp.concatenate(nears[s], axis=0)
        cross = across(near)
        sib = sibling(jnp.concatenate([near, cross], axis=0))
        query, key, value, attended, log_total, keep, send = attention_forward(
            own[s], near, cross, sib, four_all, b_query[None], b_value[None])
        kept.append((near, cross, sib, query, key, value, attended, log_total))
        both = keep.astype(F32) + sibling(send).astype(F32)
        sums_a.append(both[:quarter].astype(BF16))
        sums_b.append(across(both[quarter:].astype(BF16)))
    pieces = [two_pieces, cross_pieces, [sibling(p) for p in two_pieces], [sibling(p) for p in cross_pieces]]
    result, grad_attn, grad_low, grads_keep, grads_send, sums, sums_hidden = feed_forward(
        pieces, own[:, :quarter].reshape(seqs * quarter, width),
        jnp.concatenate(sums_a, axis=0), jnp.concatenate(sums_b, axis=0), cot_own, b_hidden_rel, vectors)

    def whole(value):
        return lax.all_gather(from_rel(value).reshape(seqs, quarter, width), "tensor", axis=1, tiled=True)

    outputs = whole(result)

    feed = grads_keep.astype(F32) + sibling(grads_send).astype(F32)
    feed_own = feed[:, 0]
    for r in range(1, shards):
        feed_own = feed_own + rotated(feed[:, r].astype(BF16), "shard", shards, r).astype(F32)
    feed_sum = feed_own[0] + across(feed_own[1].astype(BF16)).astype(F32)
    feed_sum = lax.psum(feed_sum.astype(BF16), "context").astype(F32)

    totals = []
    outs = []
    column_sums = []
    grad_parts = []
    for s in range(seqs):
        g_own = grad_attn[s * quarter : (s + 1) * quarter]
        g_cross = across(g_own)
        g_sib = sibling(jnp.concatenate([g_own, g_cross], axis=0))
        near, cross, sib, query, key, value, attended, log_total = kept[s]
        d_query, d_key, d_value, keep, send, d_out, summed = attention_backward(
            g_own, g_cross, g_sib, four_all, query, key, value, attended, log_total)
        outs.append(d_out)
        column_sums.append(summed)
        grad_parts.append((own[s], near, cross, sib, d_query, d_key, d_value))
        both = keep.astype(F32) + sibling(send).astype(F32)
        half = both.shape[0] // 2
        total = both[:half] + across(both[half:].astype(BF16)).astype(F32)
        total = total.reshape(contexts, quarter, width)
        grad = grad_low[s * quarter : (s + 1) * quarter] + total[0]
        for r in range(1, contexts):
            grad = grad + rotated(total[r].astype(BF16), "context", contexts, r).astype(F32)
        totals.append(grad.astype(BF16))
    input_grad = whole(jnp.concatenate(totals, axis=0))

    projections = [attention_gradients(*p) for p in grad_parts]
    projected = jnp.concatenate(
        [sum(projections[1:], projections[0]), sum(outs[1:], outs[0])[None]], axis=0)
    attn_sum = projected[:, :, :depth]
    for r in range(1, shards):
        away = projected[:, :, r * depth : (r + 1) * depth].astype(BF16)
        attn_sum = attn_sum + rotated(away, "shard", shards, r).astype(F32)
    attn_sum = lax.psum(attn_sum.astype(BF16), "context").astype(F32)

    summed = sum(column_sums[1:], column_sums[0])[:2]
    spread = lax.dynamic_update_slice(jnp.zeros((2, 4, cols), F32), summed[:, None], (0, tensor, 0))
    hidden_abs = jnp.concatenate([block_of(sums_hidden, 0, order, 1) for order in
                                  [(((tensor ^ t) & 2) >> 1) + (((tensor ^ t) & 1) << 1) for t in range(4)]], axis=0)
    packed = jnp.concatenate([from_rel(sums)[:6].reshape(-1), hidden_abs.reshape(-1), spread.reshape(-1)])
    packed = lax.psum(packed, ("shard", "context", "tensor"))
    wide = packed[: 6 * width].reshape(6, width)
    at = 6 * width
    grad_b_hidden = block_of(packed[at : at + 4 * hidden], 0, tensor, hidden)
    at += 4 * hidden
    grad_b_query = block_of(packed[at : at + 4 * cols], 0, tensor, cols)
    at += 4 * cols
    grad_b_value = block_of(packed[at : at + 4 * cols], 0, tensor, cols)
    return (
        outputs,
        input_grad,
        attn_sum[0].T,
        grad_b_query,
        attn_sum[1].T,
        attn_sum[2].T,
        grad_b_value,
        attn_sum[3],
        wide[0],
        wide[1],
        wide[2],
        feed_sum[:depth],
        grad_b_hidden,
        feed_sum[depth:].T,
        wide[3],
        wide[4],
        wide[5],
    )


def solution(mesh):
    shards = mesh.shape["shard"]
    contexts = mesh.shape["context"]
    rows = P("shard", "context", None)
    into = P("shard", "tensor")
    onto = P("tensor", "shard")
    heads = P("tensor")
    return jax.shard_map(
        functools.partial(on_device, shards, contexts),
        mesh=mesh,
        in_specs=(rows, into, heads, into, into, heads, onto, P(), P(), P(), into, heads, onto, P(), P(), P(), rows),
        out_specs=(rows, rows, into, heads, into, into, heads, onto, P(), P(), P(), into, heads, onto, P(), P(), P()),
        check_vma=False,
    )
```

```python
import functools

import jax
import jax.numpy as jnp
from jax import lax
from jax.experimental import pallas as pl
from jax.experimental.pallas import tpu as pltpu
from jax.sharding import PartitionSpec as P

HEAD_DIM = 64
EPSILON = 1e-05
F32 = jnp.float32
BF16 = jnp.bfloat16
VMEM_LIMIT = 56 << 20
EXTRA = 16
SUMS = 64
SMEM_SPEC = pl.BlockSpec(memory_space=pltpu.SMEM)
ANY_SPEC = pl.BlockSpec(memory_space=pl.ANY)


def nn(a, b):
    return jnp.dot(a, b, preferred_element_type=F32)


def nt(a, b):
    return lax.dot_general(a, b, (((1,), (1,)), ((), ())), preferred_element_type=F32)


def vmem(n):
    return [pl.BlockSpec(memory_space=pltpu.VMEM)] * n


def params():
    return pltpu.CompilerParams(vmem_limit_bytes=VMEM_LIMIT)


def head_lanes(shape, head):
    lane = lax.broadcasted_iota(jnp.int32, shape, len(shape) - 1)
    return (lane >= head * HEAD_DIM) & (lane < (head + 1) * HEAD_DIM)


def divisor(size, most):
    while size % most:
        most //= 2
    return most


def slot_rows(places, slot, size):
    return pl.ds(pl.multiple_of(places[slot] * size, size), size)


def forward_body(heads, index, places, inputs, near, cross, sib, w_four, b_query, b_value, query, key, value, attended, log_total, keep, send, q_heads, own, sem):
    fetch = pltpu.make_async_copy(inputs.at[index], own, sem)
    fetch.start()
    part, width = own.shape
    cols = heads * HEAD_DIM
    quarter = part // 4
    factor = HEAD_DIM**-0.5
    w_query, w_key, w_value, w_out = (w_four.at[i] for i in range(4))
    row = part
    for piece in (near, cross, sib, own):
        size = piece.shape[0]
        if piece is own:
            fetch.wait()
            query[...] = ((nt(own[...], w_query[...]) + b_query[...]).astype(BF16).astype(F32) * factor).astype(BF16)
            row = 0
        step = divisor(size, 512)

        def project(i, carry, piece=piece, row=row, step=step):
            rows = piece[pl.ds(i * step, step), :]
            out = pl.ds(row + i * step, step)
            key[out, :] = nt(rows, w_key[...]).astype(BF16)
            value[out, :] = (nt(rows, w_value[...]) + b_value[...]).astype(BF16)
            return carry

        lax.fori_loop(0, size // step, project, 0)
        row += size
    total = key.shape[0]
    block = divisor(total, 1024)
    for head in range(heads):
        mask = head_lanes((part, cols), head)
        q_heads[head] = jnp.where(mask, query[...].astype(F32), 0.0).astype(BF16)
    ones = jnp.ones((16, block), BF16)

    def attend(i, carry):
        rows = pl.ds(pl.multiple_of(i * block, block), block)
        keys = key[rows, :]
        turned = value[rows, :].T
        out = []
        for head in range(heads):
            top, mixed = carry[head]
            scores = nt(keys, q_heads[head])
            new_top = jnp.maximum(top, jnp.max(scores, axis=0, keepdims=True))
            powers = jnp.exp(scores - new_top).astype(BF16)
            values = jnp.concatenate([turned[head * HEAD_DIM : (head + 1) * HEAD_DIM, :], ones], axis=0)
            out.append((new_top, mixed * jnp.exp(top - new_top) + nn(values, powers)))
        return tuple(out)

    start = tuple((jnp.full((1, part), -jnp.inf, F32), jnp.zeros((HEAD_DIM + 16, part), F32)) for _ in range(heads))
    final = lax.fori_loop(0, total // block, attend, start)
    mixes = []
    logs = []
    for top, mixed in final:
        count = mixed[HEAD_DIM : HEAD_DIM + 1, :]
        mixes.append(mixed[:HEAD_DIM, :] / count)
        logs.append(top + jnp.log(count))
    attended[...] = jnp.concatenate(mixes, axis=0).T.astype(BF16)
    log_total[...] = jnp.concatenate(logs + [jnp.zeros((8 - heads, part), F32)], axis=0)
    for out, first in ((keep, 0), (send, 2)):
        for j in range(2):
            rows = attended[slot_rows(places, first + j, quarter), :]
            out[j * quarter : (j + 1) * quarter, :] = nn(rows, w_out[...]).astype(BF16)


def backward_body(heads, nears, index, places, g_own, g_cross, g_sib, w_four, query, key, value, attended, log_total,
                  d_query, d_key, d_value, keep, send, d_out, sums, grad, q_heads, g_heads, dq_turned):
    part, cols = query.shape
    total = key.shape[0]
    quarter = part // 4
    factor = HEAD_DIM**-0.5
    w_query, w_key, w_value, w_out = (w_four.at[i] for i in range(4))
    begin = index * quarter
    middle = g_own.shape[0]
    grad[slot_rows(places, 0, quarter), :] = g_own[begin : begin + quarter, :]
    grad[slot_rows(places, 1, quarter), :] = g_cross[begin : begin + quarter, :]
    grad[slot_rows(places, 2, quarter), :] = g_sib[begin : begin + quarter, :]
    grad[slot_rows(places, 3, quarter), :] = g_sib[middle + begin : middle + begin + quarter, :]
    grad_heads = nt(grad[...], w_out[...]).astype(BF16)
    att = attended[...]
    d_out[...] = nn(att.T, grad[...])
    product = grad_heads.astype(F32) * att.astype(F32)
    picks = jnp.concatenate(
        [jnp.where(head_lanes((1, cols), h), 1.0, 0.0) for h in range(heads)]
        + [jnp.zeros((8 - heads, cols), F32)], axis=0)
    weighted = lax.dot_general(picks, product, (((1,), (1,)), ((), ())), precision=lax.Precision.HIGHEST,
                               preferred_element_type=F32)
    for h in range(heads):
        mask = head_lanes((part, cols), h)
        q_heads[h] = jnp.where(mask, query[...].astype(F32), 0.0).astype(BF16)
        g_heads[h] = jnp.where(mask, grad_heads.astype(F32), 0.0).astype(BF16)
    dq_turned[...] = jnp.zeros_like(dq_turned)
    block = divisor(total, 1024)

    def chunk(i, carry):
        rows = pl.ds(pl.multiple_of(i * block, block), block)
        keys = key[rows, :]
        values = value[rows, :]
        keys_turned = keys.T
        dk = jnp.zeros((block, cols), F32)
        dv = jnp.zeros((block, cols), F32)
        for h in range(heads):
            scores = nt(keys, q_heads[h])
            probs = jnp.exp(scores - log_total[h : h + 1, :])
            d_probs = nt(values, g_heads[h])
            d_scores = (probs * (d_probs - weighted[h : h + 1, :])).astype(BF16)
            dv = dv + nn(probs.astype(BF16), g_heads[h])
            dk = dk + nn(d_scores, q_heads[h])
            own = slice(h * HEAD_DIM, (h + 1) * HEAD_DIM)
            dq_turned[own, :] += nn(keys_turned[own, :], d_scores)
        d_key[rows, :] = dk.astype(BF16)
        d_value[rows, :] = dv.astype(BF16)
        return carry + jnp.sum(dv.astype(BF16).astype(F32), axis=0, keepdims=True)

    sum_value = lax.fori_loop(0, total // block, chunk, jnp.zeros((1, cols), F32))
    dq = (dq_turned[...] * factor).T.astype(BF16)
    d_query[...] = dq
    sums[...] = jnp.concatenate(
        [jnp.sum(dq.astype(F32), axis=0, keepdims=True), sum_value, jnp.zeros((6, cols), F32)], axis=0)

    def back(rows):
        return nn(d_key[rows, :], w_key[...]) + nn(d_value[rows, :], w_value[...])

    row = part
    for out, first in ((keep, 0), (send, 2)):
        for j in range(2):
            mine = slot_rows(places, first + j, quarter)
            begin = j * (quarter + nears)
            out[begin : begin + quarter, :] = (back(mine) + nn(d_query[mine, :], w_query[...])).astype(BF16)
            out[begin + quarter : begin + quarter + nears, :] = back(pl.ds(row, nears)).astype(BF16)
            row += nears


def attention_forward(places, index, inputs, near, cross, sib, w_four, b_query, b_value):
    part, width = inputs.shape[1:]
    cols = w_four.shape[1]
    heads = cols // HEAD_DIM
    total = part + near.shape[0] + cross.shape[0] + sib.shape[0]
    shape = jax.ShapeDtypeStruct
    return pl.pallas_call(
        functools.partial(forward_body, heads, index),
        out_shape=(
            shape((part, cols), BF16),
            shape((total, cols), BF16),
            shape((total, cols), BF16),
            shape((part, cols), BF16),
            shape((8, part), F32),
            shape((part // 2, width), BF16),
            shape((part // 2, width), BF16),
        ),
        in_specs=[SMEM_SPEC, ANY_SPEC] + vmem(6),
        out_specs=vmem(7),
        scratch_shapes=[pltpu.VMEM((heads, part, cols), BF16), pltpu.VMEM((part, width), BF16), pltpu.SemaphoreType.DMA(())],
        compiler_params=params(),
        cost_estimate=pl.CostEstimate(
            flops=4 * total * width * cols + 16 * heads * part * total * HEAD_DIM,
            bytes_accessed=2 * (total * width + 3 * total * cols),
            transcendentals=heads * part * total,
        ),
        name="attention_forward",
    )(places, inputs, near, cross, sib, w_four, b_query, b_value)


def attention_backward(places, index, g_own, g_cross, g_sib, w_four, query, key, value, attended, log_total):
    part, cols = query.shape
    width = w_four.shape[2]
    heads = cols // HEAD_DIM
    total = key.shape[0]
    nears = (total - part) // 4
    shape = jax.ShapeDtypeStruct
    return pl.pallas_call(
        functools.partial(backward_body, heads, nears, index),
        out_shape=(
            shape((part, cols), BF16),
            shape((total, cols), BF16),
            shape((total, cols), BF16),
            shape((total // 2, width), BF16),
            shape((total // 2, width), BF16),
            shape((cols, width), F32),
            shape((8, cols), F32),
        ),
        in_specs=[SMEM_SPEC] + vmem(9),
        out_specs=vmem(7),
        scratch_shapes=[
            pltpu.VMEM((part, width), BF16),
            pltpu.VMEM((heads, part, cols), BF16),
            pltpu.VMEM((heads, part, cols), BF16),
            pltpu.VMEM((cols, part), F32),
        ],
        compiler_params=params(),
        cost_estimate=pl.CostEstimate(
            flops=4 * total * width * cols + 40 * heads * part * total * HEAD_DIM,
            bytes_accessed=2 * (total * width + 5 * total * cols),
            transcendentals=heads * part * total,
        ),
        name="attention_backward",
    )(places, g_own, g_cross, g_sib, w_four, query, key, value, attended, log_total)


def gradients_body(index, inputs, near, cross, sib, d_query, d_key, d_value, out, own, sem):
    fetch = pltpu.make_async_copy(inputs.at[index], own, sem)
    fetch.start()
    row = own.shape[0]
    for piece in (near, cross, sib, own):
        if piece is own:
            fetch.wait()
            row = 0
        rows = slice(row, row + piece.shape[0])
        for slot, grad in ((1, d_key), (2, d_value)):
            part = nn(grad[rows, :].T, piece[...])
            if piece is near:
                out[slot] = part
            else:
                out[slot] += part
        row += piece.shape[0]
    out[0] = nn(d_query[...].T, own[...])


def attention_gradients(index, inputs, near, cross, sib, d_query, d_key, d_value):
    cols = d_query.shape[1]
    width = inputs.shape[2]
    total = d_key.shape[0]
    return pl.pallas_call(
        functools.partial(gradients_body, index),
        out_shape=jax.ShapeDtypeStruct((3, cols, width), F32),
        in_specs=[ANY_SPEC] + vmem(6),
        out_specs=pl.BlockSpec(memory_space=pltpu.VMEM),
        scratch_shapes=[pltpu.VMEM(inputs.shape[1:], BF16), pltpu.SemaphoreType.DMA(())],
        compiler_params=params(),
        cost_estimate=pl.CostEstimate(
            flops=4 * total * cols * width, bytes_accessed=2 * total * (width + 2 * cols), transcendentals=0
        ),
        name="attention_gradients",
    )(inputs, near, cross, sib, d_query, d_key, d_value)


def rows_mean(a):
    return jnp.mean(a, axis=-1, keepdims=True)


def norm(values):
    centred = values - rows_mean(values)
    inverse = lax.rsqrt(rows_mean(centred * centred) + EPSILON)
    return centred * inverse, inverse


def norm_back(scaled, normed, inverse):
    return inverse * (scaled - rows_mean(scaled) - normed * rows_mean(scaled * normed))


def col_sum(a):
    return jnp.sum(a, axis=0, keepdims=True)


def feed_body(blocks, pieces, seqs, order, cotangents, *refs):
    count = blocks * pieces
    up_pieces, down_pieces, refs = refs[:count], refs[count : 2 * count], refs[2 * count :]
    shard = order[4]
    mine, keeps, gots, rests = (refs[i * seqs : (i + 1) * seqs] for i in range(4))
    vectors, result, grad_first_attn, grad_rest_attn = refs[4 * seqs : 4 * seqs + 4]
    (grad_low, act, d_inner, d_ffn, low, sums,
     up, down, bias, slope, cotangent, sems, cot_sems) = refs[4 * seqs + 4 :]
    rows, width = result.shape
    quarter = rows // seqs
    depth = width // pieces
    copies = []
    for b in range(blocks):
        for p in range(pieces):
            spot = pl.ds(pl.multiple_of(lax.rem(shard + p, pieces) * depth, depth), depth)
            source = up_pieces[b * pieces + p].at[pl.ds(0, depth), :]
            copies.append(pltpu.make_async_copy(source, up.at[b, spot, :], sems.at[b, p, 0]))
            copies.append(pltpu.make_async_copy(down_pieces[b * pieces + p], down.at[b, spot, :], sems.at[b, p, 1]))
        source = up_pieces[b * pieces].at[pl.ds(depth, EXTRA), :]
        copies.append(pltpu.make_async_copy(source, bias.at[b], sems.at[b, pieces, 0]))
    for i in range(seqs):
        source = cotangents.at[i, slot_rows(order, 0, quarter), :]
        copies.append(pltpu.make_async_copy(source, cotangent.at[pl.ds(i * quarter, quarter), :], cot_sems.at[i]))
    for copy in copies:
        copy.start()
    inputs = jnp.concatenate([r[...].astype(F32) for r in mine], axis=0)
    branch = jnp.concatenate(
        [keeps[i][:quarter, :].astype(F32) + gots[i][:quarter, :].astype(F32) + rests[i][...].astype(F32) for i in range(seqs)],
        axis=0)
    b_out, gain_one, bias_one, b_down, gain_two, bias_two = (vectors[i : i + 1, :] for i in range(6))
    pre = inputs + branch + b_out
    normed_one, inverse_one = norm(pre)
    first = normed_one * gain_one + bias_one
    first_low = first.astype(BF16)
    low[...] = first_low
    for copy in copies:
        copy.wait()

    def ahead(b, total):
        parts = bias[b].astype(F32)
        b_hidden = (parts[0:1, :] + parts[1:2, :]) + parts[2:3, :]
        inner = nn(first_low, up[b]) + b_hidden
        shape = 0.5 * (1.0 + lax.erf(inner * (0.5**0.5)))
        act_low = (inner * shape).astype(BF16)
        act[b] = act_low
        slope[b] = shape + inner * (jnp.exp(-0.5 * inner * inner) * 0.3989422804014327)
        return total + nt(act_low, down[b])

    ffn = lax.fori_loop(0, blocks, ahead, jnp.zeros((rows, width), F32))
    normed_two, inverse_two = norm(first + ffn + b_down)
    result[...] = (normed_two * gain_two + bias_two).astype(BF16)
    grad = cotangent[...].astype(F32)
    grad_second = norm_back(grad * gain_two, normed_two, inverse_two)
    grad_ffn = grad_second.astype(BF16)
    d_ffn[...] = grad_ffn

    def astern(b, total):
        grad_inner = (nn(grad_ffn, down[b]) * slope[b]).astype(BF16)
        d_inner[b] = grad_inner
        return total + nt(grad_inner, up[b])

    grad_first = lax.fori_loop(0, blocks, astern, grad_second)
    grad_pre = norm_back(grad_first * gain_one, normed_one, inverse_one)
    grad_low[...] = grad_pre
    grad_first_attn[...] = grad_pre[:quarter, :].astype(BF16)
    grad_rest_attn[...] = grad_pre[quarter:, :].astype(BF16)
    sums[...] = jnp.concatenate(
        [col_sum(grad_pre), col_sum(grad_first * normed_one), col_sum(grad_first), col_sum(grad_second),
         col_sum(grad * normed_two), col_sum(grad), jnp.zeros((2, width), F32)], axis=0)


def feed_forward(order, ups, downs, cotangents, mine, keeps, gots, rests, vectors):
    seqs = len(mine)
    blocks = len(ups)
    pieces = len(ups[0])
    flat = [w for block in ups for w in block] + [w for block in downs for w in block]
    quarter, width = mine[0].shape
    rows = quarter * seqs
    hidden = ups[0][0].shape[-1]
    shape = jax.ShapeDtypeStruct
    return pl.pallas_call(
        functools.partial(feed_body, blocks, pieces, seqs),
        out_shape=(
            shape((rows, width), BF16),
            shape((quarter, width), BF16),
            shape((rows - quarter, width), BF16),
            shape((rows, width), F32),
            shape((blocks, rows, hidden), BF16),
            shape((blocks, rows, hidden), BF16),
            shape((rows, width), BF16),
            shape((rows, width), BF16),
            shape((8, width), F32),
        ),
        in_specs=[SMEM_SPEC] + [ANY_SPEC] * (1 + len(flat)) + vmem(4 * seqs + 1),
        out_specs=vmem(9),
        scratch_shapes=[
            pltpu.VMEM((blocks, width, hidden), BF16),
            pltpu.VMEM((blocks, width, hidden), BF16),
            pltpu.VMEM((blocks, EXTRA, hidden), BF16),
            pltpu.VMEM((blocks, rows, hidden), F32),
            pltpu.VMEM((rows, width), BF16),
            pltpu.SemaphoreType.DMA((blocks, pieces + 1, 2)),
            pltpu.SemaphoreType.DMA((seqs,)),
        ],
        compiler_params=params(),
        cost_estimate=pl.CostEstimate(
            flops=8 * rows * width * hidden * blocks,
            bytes_accessed=6 * width * hidden * blocks,
            transcendentals=2 * rows * hidden * blocks,
        ),
        name="feed_forward",
    )(order, cotangents, *flat, *mine, *keeps, *gots, *rests, vectors)


def feed_gradients_body(pieces, order, act, d_inner, d_ffn, low, sums, ups, downs, low_turned, ffn_turned):
    depth = low.shape[1] // pieces
    hidden = act.shape[-1]
    shard = order[4]
    grad_inner = d_inner[0]

    @pl.when(pl.program_id(0) == 0)
    def _():
        low_turned[...] = low[...].T
        ffn_turned[...] = d_ffn[...].T

    up = nn(low_turned[...], grad_inner)
    down = nn(ffn_turned[...], act[0])
    extra = jnp.concatenate(
        [sums[:6, :], col_sum(grad_inner.astype(F32)), jnp.zeros((SUMS - 7, hidden), F32)], axis=0).astype(BF16)
    for p in range(pieces):
        spot = lax.rem(p - shard + pieces, pieces)
        ups[0, spot, :depth, :] = up[p * depth : (p + 1) * depth, :].astype(BF16)
        ups[0, spot, depth:, :] = extra
        downs[0, spot, :, :] = down[p * depth : (p + 1) * depth, :].astype(BF16)


def feed_gradients(pieces, first, order, act, d_inner, d_ffn, low, sums):
    blocks, rows, hidden = act.shape
    width = low.shape[1]
    depth = width // pieces
    shape = jax.ShapeDtypeStruct
    pick = pl.BlockSpec((1, rows, hidden), lambda i, order: (first + i, 0, 0))
    whole = pl.BlockSpec((rows, width), lambda i, order: (0, 0))
    return pl.pallas_call(
        functools.partial(feed_gradients_body, pieces),
        out_shape=(shape((2, pieces, depth + SUMS, hidden), BF16), shape((2, pieces, depth, hidden), BF16)),
        grid_spec=pltpu.PrefetchScalarGridSpec(
            num_scalar_prefetch=1,
            grid=(2,),
            in_specs=[pick, pick, whole, whole, pl.BlockSpec((8, width), lambda i, order: (0, 0))],
            out_specs=[
                pl.BlockSpec((1, pieces, depth + SUMS, hidden), lambda i, order: (i, 0, 0, 0)),
                pl.BlockSpec((1, pieces, depth, hidden), lambda i, order: (i, 0, 0, 0)),
            ],
            scratch_shapes=[pltpu.VMEM((width, rows), BF16), pltpu.VMEM((width, rows), BF16)],
        ),
        compiler_params=params(),
        cost_estimate=pl.CostEstimate(
            flops=8 * rows * width * hidden, bytes_accessed=8 * width * hidden, transcendentals=0
        ),
        name="feed_gradients",
    )(order, act, d_inner, d_ffn, low, sums)


def rotated(value, axis, count, shift):
    return lax.ppermute(value, axis, [(i, (i + shift) % count) for i in range(count)])


def across(value):
    return lax.ppermute(value, "tensor", [(i, i ^ 2) for i in range(4)])


def sibling(value):
    return lax.ppermute(value, "tensor", [(i, i ^ 1) for i in range(4)])


def stage(*values):
    return lax.optimization_barrier(values)


def added(*values):
    total = values[0].astype(F32)
    for value in values[1:]:
        total = total + value.astype(F32)
    return total


def rounded(value):
    return lax.reduce_precision(value, 8, 7)


def low_sum(*values):
    return added(*values).astype(BF16)


def thirds(value):
    high = value.astype(BF16)
    rest = value - high.astype(F32)
    middle = rest.astype(BF16)
    return high, middle, (rest - middle.astype(F32)).astype(BF16)


def on_device(shards, contexts, inputs, w_query, b_query, w_key, w_value, b_value, w_out, b_out,
              first_gain, first_bias, w_hidden, b_hidden, w_down, b_down, second_gain, second_bias, cotangent):
    seqs, part, width = inputs.shape
    cols = w_query.shape[1]
    quarter = part // 4
    depth = width // shards
    shard = lax.axis_index("shard")
    context = lax.axis_index("context")
    tensor = lax.axis_index("tensor")
    masks = [1 << i for i in range(contexts.bit_length() - 1)]
    hops = len(masks)
    places = jnp.stack([tensor ^ flip for flip in (0, 2, 1, 3)]).astype(jnp.int32)
    order = jnp.concatenate([places, shard[None].astype(jnp.int32)])

    def along(value, mask):
        return lax.ppermute(value, "context", [(i, i ^ mask) for i in range(contexts)])

    def from_shards(value):
        return [rotated(value, "shard", shards, -r) for r in range(1, shards)]

    def to_shards(parts):
        return [rotated(value, "shard", shards, r) for r, value in enumerate(parts, 1)]

    mine = [lax.dynamic_slice_in_dim(inputs[s], tensor * quarter, quarter, axis=0) for s in range(seqs)]
    nears = [[m] for m in mine]
    cross = [None] * seqs
    four = jnp.stack([w_query.T, w_key.T, w_value.T, w_out])
    line = lax.broadcasted_iota(jnp.int32, (EXTRA, w_hidden.shape[1]), 0)
    biases = jnp.zeros((EXTRA, w_hidden.shape[1]), BF16)
    for i, third in enumerate(thirds(b_hidden)):
        biases = jnp.where(line == i, third[None], biases)
    up_own = jnp.concatenate([w_hidden, lax.optimization_barrier(biases)], axis=0)
    down_own = w_down.T
    vectors = jnp.concatenate([b_out, first_gain, first_bias, b_down, second_gain, second_bias]).reshape(6, width)
    up_x = up_y = up_xy = down_x = down_y = down_xy = other = None
    up_beside, down_beside = {}, {}
    saved = [None] * seqs
    sibs = [None] * seqs
    joined = [None] * seqs
    held = [None] * seqs
    gots = []
    rests = []
    rest = None
    four_all = None
    for j in range(hops + 1 + seqs):
        flights = {}
        found = ()
        s = j - hops - 1
        if s >= 0:
            sibs[s] = sibling(jnp.concatenate([joined[s], cross[s]], axis=0))
            if s >= 1:
                gots.append(sibling(held[s - 1][1]))
                rest = low_sum(held[s - 1][0][quarter:], gots[-1][quarter:])
                sibs[s], rest = stage(sibs[s], rest)
                flights["rest"] = across(rest)
            query, key, value, attended, log_total, keep, send = attention_forward(
                places, s, inputs, joined[s], cross[s], sibs[s], four_all, b_query[None], b_value[None])
            saved[s] = (query, key, value, attended, log_total)
            found = (keep, send)
        for q in range(seqs):
            k = j - q
            if 0 <= k < hops:
                flights[f"z{q}"] = along(jnp.concatenate(nears[q], axis=0), masks[hops - 1 - k])
            if k == hops:
                joined[q] = jnp.concatenate(nears[q][1:], axis=0)
                flights[f"x{q}"] = across(joined[q])
        if j == hops - 1:
            flights["up_x"] = across(up_own)
            flights["four"] = from_shards(four)
        if j == hops:
            flights["up_y"] = from_shards(up_own)
        if j == hops + 1:
            flights["down_y"] = from_shards(down_own)
            flights["down_x"] = across(stage(down_own, sibs[0])[0])
        if j == hops + 2:
            flights["up_xy"] = from_shards(up_x)
            flights["up_c"] = sibling(up_own)
        if j == hops + 3:
            flights["down_xy"] = from_shards(down_x)
            flights["down_c"] = sibling(down_own)
        flights, found, four, up_own, down_own, vectors, nears, up_x, up_y, up_xy, down_x, down_y = stage(
            flights, found, four, up_own, down_own, vectors, nears, up_x, up_y, up_xy, down_x, down_y)
        for q in range(seqs):
            if f"z{q}" in flights:
                nears[q] = nears[q] + [flights[f"z{q}"]]
            if f"x{q}" in flights:
                cross[q] = flights[f"x{q}"]
        if s >= 0:
            held[s] = found
            if s >= 1:
                rests.append(flights["rest"])
        if j == hops - 1:
            up_x, other = flights["up_x"], flights["four"]
            if shards == 2:
                left = jnp.where(shard == 0, four, other[0])
                right = jnp.where(shard == 0, other[0], four)
                four_all = jnp.concatenate([left, right], axis=2)
            else:
                four_all = lax.all_gather(four, "shard", axis=2, tiled=True)
        if j == hops:
            up_y = flights["up_y"]
        if j == hops + 1:
            down_x, down_y = flights["down_x"], flights["down_y"]
        if j == hops + 2:
            up_xy, up_c = flights["up_xy"], flights["up_c"]
        if j == hops + 3:
            down_xy, down_c = flights["down_xy"], flights["down_c"]
    gots.append(sibling(held[seqs - 1][1]))
    rests.append(across(low_sum(held[seqs - 1][0][quarter:], gots[-1][quarter:])))
    ups = [[up_own] + up_y, [up_x] + up_xy, [up_c] + [sibling(w) for w in up_y], [sibling(w) for w in [up_x] + up_xy]]
    downs = [[down_own] + down_y, [down_x] + down_xy, [down_c] + [sibling(w) for w in down_y],
             [sibling(w) for w in [down_x] + down_xy]]
    result, g_first, g_rest, grad_low, act, d_inner, d_ffn, low, sums = feed_forward(
        order, ups, downs, cotangent, mine, [h[0] for h in held], gots, rests, vectors)

    up_send, down_send = feed_gradients(shards, 2, order, act, d_inner, d_ffn, low, sums)
    g_first_x, up_send, down_send, d_inner, g_rest = stage(across(g_first), up_send, down_send, d_inner, g_rest)
    up_keep, down_keep = feed_gradients(shards, 0, order, act, d_inner, d_ffn, low, sums)
    g_first_c, g_rest_x, up_got, down_got, up_keep, down_keep, result = stage(
        sibling(jnp.concatenate([g_first, g_first_x], axis=0)), across(g_rest),
        sibling(up_send), sibling(down_send), up_keep, down_keep, result)
    up_leave = low_sum(up_keep[1], up_got[1])
    down_leave = [low_sum(down_keep[:, r], down_got[:, r]) for r in range(1, shards)]
    up_pair = rounded(added(up_keep[0], up_got[0]))
    down_pair = rounded(added(down_keep[:, 0], down_got[:, 0]))

    def project(s, found):
        return attention_gradients(s, inputs, joined[s], cross[s], sibs[s], *found[:3])

    def leaving(terms):
        half = terms[-1].shape[0] // 2
        return low_sum(*[t[half : 2 * half] for t in terms])

    def settle(s, terms):
        return low_sum(grad_low[s * quarter : (s + 1) * quarter], *[t[:quarter] for t in terms])

    def paired(parts):
        own = parts.reshape(parts.shape[0] // quarter, quarter, width)
        return own, across(own)

    def whole(own, swapped):
        count = own.shape[0]
        beside = sibling(jnp.stack([own, swapped]))
        row, side = tensor // 2, tensor % 2
        blocks = []
        for r in range(2):
            for c in range(2):
                here = jnp.where(side == c, own, beside[0])
                there = jnp.where(side == c, swapped, beside[1])
                blocks.append(jnp.where(row == r, here, there))
        return jnp.stack(blocks, axis=1).reshape(count, part, width)

    def split(value, mask):
        half = value.shape[0] // 2
        bit = (context & mask) // mask
        stay = lax.dynamic_slice_in_dim(value, bit * half, half, axis=0)
        return stay, lax.dynamic_slice_in_dim(value, (1 - bit) * half, half, axis=0).astype(BF16)

    def join(value, got, mask):
        lower = (context & mask) == 0
        return jnp.concatenate([jnp.where(lower, value, got), jnp.where(lower, got, value)], axis=0)

    columns = []
    outs = []
    projections = []

    def work(s, *gradient):
        found = attention_backward(places, max(s - 1, 0), *gradient, four_all, *saved[s])
        columns.append(found[6])
        outs.append(found[5])
        return found

    g_first, up_leave, down_leave = stage(g_first, up_leave, down_leave)
    found = work(0, g_first, g_first_x, g_first_c)
    up_far, down_far, g_rest_c, projection, keep, send = stage(
        across(up_leave), to_shards(down_leave), sibling(jnp.concatenate([g_rest, g_rest_x], axis=0)),
        project(0, found), found[3], found[4])
    projections.append(projection)
    got = sibling(send)
    up_leave = [low_sum(up_pair[r], up_far[r]) for r in range(1, shards)]
    down_leave = low_sum(down_pair[1], *[d[1] for d in down_far])
    up_pair = rounded(added(up_pair[0], up_far[0]))
    down_pair = rounded(added(down_pair[0], *[d[0] for d in down_far]))
    terms0 = [keep, got]
    leave = leaving(terms0)
    g_rest, leave, up_leave, down_leave = stage(g_rest, leave, up_leave, down_leave)
    found = work(1, g_rest, g_rest_x, g_rest_c)
    up_far, down_far, found = stage(to_shards(up_leave), across(down_leave), found)
    feed = jnp.concatenate([low_sum(up_pair, *up_far), low_sum(down_pair, down_far)], axis=0)
    feed_stay, feed_leave = split(feed, masks[0])
    flight, projection, keep, send, feed_stay, feed_leave = stage(
        across(leave), project(1, found), found[3], found[4], feed_stay, feed_leave)
    projections.append(projection)
    terms0 = terms0 + [flight]
    z_leave = leaving(terms0)
    terms1 = [keep, sibling(send)]
    leave = leaving(terms1)
    g_rest, leave, z_leave = stage(g_rest, leave, z_leave)
    found = work(2, g_rest, g_rest_x, g_rest_c)
    flight, z0, feed_got, found = stage(across(leave), along(z_leave, masks[0]), along(feed_leave, masks[0]), found)
    terms0 = terms0 + [z0]
    terms1 = terms1 + [flight]
    z0_leave, z1_leave = leaving(terms0), leaving(terms1)
    feed_parts = split(low_sum(feed_stay, feed_got), masks[1])
    got = sibling(found[4])
    found, z0_leave, z1_leave = stage(found, z0_leave, z1_leave)
    terms1 = terms1 + [along(z1_leave, masks[0])]
    terms0 = terms0 + [along(z0_leave, masks[1])]
    projections.append(project(2, found))
    got, projections[2] = stage(got, projections[2])
    terms2 = [found[3], got]
    leave = leaving(terms2)
    half = leave.shape[0] // 2
    flight_first = across(leave[half:])
    flight = across(leave[:half])

    def scatter(parts, hop):
        return parts[0], along(parts[1], masks[hop])

    def collect(value, hop):
        return along(value, masks[hop])

    def merge(value, got, hop):
        return join(value, got, masks[hop])

    feed_parts, leave = stage(feed_parts, leave)
    feed = scatter(feed_parts, 1)
    projected = jnp.concatenate([added(*projections), added(*outs)[None]], axis=0)
    biases = added(*columns)[:2].reshape(-1)
    lines = EXTRA * contexts
    biases = jnp.pad(biases, (0, lines * depth - biases.shape[0])).reshape(lines, depth)

    def lined(value):
        return jnp.concatenate([value.reshape(4 * cols, depth), biases], axis=0).astype(BF16)

    if shards == 2:
        left, right = projected[..., :depth], projected[..., depth:]
        staying = lined(jnp.where(shard == 0, left, right))
        attn = (staying, rotated(lined(jnp.where(shard == 0, right, left)), "shard", 2, 1))
    else:
        stacked = jnp.stack([lined(projected[..., r * depth : (r + 1) * depth]) for r in range(shards)])
        attn = (lax.psum_scatter(stacked, "shard", scatter_dimension=0),)
    terms1, staying = stage(terms1, attn[0])
    attn = (staying,) + attn[1:]
    z1_leave = leaving(terms1)
    terms1 = terms1 + [along(z1_leave, masks[1])]
    flight_first, z1_leave = stage(flight_first, z1_leave)
    z2_leave = leaving([t[: 2 * half] for t in terms2[:2]] + [jnp.concatenate([flight_first, flight_first], axis=0)])
    z2 = along(z2_leave, masks[0])
    terms0, feed, z2_leave = stage(terms0, feed, z2_leave)
    early = [settle(0, terms0)]
    feed = low_sum(*feed)
    feed_got = collect(feed, hops - 1)
    attn, early, feed = stage(attn, early, feed)
    attn = split(low_sum(*attn), masks[0])
    attn_got = along(attn[1], masks[0])
    terms1, attn_leave = stage(terms1, attn[1])
    early = jnp.concatenate(early + [settle(1, terms1)], axis=0)
    early_x = paired(early)[1]
    result, early = stage(result, early)
    result_x = paired(result)[1]
    z2, flight, early = stage(z2, flight, early)
    terms2 = terms2 + [flight, z2]
    z2_leave = leaving(terms2)
    z2 = along(z2_leave, masks[1])
    attn_got, z2_leave = stage(attn_got, z2_leave)
    attn = split(low_sum(attn[0], attn_got), masks[1])
    attn_got = along(attn[1], masks[1])
    feed_got, early_x, attn_leave = stage(feed_got, early_x, attn[1])
    feed = merge(feed, feed_got, hops - 1)
    feed_got = collect(feed, 0)
    z2, feed, early_x = stage(z2, feed, early_x)
    last = settle(2, terms2 + [z2])
    last_x = paired(last)[1]
    attn_got, last = stage(attn_got, last)
    attn = low_sum(attn[0], attn_got)
    attn_got = collect(attn, 1)
    result_x, attn, early, early_x = stage(result_x, attn, early, early_x)
    early = whole(early.reshape(early_x.shape), early_x)
    last_x, attn_got, early = stage(last_x, attn_got, early)
    attn = merge(attn, attn_got, 1)
    attn_got = collect(attn, 0)
    last = whole(last.reshape(last_x.shape), last_x)
    feed_got, last = stage(feed_got, last)
    feed = merge(feed, feed_got, 0)
    outputs = whole(result.reshape(result_x.shape), result_x)
    attn_got, outputs, last, feed = stage(attn_got, outputs, last, feed)
    attn = merge(attn, attn_got, 0)
    input_grad = jnp.concatenate([early, last], axis=0)

    feed, attn = feed.astype(F32), attn.astype(F32)
    vector_sums = feed[depth : depth + 7]
    bias_sums = attn[4 * cols :].reshape(-1)[: 2 * cols]
    matrices = attn[: 4 * cols].reshape(4, cols, depth)
    return (
        outputs,
        input_grad,
        matrices[0].T,
        bias_sums[:cols],
        matrices[1].T,
        matrices[2].T,
        bias_sums[cols:],
        matrices[3],
        vector_sums[0],
        vector_sums[1],
        vector_sums[2],
        feed[:depth],
        vector_sums[6],
        feed[depth + SUMS :].T,
        vector_sums[3],
        vector_sums[4],
        vector_sums[5],
    )


def solution(mesh):
    shards = mesh.shape["shard"]
    contexts = mesh.shape["context"]
    rows = P("shard", "context", None)
    into = P("shard", "tensor")
    onto = P("tensor", "shard")
    heads = P("tensor")
    return jax.shard_map(
        functools.partial(on_device, shards, contexts),
        mesh=mesh,
        in_specs=(rows, into, heads, into, into, heads, onto, P(), P(), P(), into, heads, onto, P(), P(), P(), rows),
        out_specs=(rows, rows, into, heads, into, into, heads, onto, P(), P(), P(), into, heads, onto, P(), P(), P()),
        check_vma=False,
    )
```

```python
import functools

import jax
import jax.numpy as jnp
from jax import lax
from jax.experimental import pallas as pl
from jax.experimental.pallas import tpu as pltpu
from jax.sharding import PartitionSpec as P

HEAD_DIM = 64
EPSILON = 1e-05
F32 = jnp.float32
BF16 = jnp.bfloat16
VMEM_LIMIT = 56 << 20
EXTRA = 16
SUMS = 64
SMEM_SPEC = pl.BlockSpec(memory_space=pltpu.SMEM)
ANY_SPEC = pl.BlockSpec(memory_space=pl.ANY)


def nn(a, b):
    return jnp.dot(a, b, preferred_element_type=F32)


def nt(a, b):
    return lax.dot_general(a, b, (((1,), (1,)), ((), ())), preferred_element_type=F32)


def vmem(n):
    return [pl.BlockSpec(memory_space=pltpu.VMEM)] * n


def params():
    return pltpu.CompilerParams(vmem_limit_bytes=VMEM_LIMIT)


def head_lanes(shape, head):
    lane = lax.broadcasted_iota(jnp.int32, shape, len(shape) - 1)
    return (lane >= head * HEAD_DIM) & (lane < (head + 1) * HEAD_DIM)


def divisor(size, most):
    while size % most:
        most //= 2
    return most


def slot_rows(places, slot, size):
    return pl.ds(pl.multiple_of(places[slot] * size, size), size)


def forward_body(heads, index, places, inputs, near, cross, sib, w_four, b_query, b_value, query, key, value, attended, log_total, keep, send, q_heads, own, sem):
    fetch = pltpu.make_async_copy(inputs.at[index], own, sem)
    fetch.start()
    part, width = own.shape
    cols = heads * HEAD_DIM
    quarter = part // 4
    factor = HEAD_DIM**-0.5
    w_query, w_key, w_value, w_out = (w_four.at[i] for i in range(4))
    row = part
    for piece in (near, cross, sib, own):
        size = piece.shape[0]
        if piece is own:
            fetch.wait()
            query[...] = ((nt(own[...], w_query[...]) + b_query[...]).astype(BF16).astype(F32) * factor).astype(BF16)
            row = 0
        step = divisor(size, 512)

        def project(i, carry, piece=piece, row=row, step=step):
            rows = piece[pl.ds(i * step, step), :]
            out = pl.ds(row + i * step, step)
            key[out, :] = nt(rows, w_key[...]).astype(BF16)
            value[out, :] = (nt(rows, w_value[...]) + b_value[...]).astype(BF16)
            return carry

        lax.fori_loop(0, size // step, project, 0)
        row += size
    total = key.shape[0]
    block = divisor(total, 1024)
    for head in range(heads):
        mask = head_lanes((part, cols), head)
        q_heads[head] = jnp.where(mask, query[...].astype(F32), 0.0).astype(BF16)
    ones = jnp.ones((16, block), BF16)

    def attend(i, carry):
        rows = pl.ds(pl.multiple_of(i * block, block), block)
        keys = key[rows, :]
        turned = value[rows, :].T
        out = []
        for head in range(heads):
            top, mixed = carry[head]
            scores = nt(keys, q_heads[head])
            new_top = jnp.maximum(top, jnp.max(scores, axis=0, keepdims=True))
            powers = jnp.exp(scores - new_top).astype(BF16)
            values = jnp.concatenate([turned[head * HEAD_DIM : (head + 1) * HEAD_DIM, :], ones], axis=0)
            out.append((new_top, mixed * jnp.exp(top - new_top) + nn(values, powers)))
        return tuple(out)

    start = tuple((jnp.full((1, part), -jnp.inf, F32), jnp.zeros((HEAD_DIM + 16, part), F32)) for _ in range(heads))
    final = lax.fori_loop(0, total // block, attend, start)
    mixes = []
    logs = []
    for top, mixed in final:
        count = mixed[HEAD_DIM : HEAD_DIM + 1, :]
        mixes.append(mixed[:HEAD_DIM, :] / count)
        logs.append(top + jnp.log(count))
    attended[...] = jnp.concatenate(mixes, axis=0).T.astype(BF16)
    log_total[...] = jnp.concatenate(logs + [jnp.zeros((8 - heads, part), F32)], axis=0)
    for out, first in ((keep, 0), (send, 2)):
        for j in range(2):
            rows = attended[slot_rows(places, first + j, quarter), :]
            out[j * quarter : (j + 1) * quarter, :] = nn(rows, w_out[...]).astype(BF16)


def backward_body(heads, nears, index, places, g_own, g_cross, g_sib, w_four, query, key, value, attended, log_total,
                  d_query, d_key, d_value, keep, send, d_out, sums, grad, q_heads, g_heads, dq_turned):
    part, cols = query.shape
    total = key.shape[0]
    quarter = part // 4
    factor = HEAD_DIM**-0.5
    w_query, w_key, w_value, w_out = (w_four.at[i] for i in range(4))
    begin = index * quarter
    middle = g_own.shape[0]
    grad[slot_rows(places, 0, quarter), :] = g_own[begin : begin + quarter, :]
    grad[slot_rows(places, 1, quarter), :] = g_cross[begin : begin + quarter, :]
    grad[slot_rows(places, 2, quarter), :] = g_sib[begin : begin + quarter, :]
    grad[slot_rows(places, 3, quarter), :] = g_sib[middle + begin : middle + begin + quarter, :]
    grad_heads = nt(grad[...], w_out[...]).astype(BF16)
    att = attended[...]
    d_out[...] = nn(att.T, grad[...])
    product = grad_heads.astype(F32) * att.astype(F32)
    picks = jnp.concatenate(
        [jnp.where(head_lanes((1, cols), h), 1.0, 0.0) for h in range(heads)]
        + [jnp.zeros((8 - heads, cols), F32)], axis=0)
    weighted = lax.dot_general(picks, product, (((1,), (1,)), ((), ())), precision=lax.Precision.HIGHEST,
                               preferred_element_type=F32)
    for h in range(heads):
        mask = head_lanes((part, cols), h)
        q_heads[h] = jnp.where(mask, query[...].astype(F32), 0.0).astype(BF16)
        g_heads[h] = jnp.where(mask, grad_heads.astype(F32), 0.0).astype(BF16)
    dq_turned[...] = jnp.zeros_like(dq_turned)
    block = divisor(total, 1024)

    def chunk(i, carry):
        rows = pl.ds(pl.multiple_of(i * block, block), block)
        keys = key[rows, :]
        values = value[rows, :]
        keys_turned = keys.T
        dk = jnp.zeros((block, cols), F32)
        dv = jnp.zeros((block, cols), F32)
        for h in range(heads):
            scores = nt(keys, q_heads[h])
            probs = jnp.exp(scores - log_total[h : h + 1, :])
            d_probs = nt(values, g_heads[h])
            d_scores = (probs * (d_probs - weighted[h : h + 1, :])).astype(BF16)
            dv = dv + nn(probs.astype(BF16), g_heads[h])
            dk = dk + nn(d_scores, q_heads[h])
            own = slice(h * HEAD_DIM, (h + 1) * HEAD_DIM)
            dq_turned[own, :] += nn(keys_turned[own, :], d_scores)
        d_key[rows, :] = dk.astype(BF16)
        d_value[rows, :] = dv.astype(BF16)
        return carry + jnp.sum(dv.astype(BF16).astype(F32), axis=0, keepdims=True)

    sum_value = lax.fori_loop(0, total // block, chunk, jnp.zeros((1, cols), F32))
    dq = (dq_turned[...] * factor).T.astype(BF16)
    d_query[...] = dq
    sums[...] = jnp.concatenate(
        [jnp.sum(dq.astype(F32), axis=0, keepdims=True), sum_value, jnp.zeros((6, cols), F32)], axis=0)

    def back(rows):
        return nn(d_key[rows, :], w_key[...]) + nn(d_value[rows, :], w_value[...])

    row = part
    for out, first in ((keep, 0), (send, 2)):
        for j in range(2):
            mine = slot_rows(places, first + j, quarter)
            begin = j * (quarter + nears)
            out[begin : begin + quarter, :] = (back(mine) + nn(d_query[mine, :], w_query[...])).astype(BF16)
            out[begin + quarter : begin + quarter + nears, :] = back(pl.ds(row, nears)).astype(BF16)
            row += nears


def attention_forward(places, index, inputs, near, cross, sib, w_four, b_query, b_value):
    part, width = inputs.shape[1:]
    cols = w_four.shape[1]
    heads = cols // HEAD_DIM
    total = part + near.shape[0] + cross.shape[0] + sib.shape[0]
    shape = jax.ShapeDtypeStruct
    return pl.pallas_call(
        functools.partial(forward_body, heads, index),
        out_shape=(
            shape((part, cols), BF16),
            shape((total, cols), BF16),
            shape((total, cols), BF16),
            shape((part, cols), BF16),
            shape((8, part), F32),
            shape((part // 2, width), BF16),
            shape((part // 2, width), BF16),
        ),
        in_specs=[SMEM_SPEC, ANY_SPEC] + vmem(6),
        out_specs=vmem(7),
        scratch_shapes=[pltpu.VMEM((heads, part, cols), BF16), pltpu.VMEM((part, width), BF16), pltpu.SemaphoreType.DMA(())],
        compiler_params=params(),
        cost_estimate=pl.CostEstimate(
            flops=4 * total * width * cols + 16 * heads * part * total * HEAD_DIM,
            bytes_accessed=2 * (total * width + 3 * total * cols),
            transcendentals=heads * part * total,
        ),
        name="attention_forward",
    )(places, inputs, near, cross, sib, w_four, b_query, b_value)


def attention_backward(places, index, g_own, g_cross, g_sib, w_four, query, key, value, attended, log_total):
    part, cols = query.shape
    width = w_four.shape[2]
    heads = cols // HEAD_DIM
    total = key.shape[0]
    nears = (total - part) // 4
    shape = jax.ShapeDtypeStruct
    return pl.pallas_call(
        functools.partial(backward_body, heads, nears, index),
        out_shape=(
            shape((part, cols), BF16),
            shape((total, cols), BF16),
            shape((total, cols), BF16),
            shape((total // 2, width), BF16),
            shape((total // 2, width), BF16),
            shape((cols, width), F32),
            shape((8, cols), F32),
        ),
        in_specs=[SMEM_SPEC] + vmem(9),
        out_specs=vmem(7),
        scratch_shapes=[
            pltpu.VMEM((part, width), BF16),
            pltpu.VMEM((heads, part, cols), BF16),
            pltpu.VMEM((heads, part, cols), BF16),
            pltpu.VMEM((cols, part), F32),
        ],
        compiler_params=params(),
        cost_estimate=pl.CostEstimate(
            flops=4 * total * width * cols + 40 * heads * part * total * HEAD_DIM,
            bytes_accessed=2 * (total * width + 5 * total * cols),
            transcendentals=heads * part * total,
        ),
        name="attention_backward",
    )(places, g_own, g_cross, g_sib, w_four, query, key, value, attended, log_total)


def gradients_body(index, adds, last, *refs):
    inputs, near, cross, sib, d_query, d_key, d_value = refs[:7]
    previous, refs = refs[7 : 7 + adds], refs[7 + adds :]
    if last:
        order, biases, d_outs = refs[0], refs[1], refs[2:5]
        staying, leaving, out, own, sem = refs[5:]
    else:
        out, own, sem = refs
    fetch = pltpu.make_async_copy(inputs.at[index], own, sem)
    fetch.start()
    row = own.shape[0]
    for piece in (near, cross, sib, own):
        if piece is own:
            fetch.wait()
            row = 0
        rows = slice(row, row + piece.shape[0])
        for slot, grad in ((1, d_key), (2, d_value)):
            part = nn(grad[rows, :].T, piece[...])
            if piece is not near:
                out[slot] += part
            elif previous:
                out[slot] = previous[0][slot] + part
            else:
                out[slot] = part
        row += piece.shape[0]
    part = nn(d_query[...].T, own[...])
    out[0] = previous[0][0] + part if previous else part
    if not last:
        return
    cols, width = part.shape
    depth = width // 2
    swap = order[4] == 1
    for slot in range(4):
        total = out[slot] if slot < 3 else d_outs[0][...] + d_outs[1][...] + d_outs[2][...]
        left, right = total[:, :depth], total[:, depth:]
        spot = slice(slot * cols, (slot + 1) * cols)
        staying[spot, :] = jnp.where(swap, right, left).astype(BF16)
        leaving[spot, :] = jnp.where(swap, left, right).astype(BF16)
    staying[4 * cols :, :] = biases[...]
    leaving[4 * cols :, :] = biases[...]


def attention_gradients(index, inputs, near, cross, sib, d_query, d_key, d_value, previous=(), final=()):
    cols = d_query.shape[1]
    width = inputs.shape[2]
    total = d_key.shape[0]
    shape = jax.ShapeDtypeStruct
    sums = shape((3, cols, width), F32)
    half = shape((4 * cols + final[1].shape[0], width // 2), BF16) if final else None
    scratch = [pltpu.VMEM(inputs.shape[1:], BF16), pltpu.SemaphoreType.DMA(())]
    return pl.pallas_call(
        functools.partial(gradients_body, index, len(previous), bool(final)),
        out_shape=(half, half) if final else sums,
        in_specs=[ANY_SPEC] + vmem(6 + len(previous)) + ([SMEM_SPEC] + vmem(4) if final else []),
        out_specs=vmem(2) if final else vmem(1)[0],
        scratch_shapes=[pltpu.VMEM(sums.shape, F32)] + scratch if final else scratch,
        compiler_params=params(),
        cost_estimate=pl.CostEstimate(
            flops=4 * total * cols * width, bytes_accessed=2 * total * (width + 2 * cols), transcendentals=0
        ),
        name="attention_gradients",
    )(inputs, near, cross, sib, d_query, d_key, d_value, *previous, *final)


def rows_mean(a):
    return jnp.mean(a, axis=-1, keepdims=True)


def norm(values):
    centred = values - rows_mean(values)
    inverse = lax.rsqrt(rows_mean(centred * centred) + EPSILON)
    return centred * inverse, inverse


def norm_back(scaled, normed, inverse):
    return inverse * (scaled - rows_mean(scaled) - normed * rows_mean(scaled * normed))


def col_sum(a):
    return jnp.sum(a, axis=0, keepdims=True)


def feed_body(blocks, pieces, seqs, order, cotangents, *refs):
    count = blocks * pieces
    up_pieces, down_pieces, refs = refs[:count], refs[count : 2 * count], refs[2 * count :]
    shard = order[4]
    mine, keeps, gots, rests = (refs[i * seqs : (i + 1) * seqs] for i in range(4))
    vectors, result, grad_first_attn, grad_rest_attn = refs[4 * seqs : 4 * seqs + 4]
    (grad_low, act, d_inner, d_ffn, low, sums,
     up, down, bias, slope, cotangent, sems, cot_sems) = refs[4 * seqs + 4 :]
    rows, width = result.shape
    quarter = rows // seqs
    depth = width // pieces
    copies = []
    for b in range(blocks):
        for p in range(pieces):
            spot = pl.ds(pl.multiple_of(lax.rem(shard + p, pieces) * depth, depth), depth)
            source = up_pieces[b * pieces + p].at[pl.ds(0, depth), :]
            copies.append(pltpu.make_async_copy(source, up.at[b, spot, :], sems.at[b, p, 0]))
            copies.append(pltpu.make_async_copy(down_pieces[b * pieces + p], down.at[b, spot, :], sems.at[b, p, 1]))
        source = up_pieces[b * pieces].at[pl.ds(depth, EXTRA), :]
        copies.append(pltpu.make_async_copy(source, bias.at[b], sems.at[b, pieces, 0]))
    for i in range(seqs):
        source = cotangents.at[i, slot_rows(order, 0, quarter), :]
        copies.append(pltpu.make_async_copy(source, cotangent.at[pl.ds(i * quarter, quarter), :], cot_sems.at[i]))
    for copy in copies:
        copy.start()
    inputs = jnp.concatenate([r[...].astype(F32) for r in mine], axis=0)
    branch = jnp.concatenate(
        [keeps[i][:quarter, :].astype(F32) + gots[i][:quarter, :].astype(F32) + rests[i][...].astype(F32) for i in range(seqs)],
        axis=0)
    b_out, gain_one, bias_one, b_down, gain_two, bias_two = (vectors[i : i + 1, :] for i in range(6))
    pre = inputs + branch + b_out
    normed_one, inverse_one = norm(pre)
    first = normed_one * gain_one + bias_one
    first_low = first.astype(BF16)
    low[...] = first_low
    for copy in copies:
        copy.wait()

    def ahead(b, total):
        parts = bias[b].astype(F32)
        b_hidden = (parts[0:1, :] + parts[1:2, :]) + parts[2:3, :]
        inner = nn(first_low, up[b]) + b_hidden
        shape = 0.5 * (1.0 + lax.erf(inner * (0.5**0.5)))
        act_low = (inner * shape).astype(BF16)
        act[b] = act_low
        slope[b] = shape + inner * (jnp.exp(-0.5 * inner * inner) * 0.3989422804014327)
        return total + nt(act_low, down[b])

    ffn = lax.fori_loop(0, blocks, ahead, jnp.zeros((rows, width), F32))
    normed_two, inverse_two = norm(first + ffn + b_down)
    result[...] = (normed_two * gain_two + bias_two).astype(BF16)
    grad = cotangent[...].astype(F32)
    grad_second = norm_back(grad * gain_two, normed_two, inverse_two)
    grad_ffn = grad_second.astype(BF16)
    d_ffn[...] = grad_ffn

    def astern(b, total):
        grad_inner = (nn(grad_ffn, down[b]) * slope[b]).astype(BF16)
        d_inner[b] = grad_inner
        return total + nt(grad_inner, up[b])

    grad_first = lax.fori_loop(0, blocks, astern, grad_second)
    grad_pre = norm_back(grad_first * gain_one, normed_one, inverse_one)
    grad_low[...] = grad_pre
    grad_first_attn[...] = grad_pre[:quarter, :].astype(BF16)
    grad_rest_attn[...] = grad_pre[quarter:, :].astype(BF16)
    sums[...] = jnp.concatenate(
        [col_sum(grad_pre), col_sum(grad_first * normed_one), col_sum(grad_first), col_sum(grad_second),
         col_sum(grad * normed_two), col_sum(grad), jnp.zeros((2, width), F32)], axis=0)


def feed_forward(order, ups, downs, cotangents, mine, keeps, gots, rests, vectors):
    seqs = len(mine)
    blocks = len(ups)
    pieces = len(ups[0])
    flat = [w for block in ups for w in block] + [w for block in downs for w in block]
    quarter, width = mine[0].shape
    rows = quarter * seqs
    hidden = ups[0][0].shape[-1]
    shape = jax.ShapeDtypeStruct
    return pl.pallas_call(
        functools.partial(feed_body, blocks, pieces, seqs),
        out_shape=(
            shape((rows, width), BF16),
            shape((quarter, width), BF16),
            shape((rows - quarter, width), BF16),
            shape((rows, width), F32),
            shape((blocks, rows, hidden), BF16),
            shape((blocks, rows, hidden), BF16),
            shape((rows, width), BF16),
            shape((rows, width), BF16),
            shape((8, width), F32),
        ),
        in_specs=[SMEM_SPEC] + [ANY_SPEC] * (1 + len(flat)) + vmem(4 * seqs + 1),
        out_specs=vmem(9),
        scratch_shapes=[
            pltpu.VMEM((blocks, width, hidden), BF16),
            pltpu.VMEM((blocks, width, hidden), BF16),
            pltpu.VMEM((blocks, EXTRA, hidden), BF16),
            pltpu.VMEM((blocks, rows, hidden), F32),
            pltpu.VMEM((rows, width), BF16),
            pltpu.SemaphoreType.DMA((blocks, pieces + 1, 2)),
            pltpu.SemaphoreType.DMA((seqs,)),
        ],
        compiler_params=params(),
        cost_estimate=pl.CostEstimate(
            flops=8 * rows * width * hidden * blocks,
            bytes_accessed=6 * width * hidden * blocks,
            transcendentals=2 * rows * hidden * blocks,
        ),
        name="feed_forward",
    )(order, cotangents, *flat, *mine, *keeps, *gots, *rests, vectors)


def feed_gradients_body(pieces, order, act, d_inner, d_ffn, low, sums, ups, downs, low_turned, ffn_turned):
    depth = low.shape[1] // pieces
    hidden = act.shape[-1]
    shard = order[4]
    grad_inner = d_inner[0]

    @pl.when(pl.program_id(0) == 0)
    def _():
        low_turned[...] = low[...].T
        ffn_turned[...] = d_ffn[...].T

    up = nn(low_turned[...], grad_inner)
    down = nn(ffn_turned[...], act[0])
    extra = jnp.concatenate(
        [sums[:6, :], col_sum(grad_inner.astype(F32)), jnp.zeros((SUMS - 7, hidden), F32)], axis=0).astype(BF16)
    for p in range(pieces):
        spot = lax.rem(p - shard + pieces, pieces)
        ups[0, spot, :depth, :] = up[p * depth : (p + 1) * depth, :].astype(BF16)
        ups[0, spot, depth:, :] = extra
        downs[0, spot, :, :] = down[p * depth : (p + 1) * depth, :].astype(BF16)


def feed_gradients(pieces, first, order, act, d_inner, d_ffn, low, sums):
    blocks, rows, hidden = act.shape
    width = low.shape[1]
    depth = width // pieces
    shape = jax.ShapeDtypeStruct
    pick = pl.BlockSpec((1, rows, hidden), lambda i, order: (first + i, 0, 0))
    whole = pl.BlockSpec((rows, width), lambda i, order: (0, 0))
    return pl.pallas_call(
        functools.partial(feed_gradients_body, pieces),
        out_shape=(shape((2, pieces, depth + SUMS, hidden), BF16), shape((2, pieces, depth, hidden), BF16)),
        grid_spec=pltpu.PrefetchScalarGridSpec(
            num_scalar_prefetch=1,
            grid=(2,),
            in_specs=[pick, pick, whole, whole, pl.BlockSpec((8, width), lambda i, order: (0, 0))],
            out_specs=[
                pl.BlockSpec((1, pieces, depth + SUMS, hidden), lambda i, order: (i, 0, 0, 0)),
                pl.BlockSpec((1, pieces, depth, hidden), lambda i, order: (i, 0, 0, 0)),
            ],
            scratch_shapes=[pltpu.VMEM((width, rows), BF16), pltpu.VMEM((width, rows), BF16)],
        ),
        compiler_params=params(),
        cost_estimate=pl.CostEstimate(
            flops=8 * rows * width * hidden, bytes_accessed=8 * width * hidden, transcendentals=0
        ),
        name="feed_gradients",
    )(order, act, d_inner, d_ffn, low, sums)


def rotated(value, axis, count, shift):
    return lax.ppermute(value, axis, [(i, (i + shift) % count) for i in range(count)])


def across(value):
    return lax.ppermute(value, "tensor", [(i, i ^ 2) for i in range(4)])


def sibling(value):
    return lax.ppermute(value, "tensor", [(i, i ^ 1) for i in range(4)])


def stage(*values):
    return lax.optimization_barrier(values)


def added(*values):
    total = values[0].astype(F32)
    for value in values[1:]:
        total = total + value.astype(F32)
    return total


def rounded(value):
    return lax.reduce_precision(value, 8, 7)


def low_sum(*values):
    return added(*values).astype(BF16)


def thirds(value):
    high = value.astype(BF16)
    rest = value - high.astype(F32)
    middle = rest.astype(BF16)
    return high, middle, (rest - middle.astype(F32)).astype(BF16)


def on_device(shards, contexts, inputs, w_query, b_query, w_key, w_value, b_value, w_out, b_out,
              first_gain, first_bias, w_hidden, b_hidden, w_down, b_down, second_gain, second_bias, cotangent):
    seqs, part, width = inputs.shape
    cols = w_query.shape[1]
    quarter = part // 4
    depth = width // shards
    shard = lax.axis_index("shard")
    context = lax.axis_index("context")
    tensor = lax.axis_index("tensor")
    masks = [1 << i for i in range(contexts.bit_length() - 1)]
    hops = len(masks)
    places = jnp.stack([tensor ^ flip for flip in (0, 2, 1, 3)]).astype(jnp.int32)
    order = jnp.concatenate([places, shard[None].astype(jnp.int32)])

    def along(value, mask):
        return lax.ppermute(value, "context", [(i, i ^ mask) for i in range(contexts)])

    def from_shards(value):
        return [rotated(value, "shard", shards, -r) for r in range(1, shards)]

    def to_shards(parts):
        return [rotated(value, "shard", shards, r) for r, value in enumerate(parts, 1)]

    mine = [lax.dynamic_slice_in_dim(inputs[s], tensor * quarter, quarter, axis=0) for s in range(seqs)]
    nears = [[m] for m in mine]
    cross = [None] * seqs
    four = jnp.stack([w_query.T, w_key.T, w_value.T, w_out])
    line = lax.broadcasted_iota(jnp.int32, (EXTRA, w_hidden.shape[1]), 0)
    biases = jnp.zeros((EXTRA, w_hidden.shape[1]), BF16)
    for i, third in enumerate(thirds(b_hidden)):
        biases = jnp.where(line == i, third[None], biases)
    up_own = jnp.concatenate([w_hidden, lax.optimization_barrier(biases)], axis=0)
    down_own = w_down.T
    vectors = jnp.concatenate([b_out, first_gain, first_bias, b_down, second_gain, second_bias]).reshape(6, width)
    up_x = up_y = up_xy = down_x = down_y = down_xy = other = None
    up_beside, down_beside = {}, {}
    saved = [None] * seqs
    sibs = [None] * seqs
    joined = [None] * seqs
    held = [None] * seqs
    gots = []
    rests = []
    rest = None
    four_all = None
    for j in range(hops + 1 + seqs):
        flights = {}
        found = ()
        s = j - hops - 1
        if s >= 0:
            sibs[s] = sibling(jnp.concatenate([joined[s], cross[s]], axis=0))
            if s >= 1:
                gots.append(sibling(held[s - 1][1]))
                rest = low_sum(held[s - 1][0][quarter:], gots[-1][quarter:])
                sibs[s], rest = stage(sibs[s], rest)
            if s >= 2:
                flights["rest"] = [across(r) for r in rests + [rest]]
            query, key, value, attended, log_total, keep, send = attention_forward(
                places, s, inputs, joined[s], cross[s], sibs[s], four_all, b_query[None], b_value[None])
            saved[s] = (query, key, value, attended, log_total)
            found = (keep, send)
        for q in range(seqs):
            k = j - q
            if 0 <= k < hops:
                flights[f"z{q}"] = along(jnp.concatenate(nears[q], axis=0), masks[hops - 1 - k])
            if k == hops:
                joined[q] = jnp.concatenate(nears[q][1:], axis=0)
                flights[f"x{q}"] = across(joined[q])
        if j == hops - 1:
            flights["up_x"] = across(up_own)
            flights["four"] = from_shards(four)
        if j == hops:
            flights["up_y"] = from_shards(up_own)
            flights["four_all"] = four_all
        if j == hops + 1:
            flights["down_y"] = from_shards(down_own)
            flights["down_x1"] = across(stage(down_own[: depth // 2], sibs[0])[0])
        if j == hops + 2:
            flights["up_xy"] = from_shards(up_x)
            flights["up_c"] = sibling(up_own)
            flights["down_x2"] = across(stage(down_own[depth // 2 :], sibs[1])[0])
        if j == hops + 3:
            flights["down_xy"] = from_shards(down_x)
            flights["down_c"] = sibling(down_own)
        flights, found, four, up_own, down_own, vectors, nears, up_x, up_y, up_xy, down_x, down_y = stage(
            flights, found, four, up_own, down_own, vectors, nears, up_x, up_y, up_xy, down_x, down_y)
        for q in range(seqs):
            if f"z{q}" in flights:
                nears[q] = nears[q] + [flights[f"z{q}"]]
            if f"x{q}" in flights:
                cross[q] = flights[f"x{q}"]
        if s >= 0:
            held[s] = found
            if s >= 1:
                rests.append(rest)
            if s >= 2:
                rests = flights["rest"]
        if j == hops - 1:
            up_x, other = flights["up_x"], flights["four"]
            if shards == 2:
                left = jnp.where(shard == 0, four, other[0])
                right = jnp.where(shard == 0, other[0], four)
                four_all = jnp.concatenate([left, right], axis=2)
            else:
                four_all = lax.all_gather(four, "shard", axis=2, tiled=True)
        if j == hops:
            up_y, four_all = flights["up_y"], flights["four_all"]
        if j == hops + 1:
            down_x1, down_y = flights["down_x1"], flights["down_y"]
        if j == hops + 2:
            up_xy, up_c = flights["up_xy"], flights["up_c"]
            down_x = jnp.concatenate([down_x1, flights["down_x2"]], axis=0)
        if j == hops + 3:
            down_xy, down_c = flights["down_xy"], flights["down_c"]
    gots.append(sibling(held[seqs - 1][1]))
    rests.append(across(low_sum(held[seqs - 1][0][quarter:], gots[-1][quarter:])))
    ups = [[up_own] + up_y, [up_x] + up_xy, [up_c] + [sibling(w) for w in up_y], [sibling(w) for w in [up_x] + up_xy]]
    downs = [[down_own] + down_y, [down_x] + down_xy, [down_c] + [sibling(w) for w in down_y],
             [sibling(w) for w in [down_x] + down_xy]]
    result, g_first, g_rest, grad_low, act, d_inner, d_ffn, low, sums = feed_forward(
        order, ups, downs, cotangent, mine, [h[0] for h in held], gots, rests, vectors)

    up_send, down_send = feed_gradients(shards, 2, order, act, d_inner, d_ffn, low, sums)
    g_first_x, up_send, down_send, d_inner, g_rest = stage(across(g_first), up_send, down_send, d_inner, g_rest)
    up_keep, down_keep = feed_gradients(shards, 0, order, act, d_inner, d_ffn, low, sums)
    g_first_c, up_got, down_got, up_keep, down_keep, result = stage(
        sibling(jnp.concatenate([g_first, g_first_x], axis=0)), sibling(up_send), sibling(down_send),
        up_keep, down_keep, result)

    def up_pair(p):
        return rounded(added(up_keep[0, p], up_got[0, p]))

    def down_pair(slot):
        return rounded(added(down_keep[slot, 0], down_got[slot, 0]))

    def project(s, found, previous=(), final=()):
        return attention_gradients(s, inputs, joined[s], cross[s], sibs[s], *found[:3], previous, final)

    def leaving(terms):
        half = terms[-1].shape[0] // 2
        return low_sum(*[t[half : 2 * half] for t in terms])

    def settle(s, terms):
        return low_sum(grad_low[s * quarter : (s + 1) * quarter], *[t[:quarter] for t in terms])

    def paired(parts):
        own = parts.reshape(parts.shape[0] // quarter, quarter, width)
        return own, across(own)

    def whole(own, swapped):
        count = own.shape[0]
        beside = sibling(jnp.stack([own, swapped]))
        row, side = tensor // 2, tensor % 2
        blocks = []
        for r in range(2):
            for c in range(2):
                here = jnp.where(side == c, own, beside[0])
                there = jnp.where(side == c, swapped, beside[1])
                blocks.append(jnp.where(row == r, here, there))
        return jnp.stack(blocks, axis=1).reshape(count, part, width)

    def split(value, mask):
        half = value.shape[0] // 2
        bit = (context & mask) // mask
        stay = lax.dynamic_slice_in_dim(value, bit * half, half, axis=0)
        return stay, lax.dynamic_slice_in_dim(value, (1 - bit) * half, half, axis=0).astype(BF16)

    def join(value, got, mask):
        lower = (context & mask) == 0
        return jnp.concatenate([jnp.where(lower, value, got), jnp.where(lower, got, value)], axis=0)

    columns = []
    outs = []
    projections = []

    def work(s, *gradient):
        found = attention_backward(places, max(s - 1, 0), *gradient, four_all, *saved[s])
        columns.append(found[6])
        outs.append(found[5])
        return found

    up_leave = [low_sum(up_keep[1, p], up_got[1, p]) for p in range(1, shards)]
    down_leave = [low_sum(down_keep[1, p], down_got[1, p]) for p in range(1, shards)]
    g_first, g_rest, g_rest_x, up_leave, down_leave = stage(g_first, g_rest, across(g_rest), up_leave, down_leave)
    found0 = work(0, g_first, g_first_x, g_first_c)
    up_far, down_far, g_rest_c, found0 = stage(
        [across(u) for u in up_leave], to_shards(down_leave), sibling(jnp.concatenate([g_rest, g_rest_x], axis=0)), found0)
    got0 = sibling(found0[4])
    up_second = [low_sum(up_pair(p), up_far[p - 1]) for p in range(1, shards)]
    down_second = low_sum(down_pair(1), *down_far)
    up_leave = low_sum(up_keep[1, 0], up_got[1, 0])
    down_leave = [low_sum(down_keep[0, p], down_got[0, p]) for p in range(1, shards)]
    g_rest, up_second, down_second, up_leave, down_leave = stage(g_rest, up_second, down_second, up_leave, down_leave)
    found1 = work(1, g_rest, g_rest_x, g_rest_c)
    up_far, down_far, got0, found1 = stage(across(up_leave), to_shards(down_leave), got0, found1)
    terms0 = [found0[3], got0]
    leave = leaving(terms0)
    found0, leave, up_second, down_second, found1 = stage(found0, leave, up_second, down_second, found1)
    up_last = to_shards(up_second)
    down_last = across(down_second)
    flight0 = across(leave)
    projection = project(0, found0)
    got1, projection = stage(sibling(found1[4]), projection)
    terms1 = [found1[3], got1]
    leave = leaving(terms1)
    found1, leave = stage(found1, leave)
    flight1 = across(leave)
    projection = project(1, found1, [projection])
    up_last, down_last, projection = stage(up_last, down_last, projection)
    feed = jnp.concatenate(
        [low_sum(rounded(up_pair(0) + up_far.astype(F32)), *up_last),
         low_sum(rounded(added(down_pair(0), *down_far)), down_last)], axis=0)
    feed_stay, feed_leave = split(feed, masks[0])
    g_rest, feed_leave, feed_stay = stage(g_rest, feed_leave, feed_stay)
    found = work(2, g_rest, g_rest_x, g_rest_c)
    feed_got, flight0, found = stage(along(feed_leave, masks[0]), flight0, found)
    got = sibling(found[4])
    terms0 = terms0 + [flight0]
    z_leave = leaving(terms0)
    feed_stay, feed_leave = split(low_sum(feed_stay, feed_got), masks[1])
    found, z_leave, feed_leave = stage(found, z_leave, feed_leave)
    terms0 = terms0 + [along(z_leave, masks[0])]
    feed_got = along(feed_leave, masks[1])
    biases = added(*columns)[:2].reshape(-1)
    lines = EXTRA * contexts
    biases = jnp.pad(biases, (0, lines * depth - biases.shape[0])).reshape(lines, depth).astype(BF16)
    if shards == 2:
        staying, leave = project(2, found, [projection], (order, biases, *outs))
        got, staying, leave = stage(got, staying, leave)
        attn_got = rotated(leave, "shard", 2, 1)
    else:
        projected = jnp.concatenate([project(2, found, [projection]), added(*outs)[None]], axis=0)
        stacked = jnp.stack([
            jnp.concatenate([projected[..., r * depth : (r + 1) * depth].reshape(4 * cols, depth).astype(BF16), biases], axis=0)
            for r in range(shards)])
        staying = lax.psum_scatter(stacked, "shard", scatter_dimension=0)
        attn_got = jnp.zeros_like(staying)
        got, staying = stage(got, staying)
    terms2 = [found[3], got]
    leave = leaving(terms2)
    half = leave.shape[0] // 2
    flight_first = across(leave[half:])
    flight = across(leave[:half])
    flight1, leave = stage(flight1, leave)
    terms1 = terms1 + [flight1]
    z1_leave = leaving(terms1)
    terms1 = terms1 + [along(z1_leave, masks[0])]
    terms0, z1_leave = stage(terms0, z1_leave)
    z0_leave = leaving(terms0)
    terms0 = terms0 + [along(z0_leave, masks[1])]
    feed_got, z0_leave = stage(feed_got, z0_leave)
    feed = low_sum(feed_stay, feed_got)
    feed_got = along(feed, masks[1])
    flight_first, feed = stage(flight_first, feed)
    z2_leave = leaving([t[: 2 * half] for t in terms2[:2]] + [jnp.concatenate([flight_first, flight_first], axis=0)])
    z2 = along(z2_leave, masks[0])
    terms1, z2_leave = stage(terms1, z2_leave)
    z1_leave = leaving(terms1)
    terms1 = terms1 + [along(z1_leave, masks[1])]
    attn_got, z1_leave = stage(attn_got, z1_leave)
    attn = split(low_sum(staying, attn_got), masks[0])
    attn_got = along(attn[1], masks[0])
    z2, flight, attn_leave = stage(z2, flight, attn[1])
    terms2 = terms2 + [flight, z2]
    z2_leave = leaving(terms2)
    z2 = along(z2_leave, masks[1])
    feed_got, terms0, z2_leave = stage(feed_got, terms0, z2_leave)
    feed = join(feed, feed_got, masks[1])
    feed_got = along(feed, masks[0])
    early = settle(0, terms0)
    attn_got, feed, early = stage(attn_got, feed, early)
    attn = split(low_sum(attn[0], attn_got), masks[1])
    attn_got = along(attn[1], masks[1])
    terms1, attn_leave = stage(terms1, attn[1])
    early = jnp.concatenate([early, settle(1, terms1)], axis=0)
    early_x = paired(early)[1]
    result, early = stage(result, early)
    result_x = paired(result)[1]
    z2, early = stage(z2, early)
    last = settle(2, terms2 + [z2])
    last_x = paired(last)[1]
    attn_got, early_x, last = stage(attn_got, early_x, last)
    attn = low_sum(attn[0], attn_got)
    attn_got = along(attn, masks[1])
    early = whole(early.reshape(early_x.shape), early_x)
    last_x, early, attn = stage(last_x, early, attn)
    last = whole(last.reshape(last_x.shape), last_x)
    attn_got, last = stage(attn_got, last)
    attn = join(attn, attn_got, masks[1])
    attn_got = along(attn, masks[0])
    result_x, feed_got, attn = stage(result_x, feed_got, attn)
    feed = join(feed, feed_got, masks[0])
    outputs = whole(result.reshape(result_x.shape), result_x)
    attn_got, outputs, last, feed = stage(attn_got, outputs, last, feed)
    attn = join(attn, attn_got, masks[0])
    input_grad = jnp.concatenate([early, last], axis=0)

    feed, attn = feed.astype(F32), attn.astype(F32)
    vector_sums = feed[depth : depth + 7]
    bias_sums = attn[4 * cols :].reshape(-1)[: 2 * cols]
    matrices = attn[: 4 * cols].reshape(4, cols, depth)
    return (
        outputs,
        input_grad,
        matrices[0].T,
        bias_sums[:cols],
        matrices[1].T,
        matrices[2].T,
        bias_sums[cols:],
        matrices[3],
        vector_sums[0],
        vector_sums[1],
        vector_sums[2],
        feed[:depth],
        vector_sums[6],
        feed[depth + SUMS :].T,
        vector_sums[3],
        vector_sums[4],
        vector_sums[5],
    )


def solution(mesh):
    shards = mesh.shape["shard"]
    contexts = mesh.shape["context"]
    rows = P("shard", "context", None)
    into = P("shard", "tensor")
    onto = P("tensor", "shard")
    heads = P("tensor")
    return jax.shard_map(
        functools.partial(on_device, shards, contexts),
        mesh=mesh,
        in_specs=(rows, into, heads, into, into, heads, onto, P(), P(), P(), into, heads, onto, P(), P(), P(), rows),
        out_specs=(rows, rows, into, heads, into, into, heads, onto, P(), P(), P(), into, heads, onto, P(), P(), P()),
        check_vma=False,
    )
```

```python
import functools

import jax
import jax.numpy as jnp
from jax import lax
from jax.experimental import pallas as pl
from jax.experimental.pallas import tpu as pltpu
from jax.sharding import PartitionSpec as P

HEAD_DIM = 64
EPSILON = 1e-05
F32 = jnp.float32
BF16 = jnp.bfloat16
VMEM_LIMIT = 56 << 20
EXTRA = 16
SUMS = 64
SMEM_SPEC = pl.BlockSpec(memory_space=pltpu.SMEM)
ANY_SPEC = pl.BlockSpec(memory_space=pl.ANY)


def nn(a, b):
    return jnp.dot(a, b, preferred_element_type=F32)


def nt(a, b):
    return lax.dot_general(a, b, (((1,), (1,)), ((), ())), preferred_element_type=F32)


def vmem(n):
    return [pl.BlockSpec(memory_space=pltpu.VMEM)] * n


def params():
    return pltpu.CompilerParams(vmem_limit_bytes=VMEM_LIMIT)


def head_lanes(shape, head):
    lane = lax.broadcasted_iota(jnp.int32, shape, len(shape) - 1)
    return (lane >= head * HEAD_DIM) & (lane < (head + 1) * HEAD_DIM)


def divisor(size, most):
    while size % most:
        most //= 2
    return most


def slot_rows(places, slot, size):
    return pl.ds(pl.multiple_of(places[slot] * size, size), size)


def forward_body(heads, index, places, inputs, near, cross, sib, w_four, b_query, b_value, query, key, value, attended, log_total, keep, send, q_heads, own, sem):
    fetch = pltpu.make_async_copy(inputs.at[index], own, sem)
    fetch.start()
    part, width = own.shape
    cols = heads * HEAD_DIM
    quarter = part // 4
    factor = HEAD_DIM**-0.5
    w_query, w_key, w_value, w_out = (w_four.at[i] for i in range(4))
    row = part
    for piece in (near, cross, sib, own):
        size = piece.shape[0]
        if piece is own:
            fetch.wait()
            query[...] = ((nt(own[...], w_query[...]) + b_query[...]).astype(BF16).astype(F32) * factor).astype(BF16)
            row = 0
        step = divisor(size, 512)

        def project(i, carry, piece=piece, row=row, step=step):
            rows = piece[pl.ds(i * step, step), :]
            out = pl.ds(row + i * step, step)
            key[out, :] = nt(rows, w_key[...]).astype(BF16)
            value[out, :] = (nt(rows, w_value[...]) + b_value[...]).astype(BF16)
            return carry

        lax.fori_loop(0, size // step, project, 0)
        row += size
    total = key.shape[0]
    block = divisor(total, 1024)
    for head in range(heads):
        mask = head_lanes((part, cols), head)
        q_heads[head] = jnp.where(mask, query[...].astype(F32), 0.0).astype(BF16)
    ones = jnp.ones((16, block), BF16)

    def attend(i, carry):
        rows = pl.ds(pl.multiple_of(i * block, block), block)
        keys = key[rows, :]
        turned = value[rows, :].T
        out = []
        for head in range(heads):
            top, mixed = carry[head]
            scores = nt(keys, q_heads[head])
            new_top = jnp.maximum(top, jnp.max(scores, axis=0, keepdims=True))
            powers = jnp.exp(scores - new_top).astype(BF16)
            values = jnp.concatenate([turned[head * HEAD_DIM : (head + 1) * HEAD_DIM, :], ones], axis=0)
            out.append((new_top, mixed * jnp.exp(top - new_top) + nn(values, powers)))
        return tuple(out)

    start = tuple((jnp.full((1, part), -jnp.inf, F32), jnp.zeros((HEAD_DIM + 16, part), F32)) for _ in range(heads))
    final = lax.fori_loop(0, total // block, attend, start)
    mixes = []
    logs = []
    for top, mixed in final:
        count = mixed[HEAD_DIM : HEAD_DIM + 1, :]
        mixes.append(mixed[:HEAD_DIM, :] / count)
        logs.append(top + jnp.log(count))
    attended[...] = jnp.concatenate(mixes, axis=0).T.astype(BF16)
    log_total[...] = jnp.concatenate(logs + [jnp.zeros((8 - heads, part), F32)], axis=0)
    for out, first in ((keep, 0), (send, 2)):
        for j in range(2):
            rows = attended[slot_rows(places, first + j, quarter), :]
            out[j * quarter : (j + 1) * quarter, :] = nn(rows, w_out[...]).astype(BF16)


def backward_body(heads, nears, index, places, g_own, g_cross, g_sib, w_four, query, key, value, attended, log_total,
                  d_query, d_key, d_value, keep, send, d_out, sums, grad, q_heads, g_heads, dq_turned):
    part, cols = query.shape
    total = key.shape[0]
    quarter = part // 4
    factor = HEAD_DIM**-0.5
    w_query, w_key, w_value, w_out = (w_four.at[i] for i in range(4))
    begin = index * quarter
    middle = g_own.shape[0]
    grad[slot_rows(places, 0, quarter), :] = g_own[begin : begin + quarter, :]
    grad[slot_rows(places, 1, quarter), :] = g_cross[begin : begin + quarter, :]
    grad[slot_rows(places, 2, quarter), :] = g_sib[begin : begin + quarter, :]
    grad[slot_rows(places, 3, quarter), :] = g_sib[middle + begin : middle + begin + quarter, :]
    grad_heads = nt(grad[...], w_out[...]).astype(BF16)
    att = attended[...]
    d_out[...] = nn(att.T, grad[...])
    product = grad_heads.astype(F32) * att.astype(F32)
    picks = jnp.concatenate(
        [jnp.where(head_lanes((1, cols), h), 1.0, 0.0) for h in range(heads)]
        + [jnp.zeros((8 - heads, cols), F32)], axis=0)
    weighted = lax.dot_general(picks, product, (((1,), (1,)), ((), ())), precision=lax.Precision.HIGHEST,
                               preferred_element_type=F32)
    for h in range(heads):
        mask = head_lanes((part, cols), h)
        q_heads[h] = jnp.where(mask, query[...].astype(F32), 0.0).astype(BF16)
        g_heads[h] = jnp.where(mask, grad_heads.astype(F32), 0.0).astype(BF16)
    dq_turned[...] = jnp.zeros_like(dq_turned)
    block = divisor(total, 1024)

    def chunk(i, carry):
        rows = pl.ds(pl.multiple_of(i * block, block), block)
        keys = key[rows, :]
        values = value[rows, :]
        keys_turned = keys.T
        dk = jnp.zeros((block, cols), F32)
        dv = jnp.zeros((block, cols), F32)
        for h in range(heads):
            scores = nt(keys, q_heads[h])
            probs = jnp.exp(scores - log_total[h : h + 1, :])
            d_probs = nt(values, g_heads[h])
            d_scores = (probs * (d_probs - weighted[h : h + 1, :])).astype(BF16)
            dv = dv + nn(probs.astype(BF16), g_heads[h])
            dk = dk + nn(d_scores, q_heads[h])
            own = slice(h * HEAD_DIM, (h + 1) * HEAD_DIM)
            dq_turned[own, :] += nn(keys_turned[own, :], d_scores)
        d_key[rows, :] = dk.astype(BF16)
        d_value[rows, :] = dv.astype(BF16)
        return carry + jnp.sum(dv.astype(BF16).astype(F32), axis=0, keepdims=True)

    sum_value = lax.fori_loop(0, total // block, chunk, jnp.zeros((1, cols), F32))
    dq = (dq_turned[...] * factor).T.astype(BF16)
    d_query[...] = dq
    sums[...] = jnp.concatenate(
        [jnp.sum(dq.astype(F32), axis=0, keepdims=True), sum_value, jnp.zeros((6, cols), F32)], axis=0)

    def back(rows):
        return nn(d_key[rows, :], w_key[...]) + nn(d_value[rows, :], w_value[...])

    row = part
    for out, first in ((keep, 0), (send, 2)):
        for j in range(2):
            mine = slot_rows(places, first + j, quarter)
            begin = j * (quarter + nears)
            out[begin : begin + quarter, :] = (back(mine) + nn(d_query[mine, :], w_query[...])).astype(BF16)
            out[begin + quarter : begin + quarter + nears, :] = back(pl.ds(row, nears)).astype(BF16)
            row += nears


def attention_forward(places, index, inputs, near, cross, sib, w_four, b_query, b_value):
    part, width = inputs.shape[1:]
    cols = w_four.shape[1]
    heads = cols // HEAD_DIM
    total = part + near.shape[0] + cross.shape[0] + sib.shape[0]
    shape = jax.ShapeDtypeStruct
    return pl.pallas_call(
        functools.partial(forward_body, heads, index),
        out_shape=(
            shape((part, cols), BF16),
            shape((total, cols), BF16),
            shape((total, cols), BF16),
            shape((part, cols), BF16),
            shape((8, part), F32),
            shape((part // 2, width), BF16),
            shape((part // 2, width), BF16),
        ),
        in_specs=[SMEM_SPEC, ANY_SPEC] + vmem(6),
        out_specs=vmem(7),
        scratch_shapes=[pltpu.VMEM((heads, part, cols), BF16), pltpu.VMEM((part, width), BF16), pltpu.SemaphoreType.DMA(())],
        compiler_params=params(),
        cost_estimate=pl.CostEstimate(
            flops=4 * total * width * cols + 16 * heads * part * total * HEAD_DIM,
            bytes_accessed=2 * (total * width + 3 * total * cols),
            transcendentals=heads * part * total,
        ),
        name="attention_forward",
    )(places, inputs, near, cross, sib, w_four, b_query, b_value)


def attention_backward(places, index, g_own, g_cross, g_sib, w_four, query, key, value, attended, log_total):
    part, cols = query.shape
    width = w_four.shape[2]
    heads = cols // HEAD_DIM
    total = key.shape[0]
    nears = (total - part) // 4
    shape = jax.ShapeDtypeStruct
    return pl.pallas_call(
        functools.partial(backward_body, heads, nears, index),
        out_shape=(
            shape((part, cols), BF16),
            shape((total, cols), BF16),
            shape((total, cols), BF16),
            shape((total // 2, width), BF16),
            shape((total // 2, width), BF16),
            shape((cols, width), F32),
            shape((8, cols), F32),
        ),
        in_specs=[SMEM_SPEC] + vmem(9),
        out_specs=vmem(7),
        scratch_shapes=[
            pltpu.VMEM((part, width), BF16),
            pltpu.VMEM((heads, part, cols), BF16),
            pltpu.VMEM((heads, part, cols), BF16),
            pltpu.VMEM((cols, part), F32),
        ],
        compiler_params=params(),
        cost_estimate=pl.CostEstimate(
            flops=4 * total * width * cols + 40 * heads * part * total * HEAD_DIM,
            bytes_accessed=2 * (total * width + 5 * total * cols),
            transcendentals=heads * part * total,
        ),
        name="attention_backward",
    )(places, g_own, g_cross, g_sib, w_four, query, key, value, attended, log_total)


def gradients_body(index, adds, last, *refs):
    inputs, near, cross, sib, d_query, d_key, d_value = refs[:7]
    previous, refs = refs[7 : 7 + adds], refs[7 + adds :]
    if last:
        order, biases, d_outs = refs[0], refs[1], refs[2:5]
        staying, leaving, out, own, sem = refs[5:]
    else:
        out, own, sem = refs
    fetch = pltpu.make_async_copy(inputs.at[index], own, sem)
    fetch.start()
    row = own.shape[0]
    for piece in (near, cross, sib, own):
        if piece is own:
            fetch.wait()
            row = 0
        rows = slice(row, row + piece.shape[0])
        for slot, grad in ((1, d_key), (2, d_value)):
            part = nn(grad[rows, :].T, piece[...])
            if piece is not near:
                out[slot] += part
            elif previous:
                out[slot] = previous[0][slot] + part
            else:
                out[slot] = part
        row += piece.shape[0]
    part = nn(d_query[...].T, own[...])
    out[0] = previous[0][0] + part if previous else part
    if not last:
        return
    cols, width = part.shape
    depth = width // 2
    swap = order[4] == 1
    for slot in range(4):
        total = out[slot] if slot < 3 else d_outs[0][...] + d_outs[1][...] + d_outs[2][...]
        left, right = total[:, :depth], total[:, depth:]
        spot = slice(slot * cols, (slot + 1) * cols)
        staying[spot, :] = jnp.where(swap, right, left).astype(BF16)
        leaving[spot, :] = jnp.where(swap, left, right).astype(BF16)
    staying[4 * cols :, :] = biases[...]
    leaving[4 * cols :, :] = biases[...]


def attention_gradients(index, inputs, near, cross, sib, d_query, d_key, d_value, previous=(), final=()):
    cols = d_query.shape[1]
    width = inputs.shape[2]
    total = d_key.shape[0]
    shape = jax.ShapeDtypeStruct
    sums = shape((3, cols, width), F32)
    half = shape((4 * cols + final[1].shape[0], width // 2), BF16) if final else None
    scratch = [pltpu.VMEM(inputs.shape[1:], BF16), pltpu.SemaphoreType.DMA(())]
    return pl.pallas_call(
        functools.partial(gradients_body, index, len(previous), bool(final)),
        out_shape=(half, half) if final else sums,
        in_specs=[ANY_SPEC] + vmem(6 + len(previous)) + ([SMEM_SPEC] + vmem(4) if final else []),
        out_specs=vmem(2) if final else vmem(1)[0],
        scratch_shapes=[pltpu.VMEM(sums.shape, F32)] + scratch if final else scratch,
        compiler_params=params(),
        cost_estimate=pl.CostEstimate(
            flops=4 * total * cols * width, bytes_accessed=2 * total * (width + 2 * cols), transcendentals=0
        ),
        name="attention_gradients",
    )(inputs, near, cross, sib, d_query, d_key, d_value, *previous, *final)


def rows_mean(a):
    return jnp.mean(a, axis=-1, keepdims=True)


def norm(values):
    centred = values - rows_mean(values)
    inverse = lax.rsqrt(rows_mean(centred * centred) + EPSILON)
    return centred * inverse, inverse


def norm_back(scaled, normed, inverse):
    return inverse * (scaled - rows_mean(scaled) - normed * rows_mean(scaled * normed))


def col_sum(a):
    return jnp.sum(a, axis=0, keepdims=True)


def feed_body(blocks, pieces, seqs, order, cotangents, *refs):
    count = blocks * pieces
    up_pieces, down_pieces, refs = refs[:count], refs[count : 2 * count], refs[2 * count :]
    shard = order[4]
    mine, keeps, gots, rests = (refs[i * seqs : (i + 1) * seqs] for i in range(4))
    vectors, result, grad_first_attn, grad_rest_attn = refs[4 * seqs : 4 * seqs + 4]
    (grad_low, act, d_inner, d_ffn, low, sums,
     up, down, bias, slope, cotangent, sems, cot_sems) = refs[4 * seqs + 4 :]
    rows, width = result.shape
    quarter = rows // seqs
    depth = width // pieces
    copies = []
    for b in range(blocks):
        for p in range(pieces):
            spot = pl.ds(pl.multiple_of(lax.rem(shard + p, pieces) * depth, depth), depth)
            source = up_pieces[b * pieces + p].at[pl.ds(0, depth), :]
            copies.append(pltpu.make_async_copy(source, up.at[b, spot, :], sems.at[b, p, 0]))
            copies.append(pltpu.make_async_copy(down_pieces[b * pieces + p], down.at[b, spot, :], sems.at[b, p, 1]))
        source = up_pieces[b * pieces].at[pl.ds(depth, EXTRA), :]
        copies.append(pltpu.make_async_copy(source, bias.at[b], sems.at[b, pieces, 0]))
    for i in range(seqs):
        source = cotangents.at[i, slot_rows(order, 0, quarter), :]
        copies.append(pltpu.make_async_copy(source, cotangent.at[pl.ds(i * quarter, quarter), :], cot_sems.at[i]))
    for copy in copies:
        copy.start()
    inputs = jnp.concatenate([r[...].astype(F32) for r in mine], axis=0)
    branch = jnp.concatenate(
        [keeps[i][:quarter, :].astype(F32) + gots[i][:quarter, :].astype(F32) + rests[i][...].astype(F32) for i in range(seqs)],
        axis=0)
    b_out, gain_one, bias_one, b_down, gain_two, bias_two = (vectors[i : i + 1, :] for i in range(6))
    pre = inputs + branch + b_out
    normed_one, inverse_one = norm(pre)
    first = normed_one * gain_one + bias_one
    first_low = first.astype(BF16)
    low[...] = first_low
    for copy in copies:
        copy.wait()

    def ahead(b, total):
        parts = bias[b].astype(F32)
        b_hidden = (parts[0:1, :] + parts[1:2, :]) + parts[2:3, :]
        inner = nn(first_low, up[b]) + b_hidden
        shape = 0.5 * (1.0 + lax.erf(inner * (0.5**0.5)))
        act_low = (inner * shape).astype(BF16)
        act[b] = act_low
        slope[b] = shape + inner * (jnp.exp(-0.5 * inner * inner) * 0.3989422804014327)
        return total + nt(act_low, down[b])

    ffn = lax.fori_loop(0, blocks, ahead, jnp.zeros((rows, width), F32))
    normed_two, inverse_two = norm(first + ffn + b_down)
    result[...] = (normed_two * gain_two + bias_two).astype(BF16)
    grad = cotangent[...].astype(F32)
    grad_second = norm_back(grad * gain_two, normed_two, inverse_two)
    grad_ffn = grad_second.astype(BF16)
    d_ffn[...] = grad_ffn

    def astern(b, total):
        grad_inner = (nn(grad_ffn, down[b]) * slope[b]).astype(BF16)
        d_inner[b] = grad_inner
        return total + nt(grad_inner, up[b])

    grad_first = lax.fori_loop(0, blocks, astern, grad_second)
    grad_pre = norm_back(grad_first * gain_one, normed_one, inverse_one)
    grad_low[...] = grad_pre
    grad_first_attn[...] = grad_pre[:quarter, :].astype(BF16)
    grad_rest_attn[...] = grad_pre[quarter:, :].astype(BF16)
    sums[...] = jnp.concatenate(
        [col_sum(grad_pre), col_sum(grad_first * normed_one), col_sum(grad_first), col_sum(grad_second),
         col_sum(grad * normed_two), col_sum(grad), jnp.zeros((2, width), F32)], axis=0)


def feed_forward(order, ups, downs, cotangents, mine, keeps, gots, rests, vectors):
    seqs = len(mine)
    blocks = len(ups)
    pieces = len(ups[0])
    flat = [w for block in ups for w in block] + [w for block in downs for w in block]
    quarter, width = mine[0].shape
    rows = quarter * seqs
    hidden = ups[0][0].shape[-1]
    shape = jax.ShapeDtypeStruct
    return pl.pallas_call(
        functools.partial(feed_body, blocks, pieces, seqs),
        out_shape=(
            shape((rows, width), BF16),
            shape((quarter, width), BF16),
            shape((rows - quarter, width), BF16),
            shape((rows, width), F32),
            shape((blocks, rows, hidden), BF16),
            shape((blocks, rows, hidden), BF16),
            shape((rows, width), BF16),
            shape((rows, width), BF16),
            shape((8, width), F32),
        ),
        in_specs=[SMEM_SPEC] + [ANY_SPEC] * (1 + len(flat)) + vmem(4 * seqs + 1),
        out_specs=vmem(9),
        scratch_shapes=[
            pltpu.VMEM((blocks, width, hidden), BF16),
            pltpu.VMEM((blocks, width, hidden), BF16),
            pltpu.VMEM((blocks, EXTRA, hidden), BF16),
            pltpu.VMEM((blocks, rows, hidden), F32),
            pltpu.VMEM((rows, width), BF16),
            pltpu.SemaphoreType.DMA((blocks, pieces + 1, 2)),
            pltpu.SemaphoreType.DMA((seqs,)),
        ],
        compiler_params=params(),
        cost_estimate=pl.CostEstimate(
            flops=8 * rows * width * hidden * blocks,
            bytes_accessed=6 * width * hidden * blocks,
            transcendentals=2 * rows * hidden * blocks,
        ),
        name="feed_forward",
    )(order, cotangents, *flat, *mine, *keeps, *gots, *rests, vectors)


def feed_gradients_body(pieces, order, act, d_inner, d_ffn, low, sums, ups, downs, low_turned, ffn_turned):
    depth = low.shape[1] // pieces
    hidden = act.shape[-1]
    shard = order[4]
    grad_inner = d_inner[0]

    @pl.when(pl.program_id(0) == 0)
    def _():
        low_turned[...] = low[...].T
        ffn_turned[...] = d_ffn[...].T

    up = nn(low_turned[...], grad_inner)
    down = nn(ffn_turned[...], act[0])
    extra = jnp.concatenate(
        [sums[:6, :], col_sum(grad_inner.astype(F32)), jnp.zeros((SUMS - 7, hidden), F32)], axis=0).astype(BF16)
    for p in range(pieces):
        spot = lax.rem(p - shard + pieces, pieces)
        ups[0, spot, :depth, :] = up[p * depth : (p + 1) * depth, :].astype(BF16)
        ups[0, spot, depth:, :] = extra
        downs[0, spot, :, :] = down[p * depth : (p + 1) * depth, :].astype(BF16)


def feed_gradients(pieces, first, order, act, d_inner, d_ffn, low, sums):
    blocks, rows, hidden = act.shape
    width = low.shape[1]
    depth = width // pieces
    shape = jax.ShapeDtypeStruct
    pick = pl.BlockSpec((1, rows, hidden), lambda i, order: (first + i, 0, 0))
    whole = pl.BlockSpec((rows, width), lambda i, order: (0, 0))
    return pl.pallas_call(
        functools.partial(feed_gradients_body, pieces),
        out_shape=(shape((2, pieces, depth + SUMS, hidden), BF16), shape((2, pieces, depth, hidden), BF16)),
        grid_spec=pltpu.PrefetchScalarGridSpec(
            num_scalar_prefetch=1,
            grid=(2,),
            in_specs=[pick, pick, whole, whole, pl.BlockSpec((8, width), lambda i, order: (0, 0))],
            out_specs=[
                pl.BlockSpec((1, pieces, depth + SUMS, hidden), lambda i, order: (i, 0, 0, 0)),
                pl.BlockSpec((1, pieces, depth, hidden), lambda i, order: (i, 0, 0, 0)),
            ],
            scratch_shapes=[pltpu.VMEM((width, rows), BF16), pltpu.VMEM((width, rows), BF16)],
        ),
        compiler_params=params(),
        cost_estimate=pl.CostEstimate(
            flops=8 * rows * width * hidden, bytes_accessed=8 * width * hidden, transcendentals=0
        ),
        name="feed_gradients",
    )(order, act, d_inner, d_ffn, low, sums)


def rotated(value, axis, count, shift):
    return lax.ppermute(value, axis, [(i, (i + shift) % count) for i in range(count)])


def across(value):
    return lax.ppermute(value, "tensor", [(i, i ^ 2) for i in range(4)])


def sibling(value):
    return lax.ppermute(value, "tensor", [(i, i ^ 1) for i in range(4)])


def stage(*values):
    return lax.optimization_barrier(values)


def added(*values):
    total = values[0].astype(F32)
    for value in values[1:]:
        total = total + value.astype(F32)
    return total


def rounded(value):
    return lax.reduce_precision(value, 8, 7)


def low_sum(*values):
    return added(*values).astype(BF16)


def thirds(value):
    high = value.astype(BF16)
    rest = value - high.astype(F32)
    middle = rest.astype(BF16)
    return high, middle, (rest - middle.astype(F32)).astype(BF16)


def on_device(shards, contexts, inputs, w_query, b_query, w_key, w_value, b_value, w_out, b_out,
              first_gain, first_bias, w_hidden, b_hidden, w_down, b_down, second_gain, second_bias, cotangent):
    seqs, part, width = inputs.shape
    cols = w_query.shape[1]
    quarter = part // 4
    depth = width // shards
    shard = lax.axis_index("shard")
    context = lax.axis_index("context")
    tensor = lax.axis_index("tensor")
    masks = [1 << i for i in range(contexts.bit_length() - 1)]
    hops = len(masks)
    places = jnp.stack([tensor ^ flip for flip in (0, 2, 1, 3)]).astype(jnp.int32)
    order = jnp.concatenate([places, shard[None].astype(jnp.int32)])

    def along(value, mask):
        return lax.ppermute(value, "context", [(i, i ^ mask) for i in range(contexts)])

    def from_shards(value):
        return [rotated(value, "shard", shards, -r) for r in range(1, shards)]

    def to_shards(parts):
        return [rotated(value, "shard", shards, r) for r, value in enumerate(parts, 1)]

    mine = [lax.dynamic_slice_in_dim(inputs[s], tensor * quarter, quarter, axis=0) for s in range(seqs)]
    nears = [[m] for m in mine]
    cross = [None] * seqs
    four = jnp.stack([w_query.T, w_key.T, w_value.T, w_out])
    line = lax.broadcasted_iota(jnp.int32, (EXTRA, w_hidden.shape[1]), 0)
    biases = jnp.zeros((EXTRA, w_hidden.shape[1]), BF16)
    for i, third in enumerate(thirds(b_hidden)):
        biases = jnp.where(line == i, third[None], biases)
    up_own = jnp.concatenate([w_hidden, lax.optimization_barrier(biases)], axis=0)
    down_own = w_down.T
    vectors = jnp.concatenate([b_out, first_gain, first_bias, b_down, second_gain, second_bias]).reshape(6, width)
    up_x = up_y = up_xy = down_x = down_y = down_xy = other = None
    up_beside, down_beside = {}, {}
    saved = [None] * seqs
    sibs = [None] * seqs
    joined = [None] * seqs
    held = [None] * seqs
    gots = []
    rests = []
    rest = None
    four_all = None
    for j in range(hops + 1 + seqs):
        flights = {}
        found = ()
        s = j - hops - 1
        if s >= 0:
            sibs[s] = sibling(jnp.concatenate([joined[s], cross[s]], axis=0))
            if s >= 1:
                gots.append(sibling(held[s - 1][1]))
                rest = low_sum(held[s - 1][0][quarter:], gots[-1][quarter:])
                sibs[s], rest = stage(sibs[s], rest)
            if s >= 2:
                flights["rest"] = [across(r) for r in rests + [rest]]
            query, key, value, attended, log_total, keep, send = attention_forward(
                places, s, inputs, joined[s], cross[s], sibs[s], four_all, b_query[None], b_value[None])
            saved[s] = (query, key, value, attended, log_total)
            found = (keep, send)
        for q in range(seqs):
            k = j - q
            if 0 <= k < hops:
                flights[f"z{q}"] = along(jnp.concatenate(nears[q], axis=0), masks[hops - 1 - k])
            if k == hops:
                joined[q] = jnp.concatenate(nears[q][1:], axis=0)
                flights[f"x{q}"] = across(joined[q])
        if j == hops - 1:
            flights["up_x"] = across(up_own)
            flights["four"] = from_shards(four)
        if j == hops:
            flights["up_y"] = from_shards(up_own)
            flights["four_all"] = four_all
        if j == hops + 1:
            flights["down_y"] = from_shards(down_own)
            flights["down_x1"] = across(stage(down_own[: depth // 2], sibs[0])[0])
        if j == hops + 2:
            flights["up_xy"] = from_shards(up_x)
            flights["up_c"] = sibling(up_own)
            flights["down_x2"] = across(stage(down_own[depth // 2 :], sibs[1])[0])
        if j == hops + 3:
            flights["down_xy"] = from_shards(down_x)
            flights["down_c"] = sibling(down_own)
        flights, found, four, up_own, down_own, vectors, nears, up_x, up_y, up_xy, down_x, down_y = stage(
            flights, found, four, up_own, down_own, vectors, nears, up_x, up_y, up_xy, down_x, down_y)
        for q in range(seqs):
            if f"z{q}" in flights:
                nears[q] = nears[q] + [flights[f"z{q}"]]
            if f"x{q}" in flights:
                cross[q] = flights[f"x{q}"]
        if s >= 0:
            held[s] = found
            if s >= 1:
                rests.append(rest)
            if s >= 2:
                rests = flights["rest"]
        if j == hops - 1:
            up_x, other = flights["up_x"], flights["four"]
            if shards == 2:
                left = jnp.where(shard == 0, four, other[0])
                right = jnp.where(shard == 0, other[0], four)
                four_all = jnp.concatenate([left, right], axis=2)
            else:
                four_all = lax.all_gather(four, "shard", axis=2, tiled=True)
        if j == hops:
            up_y, four_all = flights["up_y"], flights["four_all"]
        if j == hops + 1:
            down_x1, down_y = flights["down_x1"], flights["down_y"]
        if j == hops + 2:
            up_xy, up_c = flights["up_xy"], flights["up_c"]
            down_x = jnp.concatenate([down_x1, flights["down_x2"]], axis=0)
        if j == hops + 3:
            down_xy, down_c = flights["down_xy"], flights["down_c"]
    gots.append(sibling(held[seqs - 1][1]))
    rests.append(across(low_sum(held[seqs - 1][0][quarter:], gots[-1][quarter:])))
    ups = [[up_own] + up_y, [up_x] + up_xy, [up_c] + [sibling(w) for w in up_y], [sibling(w) for w in [up_x] + up_xy]]
    downs = [[down_own] + down_y, [down_x] + down_xy, [down_c] + [sibling(w) for w in down_y],
             [sibling(w) for w in [down_x] + down_xy]]
    result, g_first, g_rest, grad_low, act, d_inner, d_ffn, low, sums = feed_forward(
        order, ups, downs, cotangent, mine, [h[0] for h in held], gots, rests, vectors)

    up_send, down_send = feed_gradients(shards, 2, order, act, d_inner, d_ffn, low, sums)
    g_first_x, up_send, down_send, d_inner, g_rest = stage(across(g_first), up_send, down_send, d_inner, g_rest)
    up_keep, down_keep = feed_gradients(shards, 0, order, act, d_inner, d_ffn, low, sums)
    g_first_c, up_got, down_got, up_keep, down_keep, result = stage(
        sibling(jnp.concatenate([g_first, g_first_x], axis=0)), sibling(up_send), sibling(down_send),
        up_keep, down_keep, result)

    def up_pair(p):
        return rounded(added(up_keep[0, p], up_got[0, p]))

    def down_pair(slot):
        return rounded(added(down_keep[slot, 0], down_got[slot, 0]))

    def project(s, found, previous=(), final=()):
        return attention_gradients(s, inputs, joined[s], cross[s], sibs[s], *found[:3], previous, final)

    def leaving(terms):
        half = terms[-1].shape[0] // 2
        return low_sum(*[t[half : 2 * half] for t in terms])

    def settle(s, terms):
        return low_sum(grad_low[s * quarter : (s + 1) * quarter], *[t[:quarter] for t in terms])

    def paired(parts):
        own = parts.reshape(parts.shape[0] // quarter, quarter, width)
        return own, across(own)

    def whole(own, swapped):
        count = own.shape[0]
        beside = sibling(jnp.stack([own, swapped]))
        row, side = tensor // 2, tensor % 2
        blocks = []
        for r in range(2):
            for c in range(2):
                here = jnp.where(side == c, own, beside[0])
                there = jnp.where(side == c, swapped, beside[1])
                blocks.append(jnp.where(row == r, here, there))
        return jnp.stack(blocks, axis=1).reshape(count, part, width)

    def split(value, mask):
        half = value.shape[0] // 2
        bit = (context & mask) // mask
        stay = lax.dynamic_slice_in_dim(value, bit * half, half, axis=0)
        return stay, lax.dynamic_slice_in_dim(value, (1 - bit) * half, half, axis=0).astype(BF16)

    def join(value, got, mask):
        lower = (context & mask) == 0
        return jnp.concatenate([jnp.where(lower, value, got), jnp.where(lower, got, value)], axis=0)

    columns = []
    outs = []
    projections = []

    def work(s, *gradient):
        found = attention_backward(places, max(s - 1, 0), *gradient, four_all, *saved[s])
        columns.append(found[6])
        outs.append(found[5])
        return found

    up_leave = [low_sum(up_keep[1, p], up_got[1, p]) for p in range(1, shards)]
    down_leave = [low_sum(down_keep[1, p], down_got[1, p]) for p in range(1, shards)]
    g_first, g_rest, g_rest_x, up_leave, down_leave = stage(g_first, g_rest, across(g_rest), up_leave, down_leave)
    found0 = work(0, g_first, g_first_x, g_first_c)
    up_far, down_far, g_rest_c, found0 = stage(
        [across(u) for u in up_leave], to_shards(down_leave), sibling(jnp.concatenate([g_rest, g_rest_x], axis=0)), found0)
    got0 = sibling(found0[4])
    up_second = [low_sum(up_pair(p), up_far[p - 1]) for p in range(1, shards)]
    down_second = low_sum(down_pair(1), *down_far)
    up_leave = low_sum(up_keep[1, 0], up_got[1, 0])
    down_leave = [low_sum(down_keep[0, p], down_got[0, p]) for p in range(1, shards)]
    g_rest, up_second, down_second, up_leave, down_leave = stage(g_rest, up_second, down_second, up_leave, down_leave)
    found1 = work(1, g_rest, g_rest_x, g_rest_c)
    up_far, down_far, got0, found1 = stage(across(up_leave), to_shards(down_leave), got0, found1)
    terms0 = [found0[3], got0]
    leave = leaving(terms0)
    found0, leave, up_second, down_second, found1 = stage(found0, leave, up_second, down_second, found1)
    up_last = to_shards(up_second)
    down_last = across(down_second)
    flight0 = across(leave)
    projection = project(0, found0)
    got1, projection = stage(sibling(found1[4]), projection)
    terms1 = [found1[3], got1]
    leave = leaving(terms1)
    found1, leave = stage(found1, leave)
    flight1 = across(leave)
    projection = project(1, found1, [projection])
    up_last, down_last, projection = stage(up_last, down_last, projection)
    feed = jnp.concatenate(
        [low_sum(rounded(up_pair(0) + up_far.astype(F32)), *up_last),
         low_sum(rounded(added(down_pair(0), *down_far)), down_last)], axis=0)
    feed_stay, feed_leave = split(feed, masks[0])
    g_rest, feed_leave, feed_stay = stage(g_rest, feed_leave, feed_stay)
    found = work(2, g_rest, g_rest_x, g_rest_c)
    feed_got, flight0, found = stage(along(feed_leave, masks[0]), flight0, found)
    got = sibling(found[4])
    terms0 = terms0 + [flight0]
    z_leave = leaving(terms0)
    feed_stay, feed_leave = split(low_sum(feed_stay, feed_got), masks[1])
    found, z_leave, feed_leave = stage(found, z_leave, feed_leave)
    terms0 = terms0 + [along(z_leave, masks[0])]
    feed_got = along(feed_leave, masks[1])
    biases = added(*columns)[:2].reshape(-1)
    lines = EXTRA * contexts
    biases = jnp.pad(biases, (0, lines * depth - biases.shape[0])).reshape(lines, depth).astype(BF16)
    if shards == 2:
        staying, leave = project(2, found, [projection], (order, biases, *outs))
        got, staying, leave = stage(got, staying, leave)
        attn_got = rotated(leave, "shard", 2, 1)
    else:
        projected = jnp.concatenate([project(2, found, [projection]), added(*outs)[None]], axis=0)
        stacked = jnp.stack([
            jnp.concatenate([projected[..., r * depth : (r + 1) * depth].reshape(4 * cols, depth).astype(BF16), biases], axis=0)
            for r in range(shards)])
        staying = lax.psum_scatter(stacked, "shard", scatter_dimension=0)
        attn_got = jnp.zeros_like(staying)
        got, staying = stage(got, staying)
    terms2 = [found[3], got]
    leave = leaving(terms2)
    half = leave.shape[0] // 2
    flight_first = across(leave[half:])
    flight = across(leave[:half])
    flight1, leave = stage(flight1, leave)
    terms1 = terms1 + [flight1]
    z1_leave = leaving(terms1)
    terms1 = terms1 + [along(z1_leave, masks[0])]
    terms0, z1_leave = stage(terms0, z1_leave)
    z0_leave = leaving(terms0)
    terms0 = terms0 + [along(z0_leave, masks[1])]
    feed_got, z0_leave = stage(feed_got, z0_leave)
    feed = low_sum(feed_stay, feed_got)
    feed_got = along(feed, masks[1])
    flight_first, feed = stage(flight_first, feed)
    z2_leave = leaving([t[: 2 * half] for t in terms2[:2]] + [jnp.concatenate([flight_first, flight_first], axis=0)])
    z2 = along(z2_leave, masks[0])
    terms1, z2_leave = stage(terms1, z2_leave)
    z1_leave = leaving(terms1)
    terms1 = terms1 + [along(z1_leave, masks[1])]
    attn_got, z1_leave = stage(attn_got, z1_leave)
    attn = split(low_sum(staying, attn_got), masks[0])
    attn_got = along(attn[1], masks[0])
    z2, flight, attn_leave = stage(z2, flight, attn[1])
    terms2 = terms2 + [flight, z2]
    z2_leave = leaving(terms2)
    z2 = along(z2_leave, masks[1])
    feed_got, terms0, z2_leave = stage(feed_got, terms0, z2_leave)
    feed = join(feed, feed_got, masks[1])
    feed_got = along(feed, masks[0])
    early = settle(0, terms0)
    attn_got, feed, early = stage(attn_got, feed, early)
    attn = split(low_sum(attn[0], attn_got), masks[1])
    attn_got = along(attn[1], masks[1])
    terms1, attn_leave = stage(terms1, attn[1])
    early = jnp.concatenate([early, settle(1, terms1)], axis=0)
    early_x = paired(early)[1]
    result, early = stage(result, early)
    result_x = paired(result)[1]
    z2, early = stage(z2, early)
    last = settle(2, terms2 + [z2])
    last_x = paired(last)[1]
    attn_got, early_x, last = stage(attn_got, early_x, last)
    attn = low_sum(attn[0], attn_got)
    attn_got = along(attn, masks[1])
    early = whole(early.reshape(early_x.shape), early_x)
    last_x, attn_got, early, result_x = stage(last_x, attn_got, early, result_x)
    attn = join(attn, attn_got, masks[1])
    attn_got = along(attn, masks[0])
    last = whole(last.reshape(last_x.shape), last_x)
    feed_got, last = stage(feed_got, last)
    feed = join(feed, feed_got, masks[0])
    outputs = whole(result.reshape(result_x.shape), result_x)
    attn_got, outputs, last, feed = stage(attn_got, outputs, last, feed)
    attn = join(attn, attn_got, masks[0])
    input_grad = jnp.concatenate([early, last], axis=0)

    feed, attn = feed.astype(F32), attn.astype(F32)
    vector_sums = feed[depth : depth + 7]
    bias_sums = attn[4 * cols :].reshape(-1)[: 2 * cols]
    matrices = attn[: 4 * cols].reshape(4, cols, depth)
    return (
        outputs,
        input_grad,
        matrices[0].T,
        bias_sums[:cols],
        matrices[1].T,
        matrices[2].T,
        bias_sums[cols:],
        matrices[3],
        vector_sums[0],
        vector_sums[1],
        vector_sums[2],
        feed[:depth],
        vector_sums[6],
        feed[depth + SUMS :].T,
        vector_sums[3],
        vector_sums[4],
        vector_sums[5],
    )


def solution(mesh):
    shards = mesh.shape["shard"]
    contexts = mesh.shape["context"]
    rows = P("shard", "context", None)
    into = P("shard", "tensor")
    onto = P("tensor", "shard")
    heads = P("tensor")
    return jax.shard_map(
        functools.partial(on_device, shards, contexts),
        mesh=mesh,
        in_specs=(rows, into, heads, into, into, heads, onto, P(), P(), P(), into, heads, onto, P(), P(), P(), rows),
        out_specs=(rows, rows, into, heads, into, into, heads, onto, P(), P(), P(), into, heads, onto, P(), P(), P()),
        check_vma=False,
    )
```

```python
import functools

import jax
import jax.numpy as jnp
from jax import lax
from jax.experimental import pallas as pl
from jax.experimental.pallas import tpu as pltpu
from jax.sharding import PartitionSpec as P

HEAD_DIM = 64
EPSILON = 1e-05
F32 = jnp.float32
BF16 = jnp.bfloat16
VMEM_LIMIT = 53 << 20
EXTRA = 16
SUMS = 64
SMEM_SPEC = pl.BlockSpec(memory_space=pltpu.SMEM)
ANY_SPEC = pl.BlockSpec(memory_space=pl.ANY)


def nn(a, b):
    return jnp.dot(a, b, preferred_element_type=F32)


def nt(a, b):
    return lax.dot_general(a, b, (((1,), (1,)), ((), ())), preferred_element_type=F32)


def vmem(n):
    return [pl.BlockSpec(memory_space=pltpu.VMEM)] * n


def params():
    return pltpu.CompilerParams(vmem_limit_bytes=VMEM_LIMIT)


def head_lanes(shape, head):
    lane = lax.broadcasted_iota(jnp.int32, shape, len(shape) - 1)
    return (lane >= head * HEAD_DIM) & (lane < (head + 1) * HEAD_DIM)


def divisor(size, most):
    while size % most:
        most //= 2
    return most


def slot_rows(places, slot, size):
    return pl.ds(pl.multiple_of(places[slot] * size, size), size)


def forward_body(heads, index, places, inputs, near, cross, sib, w_four, b_query, b_value, query, key, value, attended, log_total, keep, send, q_heads, own, sem):
    fetch = pltpu.make_async_copy(inputs.at[index], own, sem)
    fetch.start()
    part, width = own.shape
    cols = heads * HEAD_DIM
    quarter = part // 4
    factor = HEAD_DIM**-0.5
    w_query, w_key, w_value, w_out = (w_four.at[i] for i in range(4))
    row = part
    for piece in (near, cross, sib, own):
        size = piece.shape[0]
        if piece is own:
            fetch.wait()
            query[...] = ((nt(own[...], w_query[...]) + b_query[...]).astype(BF16).astype(F32) * factor).astype(BF16)
            row = 0
        step = divisor(size, 512)

        def project(i, carry, piece=piece, row=row, step=step):
            rows = piece[pl.ds(i * step, step), :]
            out = pl.ds(row + i * step, step)
            key[out, :] = nt(rows, w_key[...]).astype(BF16)
            value[out, :] = (nt(rows, w_value[...]) + b_value[...]).astype(BF16)
            return carry

        lax.fori_loop(0, size // step, project, 0)
        row += size
    total = key.shape[0]
    block = divisor(total, 2048)
    for head in range(heads):
        mask = head_lanes((part, cols), head)
        q_heads[head] = jnp.where(mask, query[...].astype(F32), 0.0).astype(BF16)
    ones = jnp.ones((16, block), BF16)

    def attend(i, carry):
        rows = pl.ds(pl.multiple_of(i * block, block), block)
        keys = key[rows, :]
        turned = value[rows, :].T
        out = []
        for head in range(heads):
            top, mixed = carry[head]
            scores = nt(keys, q_heads[head])
            new_top = jnp.maximum(top, jnp.max(scores, axis=0, keepdims=True))
            powers = jnp.exp(scores - new_top).astype(BF16)
            values = jnp.concatenate([turned[head * HEAD_DIM : (head + 1) * HEAD_DIM, :], ones], axis=0)
            out.append((new_top, mixed * jnp.exp(top - new_top) + nn(values, powers)))
        return tuple(out)

    start = tuple((jnp.full((1, part), -jnp.inf, F32), jnp.zeros((HEAD_DIM + 16, part), F32)) for _ in range(heads))
    final = lax.fori_loop(0, total // block, attend, start)
    mixes = []
    logs = []
    for top, mixed in final:
        count = mixed[HEAD_DIM : HEAD_DIM + 1, :]
        mixes.append(mixed[:HEAD_DIM, :] / count)
        logs.append(top + jnp.log(count))
    attended[...] = jnp.concatenate(mixes, axis=0).T.astype(BF16)
    log_total[...] = jnp.concatenate(logs + [jnp.zeros((8 - heads, part), F32)], axis=0)
    for out, first in ((keep, 0), (send, 2)):
        for j in range(2):
            rows = attended[slot_rows(places, first + j, quarter), :]
            out[j * quarter : (j + 1) * quarter, :] = nn(rows, w_out[...]).astype(BF16)


def backward_body(heads, nears, index, places, g_own, g_cross, g_sib, w_four, query, key, value, attended, log_total,
                  d_query, d_key, d_value, keep, send, d_out, sums, grad, q_heads, g_heads, dq_turned):
    part, cols = query.shape
    total = key.shape[0]
    quarter = part // 4
    factor = HEAD_DIM**-0.5
    w_query, w_key, w_value, w_out = (w_four.at[i] for i in range(4))
    begin = index * quarter
    middle = g_own.shape[0]
    grad[slot_rows(places, 0, quarter), :] = g_own[begin : begin + quarter, :]
    grad[slot_rows(places, 1, quarter), :] = g_cross[begin : begin + quarter, :]
    grad[slot_rows(places, 2, quarter), :] = g_sib[begin : begin + quarter, :]
    grad[slot_rows(places, 3, quarter), :] = g_sib[middle + begin : middle + begin + quarter, :]
    grad_heads = nt(grad[...], w_out[...]).astype(BF16)
    att = attended[...]
    d_out[...] = nn(att.T, grad[...])
    product = grad_heads.astype(F32) * att.astype(F32)
    picks = jnp.concatenate(
        [jnp.where(head_lanes((1, cols), h), 1.0, 0.0) for h in range(heads)]
        + [jnp.zeros((8 - heads, cols), F32)], axis=0)
    weighted = lax.dot_general(picks, product, (((1,), (1,)), ((), ())), precision=lax.Precision.HIGHEST,
                               preferred_element_type=F32)
    for h in range(heads):
        mask = head_lanes((part, cols), h)
        q_heads[h] = jnp.where(mask, query[...].astype(F32), 0.0).astype(BF16)
        g_heads[h] = jnp.where(mask, grad_heads.astype(F32), 0.0).astype(BF16)
    dq_turned[...] = jnp.zeros_like(dq_turned)
    block = divisor(total, 2048)

    def chunk(i, carry):
        rows = pl.ds(pl.multiple_of(i * block, block), block)
        keys = key[rows, :]
        values = value[rows, :]
        keys_turned = keys.T
        dk = jnp.zeros((block, cols), F32)
        dv = jnp.zeros((block, cols), F32)
        for h in range(heads):
            scores = nt(keys, q_heads[h])
            probs = jnp.exp(scores - log_total[h : h + 1, :])
            d_probs = nt(values, g_heads[h])
            d_scores = (probs * (d_probs - weighted[h : h + 1, :])).astype(BF16)
            dv = dv + nn(probs.astype(BF16), g_heads[h])
            dk = dk + nn(d_scores, q_heads[h])
            own = slice(h * HEAD_DIM, (h + 1) * HEAD_DIM)
            dq_turned[own, :] += nn(keys_turned[own, :], d_scores)
        d_key[rows, :] = dk.astype(BF16)
        d_value[rows, :] = dv.astype(BF16)
        return carry + jnp.sum(dv.astype(BF16).astype(F32), axis=0, keepdims=True)

    sum_value = lax.fori_loop(0, total // block, chunk, jnp.zeros((1, cols), F32))
    dq = (dq_turned[...] * factor).T.astype(BF16)
    d_query[...] = dq
    sums[...] = jnp.concatenate(
        [jnp.sum(dq.astype(F32), axis=0, keepdims=True), sum_value, jnp.zeros((6, cols), F32)], axis=0)

    def back(rows):
        return nn(d_key[rows, :], w_key[...]) + nn(d_value[rows, :], w_value[...])

    row = part
    for out, first in ((keep, 0), (send, 2)):
        for j in range(2):
            mine = slot_rows(places, first + j, quarter)
            begin = j * (quarter + nears)
            out[begin : begin + quarter, :] = (back(mine) + nn(d_query[mine, :], w_query[...])).astype(BF16)
            out[begin + quarter : begin + quarter + nears, :] = back(pl.ds(row, nears)).astype(BF16)
            row += nears


def attention_forward(places, index, inputs, near, cross, sib, w_four, b_query, b_value):
    part, width = inputs.shape[1:]
    cols = w_four.shape[1]
    heads = cols // HEAD_DIM
    total = part + near.shape[0] + cross.shape[0] + sib.shape[0]
    shape = jax.ShapeDtypeStruct
    return pl.pallas_call(
        functools.partial(forward_body, heads, index),
        out_shape=(
            shape((part, cols), BF16),
            shape((total, cols), BF16),
            shape((total, cols), BF16),
            shape((part, cols), BF16),
            shape((8, part), F32),
            shape((part // 2, width), BF16),
            shape((part // 2, width), BF16),
        ),
        in_specs=[SMEM_SPEC, ANY_SPEC] + vmem(6),
        out_specs=vmem(7),
        scratch_shapes=[pltpu.VMEM((heads, part, cols), BF16), pltpu.VMEM((part, width), BF16), pltpu.SemaphoreType.DMA(())],
        compiler_params=params(),
        cost_estimate=pl.CostEstimate(
            flops=4 * total * width * cols + 16 * heads * part * total * HEAD_DIM,
            bytes_accessed=2 * (total * width + 3 * total * cols),
            transcendentals=heads * part * total,
        ),
        name="attention_forward",
    )(places, inputs, near, cross, sib, w_four, b_query, b_value)


def attention_backward(places, index, g_own, g_cross, g_sib, w_four, query, key, value, attended, log_total):
    part, cols = query.shape
    width = w_four.shape[2]
    heads = cols // HEAD_DIM
    total = key.shape[0]
    nears = (total - part) // 4
    shape = jax.ShapeDtypeStruct
    return pl.pallas_call(
        functools.partial(backward_body, heads, nears, index),
        out_shape=(
            shape((part, cols), BF16),
            shape((total, cols), BF16),
            shape((total, cols), BF16),
            shape((total // 2, width), BF16),
            shape((total // 2, width), BF16),
            shape((cols, width), F32),
            shape((8, cols), F32),
        ),
        in_specs=[SMEM_SPEC] + vmem(9),
        out_specs=vmem(7),
        scratch_shapes=[
            pltpu.VMEM((part, width), BF16),
            pltpu.VMEM((heads, part, cols), BF16),
            pltpu.VMEM((heads, part, cols), BF16),
            pltpu.VMEM((cols, part), F32),
        ],
        compiler_params=params(),
        cost_estimate=pl.CostEstimate(
            flops=4 * total * width * cols + 40 * heads * part * total * HEAD_DIM,
            bytes_accessed=2 * (total * width + 5 * total * cols),
            transcendentals=heads * part * total,
        ),
        name="attention_backward",
    )(places, g_own, g_cross, g_sib, w_four, query, key, value, attended, log_total)


def gradients_body(index, adds, last, *refs):
    inputs, near, cross, sib, d_query, d_key, d_value = refs[:7]
    previous, refs = refs[7 : 7 + adds], refs[7 + adds :]
    if last:
        order, biases, d_outs = refs[0], refs[1], refs[2:5]
        staying, leaving, out, own, sem = refs[5:]
    else:
        out, own, sem = refs
    fetch = pltpu.make_async_copy(inputs.at[index], own, sem)
    fetch.start()
    row = own.shape[0]
    for piece in (near, cross, sib, own):
        if piece is own:
            fetch.wait()
            row = 0
        rows = slice(row, row + piece.shape[0])
        for slot, grad in ((1, d_key), (2, d_value)):
            part = nn(grad[rows, :].T, piece[...])
            if piece is not near:
                out[slot] += part
            elif previous:
                out[slot] = previous[0][slot] + part
            else:
                out[slot] = part
        row += piece.shape[0]
    part = nn(d_query[...].T, own[...])
    out[0] = previous[0][0] + part if previous else part
    if not last:
        return
    cols, width = part.shape
    depth = width // 2
    swap = order[4] == 1
    for slot in range(4):
        total = out[slot] if slot < 3 else d_outs[0][...] + d_outs[1][...] + d_outs[2][...]
        left, right = total[:, :depth], total[:, depth:]
        spot = slice(slot * cols, (slot + 1) * cols)
        staying[spot, :] = jnp.where(swap, right, left).astype(BF16)
        leaving[spot, :] = jnp.where(swap, left, right).astype(BF16)
    staying[4 * cols :, :] = biases[...]
    leaving[4 * cols :, :] = biases[...]


def attention_gradients(index, inputs, near, cross, sib, d_query, d_key, d_value, previous=(), final=()):
    cols = d_query.shape[1]
    width = inputs.shape[2]
    total = d_key.shape[0]
    shape = jax.ShapeDtypeStruct
    sums = shape((3, cols, width), F32)
    half = shape((4 * cols + final[1].shape[0], width // 2), BF16) if final else None
    scratch = [pltpu.VMEM(inputs.shape[1:], BF16), pltpu.SemaphoreType.DMA(())]
    return pl.pallas_call(
        functools.partial(gradients_body, index, len(previous), bool(final)),
        out_shape=(half, half) if final else sums,
        in_specs=[ANY_SPEC] + vmem(6 + len(previous)) + ([SMEM_SPEC] + vmem(4) if final else []),
        out_specs=vmem(2) if final else vmem(1)[0],
        scratch_shapes=[pltpu.VMEM(sums.shape, F32)] + scratch if final else scratch,
        compiler_params=params(),
        cost_estimate=pl.CostEstimate(
            flops=4 * total * cols * width, bytes_accessed=2 * total * (width + 2 * cols), transcendentals=0
        ),
        name="attention_gradients",
    )(inputs, near, cross, sib, d_query, d_key, d_value, *previous, *final)


def rows_mean(a):
    return jnp.mean(a, axis=-1, keepdims=True)


def norm(values):
    centred = values - rows_mean(values)
    inverse = lax.rsqrt(rows_mean(centred * centred) + EPSILON)
    return centred * inverse, inverse


def norm_back(scaled, normed, inverse):
    return inverse * (scaled - rows_mean(scaled) - normed * rows_mean(scaled * normed))


def col_sum(a):
    return jnp.sum(a, axis=0, keepdims=True)


def feed_body(blocks, pieces, seqs, order, cotangents, *refs):
    count = blocks * pieces
    up_pieces, down_pieces, refs = refs[:count], refs[count : 2 * count], refs[2 * count :]
    shard = order[4]
    mine, keeps, gots, rests = (refs[i * seqs : (i + 1) * seqs] for i in range(4))
    vectors, result, grad_first_attn, grad_rest_attn = refs[4 * seqs : 4 * seqs + 4]
    (grad_low, act, d_inner, d_ffn, low, sums,
     up, down, bias, slope, cotangent, sems, cot_sems) = refs[4 * seqs + 4 :]
    rows, width = result.shape
    quarter = rows // seqs
    depth = width // pieces
    copies = []
    for b in range(blocks):
        for p in range(pieces):
            spot = pl.ds(pl.multiple_of(lax.rem(shard + p, pieces) * depth, depth), depth)
            source = up_pieces[b * pieces + p].at[pl.ds(0, depth), :]
            copies.append(pltpu.make_async_copy(source, up.at[b, spot, :], sems.at[b, p, 0]))
            copies.append(pltpu.make_async_copy(down_pieces[b * pieces + p], down.at[b, spot, :], sems.at[b, p, 1]))
        source = up_pieces[b * pieces].at[pl.ds(depth, EXTRA), :]
        copies.append(pltpu.make_async_copy(source, bias.at[b], sems.at[b, pieces, 0]))
    for i in range(seqs):
        source = cotangents.at[i, slot_rows(order, 0, quarter), :]
        copies.append(pltpu.make_async_copy(source, cotangent.at[pl.ds(i * quarter, quarter), :], cot_sems.at[i]))
    for copy in copies:
        copy.start()
    inputs = jnp.concatenate([r[...].astype(F32) for r in mine], axis=0)
    branch = jnp.concatenate(
        [keeps[i][:quarter, :].astype(F32) + gots[i][:quarter, :].astype(F32) + rests[i][...].astype(F32) for i in range(seqs)],
        axis=0)
    b_out, gain_one, bias_one, b_down, gain_two, bias_two = (vectors[i : i + 1, :] for i in range(6))
    pre = inputs + branch + b_out
    normed_one, inverse_one = norm(pre)
    first = normed_one * gain_one + bias_one
    first_low = first.astype(BF16)
    low[...] = first_low
    for copy in copies:
        copy.wait()

    def ahead(b, total):
        parts = bias[b].astype(F32)
        b_hidden = (parts[0:1, :] + parts[1:2, :]) + parts[2:3, :]
        inner = nn(first_low, up[b]) + b_hidden
        shape = 0.5 * (1.0 + lax.erf(inner * (0.5**0.5)))
        act_low = (inner * shape).astype(BF16)
        act[b] = act_low
        slope[b] = shape + inner * (jnp.exp(-0.5 * inner * inner) * 0.3989422804014327)
        return total + nt(act_low, down[b])

    ffn = lax.fori_loop(0, blocks, ahead, jnp.zeros((rows, width), F32))
    normed_two, inverse_two = norm(first + ffn + b_down)
    result[...] = (normed_two * gain_two + bias_two).astype(BF16)
    grad = cotangent[...].astype(F32)
    grad_second = norm_back(grad * gain_two, normed_two, inverse_two)
    grad_ffn = grad_second.astype(BF16)
    d_ffn[...] = grad_ffn

    def astern(b, total):
        grad_inner = (nn(grad_ffn, down[b]) * slope[b]).astype(BF16)
        d_inner[b] = grad_inner
        return total + nt(grad_inner, up[b])

    grad_first = lax.fori_loop(0, blocks, astern, grad_second)
    grad_pre = norm_back(grad_first * gain_one, normed_one, inverse_one)
    grad_low[...] = grad_pre
    grad_first_attn[...] = grad_pre[:quarter, :].astype(BF16)
    grad_rest_attn[...] = grad_pre[quarter:, :].astype(BF16)
    sums[...] = jnp.concatenate(
        [col_sum(grad_pre), col_sum(grad_first * normed_one), col_sum(grad_first), col_sum(grad_second),
         col_sum(grad * normed_two), col_sum(grad), jnp.zeros((2, width), F32)], axis=0)


def feed_forward(order, ups, downs, cotangents, mine, keeps, gots, rests, vectors):
    seqs = len(mine)
    blocks = len(ups)
    pieces = len(ups[0])
    flat = [w for block in ups for w in block] + [w for block in downs for w in block]
    quarter, width = mine[0].shape
    rows = quarter * seqs
    hidden = ups[0][0].shape[-1]
    shape = jax.ShapeDtypeStruct
    return pl.pallas_call(
        functools.partial(feed_body, blocks, pieces, seqs),
        out_shape=(
            shape((rows, width), BF16),
            shape((quarter, width), BF16),
            shape((rows - quarter, width), BF16),
            shape((rows, width), F32),
            shape((blocks, rows, hidden), BF16),
            shape((blocks, rows, hidden), BF16),
            shape((rows, width), BF16),
            shape((rows, width), BF16),
            shape((8, width), F32),
        ),
        in_specs=[SMEM_SPEC] + [ANY_SPEC] * (1 + len(flat)) + vmem(4 * seqs + 1),
        out_specs=vmem(9),
        scratch_shapes=[
            pltpu.VMEM((blocks, width, hidden), BF16),
            pltpu.VMEM((blocks, width, hidden), BF16),
            pltpu.VMEM((blocks, EXTRA, hidden), BF16),
            pltpu.VMEM((blocks, rows, hidden), F32),
            pltpu.VMEM((rows, width), BF16),
            pltpu.SemaphoreType.DMA((blocks, pieces + 1, 2)),
            pltpu.SemaphoreType.DMA((seqs,)),
        ],
        compiler_params=params(),
        cost_estimate=pl.CostEstimate(
            flops=8 * rows * width * hidden * blocks,
            bytes_accessed=6 * width * hidden * blocks,
            transcendentals=2 * rows * hidden * blocks,
        ),
        name="feed_forward",
    )(order, cotangents, *flat, *mine, *keeps, *gots, *rests, vectors)


def feed_gradients_body(pieces, order, act, d_inner, d_ffn, low, sums, ups, downs, low_turned, ffn_turned):
    depth = low.shape[1] // pieces
    hidden = act.shape[-1]
    shard = order[4]
    grad_inner = d_inner[0]

    @pl.when(pl.program_id(0) == 0)
    def _():
        low_turned[...] = low[...].T
        ffn_turned[...] = d_ffn[...].T

    up = nn(low_turned[...], grad_inner)
    down = nn(ffn_turned[...], act[0])
    extra = jnp.concatenate(
        [sums[:6, :], col_sum(grad_inner.astype(F32)), jnp.zeros((SUMS - 7, hidden), F32)], axis=0).astype(BF16)
    for p in range(pieces):
        spot = lax.rem(p - shard + pieces, pieces)
        ups[0, spot, :depth, :] = up[p * depth : (p + 1) * depth, :].astype(BF16)
        ups[0, spot, depth:, :] = extra
        downs[0, spot, :, :] = down[p * depth : (p + 1) * depth, :].astype(BF16)


def feed_gradients(pieces, first, order, act, d_inner, d_ffn, low, sums):
    blocks, rows, hidden = act.shape
    width = low.shape[1]
    depth = width // pieces
    shape = jax.ShapeDtypeStruct
    pick = pl.BlockSpec((1, rows, hidden), lambda i, order: (first + i, 0, 0))
    whole = pl.BlockSpec((rows, width), lambda i, order: (0, 0))
    return pl.pallas_call(
        functools.partial(feed_gradients_body, pieces),
        out_shape=(shape((2, pieces, depth + SUMS, hidden), BF16), shape((2, pieces, depth, hidden), BF16)),
        grid_spec=pltpu.PrefetchScalarGridSpec(
            num_scalar_prefetch=1,
            grid=(2,),
            in_specs=[pick, pick, whole, whole, pl.BlockSpec((8, width), lambda i, order: (0, 0))],
            out_specs=[
                pl.BlockSpec((1, pieces, depth + SUMS, hidden), lambda i, order: (i, 0, 0, 0)),
                pl.BlockSpec((1, pieces, depth, hidden), lambda i, order: (i, 0, 0, 0)),
            ],
            scratch_shapes=[pltpu.VMEM((width, rows), BF16), pltpu.VMEM((width, rows), BF16)],
        ),
        compiler_params=params(),
        cost_estimate=pl.CostEstimate(
            flops=8 * rows * width * hidden, bytes_accessed=8 * width * hidden, transcendentals=0
        ),
        name="feed_gradients",
    )(order, act, d_inner, d_ffn, low, sums)


def rotated(value, axis, count, shift):
    return lax.ppermute(value, axis, [(i, (i + shift) % count) for i in range(count)])


def across(value):
    return lax.ppermute(value, "tensor", [(i, i ^ 2) for i in range(4)])


def sibling(value):
    return lax.ppermute(value, "tensor", [(i, i ^ 1) for i in range(4)])


def stage(*values):
    return lax.optimization_barrier(values)


def added(*values):
    total = values[0].astype(F32)
    for value in values[1:]:
        total = total + value.astype(F32)
    return total


def rounded(value):
    return lax.reduce_precision(value, 8, 7)


def low_sum(*values):
    return added(*values).astype(BF16)


def thirds(value):
    high = value.astype(BF16)
    rest = value - high.astype(F32)
    middle = rest.astype(BF16)
    return high, middle, (rest - middle.astype(F32)).astype(BF16)


def on_device(shards, contexts, inputs, w_query, b_query, w_key, w_value, b_value, w_out, b_out,
              first_gain, first_bias, w_hidden, b_hidden, w_down, b_down, second_gain, second_bias, cotangent):
    seqs, part, width = inputs.shape
    cols = w_query.shape[1]
    quarter = part // 4
    depth = width // shards
    shard = lax.axis_index("shard")
    context = lax.axis_index("context")
    tensor = lax.axis_index("tensor")
    masks = [1 << i for i in range(contexts.bit_length() - 1)]
    hops = len(masks)
    places = jnp.stack([tensor ^ flip for flip in (0, 2, 1, 3)]).astype(jnp.int32)
    order = jnp.concatenate([places, shard[None].astype(jnp.int32)])

    def along(value, mask):
        return lax.ppermute(value, "context", [(i, i ^ mask) for i in range(contexts)])

    def from_shards(value):
        return [rotated(value, "shard", shards, -r) for r in range(1, shards)]

    def to_shards(parts):
        return [rotated(value, "shard", shards, r) for r, value in enumerate(parts, 1)]

    mine = [lax.dynamic_slice_in_dim(inputs[s], tensor * quarter, quarter, axis=0) for s in range(seqs)]
    nears = [[m] for m in mine]
    cross = [None] * seqs
    four = jnp.stack([w_query.T, w_key.T, w_value.T, w_out])
    line = lax.broadcasted_iota(jnp.int32, (EXTRA, w_hidden.shape[1]), 0)
    biases = jnp.zeros((EXTRA, w_hidden.shape[1]), BF16)
    for i, third in enumerate(thirds(b_hidden)):
        biases = jnp.where(line == i, third[None], biases)
    up_own = jnp.concatenate([w_hidden, lax.optimization_barrier(biases)], axis=0)
    down_own = w_down.T
    vectors = jnp.concatenate([b_out, first_gain, first_bias, b_down, second_gain, second_bias]).reshape(6, width)
    up_x = up_y = up_xy = down_x = down_y = down_xy = other = None
    up_beside, down_beside = {}, {}
    saved = [None] * seqs
    sibs = [None] * seqs
    joined = [None] * seqs
    held = [None] * seqs
    gots = []
    rests = []
    rest = None
    four_all = None
    for j in range(hops + 1 + seqs):
        flights = {}
        found = ()
        s = j - hops - 1
        if s >= 0:
            sibs[s] = sibling(jnp.concatenate([joined[s], cross[s]], axis=0))
            if s >= 1:
                gots.append(sibling(held[s - 1][1]))
                rest = low_sum(held[s - 1][0][quarter:], gots[-1][quarter:])
                sibs[s], rest = stage(sibs[s], rest)
            if s >= 2:
                flights["rest"] = [across(r) for r in rests + [rest]]
            query, key, value, attended, log_total, keep, send = attention_forward(
                places, s, inputs, joined[s], cross[s], sibs[s], four_all, b_query[None], b_value[None])
            saved[s] = (query, key, value, attended, log_total)
            found = (keep, send)
        for q in range(seqs):
            k = j - q
            if 0 <= k < hops:
                flights[f"z{q}"] = along(jnp.concatenate(nears[q], axis=0), masks[hops - 1 - k])
            if k == hops:
                joined[q] = jnp.concatenate(nears[q][1:], axis=0)
                flights[f"x{q}"] = across(joined[q])
        if j == hops - 1:
            flights["up_x"] = across(up_own)
            flights["four"] = from_shards(four)
        if j == hops:
            flights["up_y"] = from_shards(up_own)
            flights["four_all"] = four_all
        if j == hops + 1:
            flights["down_y"] = from_shards(down_own)
            flights["down_x1"] = across(stage(down_own[: depth // 2], sibs[0])[0])
        if j == hops + 2:
            flights["up_xy"] = from_shards(up_x)
            flights["up_c"] = sibling(up_own)
            flights["down_x2"] = across(stage(down_own[depth // 2 :], sibs[1])[0])
        if j == hops + 3:
            flights["down_xy"] = from_shards(down_x)
            flights["down_c"] = sibling(down_own)
        flights, found, four, up_own, down_own, vectors, nears, up_x, up_y, up_xy, down_x, down_y = stage(
            flights, found, four, up_own, down_own, vectors, nears, up_x, up_y, up_xy, down_x, down_y)
        for q in range(seqs):
            if f"z{q}" in flights:
                nears[q] = nears[q] + [flights[f"z{q}"]]
            if f"x{q}" in flights:
                cross[q] = flights[f"x{q}"]
        if s >= 0:
            held[s] = found
            if s >= 1:
                rests.append(rest)
            if s >= 2:
                rests = flights["rest"]
        if j == hops - 1:
            up_x, other = flights["up_x"], flights["four"]
            if shards == 2:
                left = jnp.where(shard == 0, four, other[0])
                right = jnp.where(shard == 0, other[0], four)
                four_all = jnp.concatenate([left, right], axis=2)
            else:
                four_all = lax.all_gather(four, "shard", axis=2, tiled=True)
        if j == hops:
            up_y, four_all = flights["up_y"], flights["four_all"]
        if j == hops + 1:
            down_x1, down_y = flights["down_x1"], flights["down_y"]
        if j == hops + 2:
            up_xy, up_c = flights["up_xy"], flights["up_c"]
            down_x = jnp.concatenate([down_x1, flights["down_x2"]], axis=0)
        if j == hops + 3:
            down_xy, down_c = flights["down_xy"], flights["down_c"]
    gots.append(sibling(held[seqs - 1][1]))
    rests.append(across(low_sum(held[seqs - 1][0][quarter:], gots[-1][quarter:])))
    ups = [[up_own] + up_y, [up_x] + up_xy, [up_c] + [sibling(w) for w in up_y], [sibling(w) for w in [up_x] + up_xy]]
    downs = [[down_own] + down_y, [down_x] + down_xy, [down_c] + [sibling(w) for w in down_y],
             [sibling(w) for w in [down_x] + down_xy]]
    result, g_first, g_rest, grad_low, act, d_inner, d_ffn, low, sums = feed_forward(
        order, ups, downs, cotangent, mine, [h[0] for h in held], gots, rests, vectors)

    up_send, down_send = feed_gradients(shards, 2, order, act, d_inner, d_ffn, low, sums)
    g_first_x, up_send, down_send, d_inner, g_rest = stage(across(g_first), up_send, down_send, d_inner, g_rest)
    up_keep, down_keep = feed_gradients(shards, 0, order, act, d_inner, d_ffn, low, sums)
    g_first_c, up_got, down_got, up_keep, down_keep, result = stage(
        sibling(jnp.concatenate([g_first, g_first_x], axis=0)), sibling(up_send), sibling(down_send),
        up_keep, down_keep, result)

    def up_pair(p):
        return rounded(added(up_keep[0, p], up_got[0, p]))

    def down_pair(slot):
        return rounded(added(down_keep[slot, 0], down_got[slot, 0]))

    def project(s, found, previous=(), final=()):
        return attention_gradients(s, inputs, joined[s], cross[s], sibs[s], *found[:3], previous, final)

    def leaving(terms):
        half = terms[-1].shape[0] // 2
        return low_sum(*[t[half : 2 * half] for t in terms])

    def settle(s, terms):
        return low_sum(grad_low[s * quarter : (s + 1) * quarter], *[t[:quarter] for t in terms])

    def paired(parts):
        own = parts.reshape(parts.shape[0] // quarter, quarter, width)
        return own, across(own)

    def whole(own, swapped):
        count = own.shape[0]
        beside = sibling(jnp.stack([own, swapped]))
        row, side = tensor // 2, tensor % 2
        blocks = []
        for r in range(2):
            for c in range(2):
                here = jnp.where(side == c, own, beside[0])
                there = jnp.where(side == c, swapped, beside[1])
                blocks.append(jnp.where(row == r, here, there))
        return jnp.stack(blocks, axis=1).reshape(count, part, width)

    def split(value, mask):
        half = value.shape[0] // 2
        bit = (context & mask) // mask
        stay = lax.dynamic_slice_in_dim(value, bit * half, half, axis=0)
        return stay, lax.dynamic_slice_in_dim(value, (1 - bit) * half, half, axis=0).astype(BF16)

    def join(value, got, mask):
        lower = (context & mask) == 0
        return jnp.concatenate([jnp.where(lower, value, got), jnp.where(lower, got, value)], axis=0)

    columns = []
    outs = []
    projections = []

    def work(s, *gradient):
        found = attention_backward(places, max(s - 1, 0), *gradient, four_all, *saved[s])
        columns.append(found[6])
        outs.append(found[5])
        return found

    up_leave = [low_sum(up_keep[1, p], up_got[1, p]) for p in range(1, shards)]
    down_leave = [low_sum(down_keep[1, p], down_got[1, p]) for p in range(1, shards)]
    g_first, g_rest, g_rest_x, up_leave, down_leave = stage(g_first, g_rest, across(g_rest), up_leave, down_leave)
    found0 = work(0, g_first, g_first_x, g_first_c)
    up_far, down_far, g_rest_c, found0 = stage(
        [across(u) for u in up_leave], to_shards(down_leave), sibling(jnp.concatenate([g_rest, g_rest_x], axis=0)), found0)
    got0 = sibling(found0[4])
    up_second = [low_sum(up_pair(p), up_far[p - 1]) for p in range(1, shards)]
    down_second = low_sum(down_pair(1), *down_far)
    up_leave = low_sum(up_keep[1, 0], up_got[1, 0])
    down_leave = [low_sum(down_keep[0, p], down_got[0, p]) for p in range(1, shards)]
    g_rest, up_second, down_second, up_leave, down_leave = stage(g_rest, up_second, down_second, up_leave, down_leave)
    found1 = work(1, g_rest, g_rest_x, g_rest_c)
    up_far, down_far, got0, found1 = stage(across(up_leave), to_shards(down_leave), got0, found1)
    terms0 = [found0[3], got0]
    leave = leaving(terms0)
    found0, leave, up_second, down_second, found1 = stage(found0, leave, up_second, down_second, found1)
    up_last = to_shards(up_second)
    down_last = across(down_second)
    flight0 = across(leave)
    projection = project(0, found0)
    got1, projection = stage(sibling(found1[4]), projection)
    terms1 = [found1[3], got1]
    leave = leaving(terms1)
    found1, leave = stage(found1, leave)
    flight1 = across(leave)
    projection = project(1, found1, [projection])
    up_last, down_last, projection = stage(up_last, down_last, projection)
    feed = jnp.concatenate(
        [low_sum(rounded(up_pair(0) + up_far.astype(F32)), *up_last),
         low_sum(rounded(added(down_pair(0), *down_far)), down_last)], axis=0)
    feed_stay, feed_leave = split(feed, masks[0])
    g_rest, feed_leave, feed_stay = stage(g_rest, feed_leave, feed_stay)
    found = work(2, g_rest, g_rest_x, g_rest_c)
    feed_got, flight0, found = stage(along(feed_leave, masks[0]), flight0, found)
    got = sibling(found[4])
    terms0 = terms0 + [flight0]
    z_leave = leaving(terms0)
    feed_stay, feed_leave = split(low_sum(feed_stay, feed_got), masks[1])
    found, z_leave, feed_leave = stage(found, z_leave, feed_leave)
    terms0 = terms0 + [along(z_leave, masks[0])]
    feed_got = along(feed_leave, masks[1])
    biases = added(*columns)[:2].reshape(-1)
    lines = EXTRA * contexts
    biases = jnp.pad(biases, (0, lines * depth - biases.shape[0])).reshape(lines, depth).astype(BF16)
    if shards == 2:
        staying, leave = project(2, found, [projection], (order, biases, *outs))
        got, staying, leave = stage(got, staying, leave)
        attn_got = rotated(leave, "shard", 2, 1)
    else:
        projected = jnp.concatenate([project(2, found, [projection]), added(*outs)[None]], axis=0)
        stacked = jnp.stack([
            jnp.concatenate([projected[..., r * depth : (r + 1) * depth].reshape(4 * cols, depth).astype(BF16), biases], axis=0)
            for r in range(shards)])
        staying = lax.psum_scatter(stacked, "shard", scatter_dimension=0)
        attn_got = jnp.zeros_like(staying)
        got, staying = stage(got, staying)
    terms2 = [found[3], got]
    leave = leaving(terms2)
    half = leave.shape[0] // 2
    flight_first = across(leave[half:])
    flight = across(leave[:half])
    flight1, leave = stage(flight1, leave)
    terms1 = terms1 + [flight1]
    z1_leave = leaving(terms1)
    terms1 = terms1 + [along(z1_leave, masks[0])]
    terms0, z1_leave = stage(terms0, z1_leave)
    z0_leave = leaving(terms0)
    terms0 = terms0 + [along(z0_leave, masks[1])]
    feed_got, z0_leave = stage(feed_got, z0_leave)
    feed = low_sum(feed_stay, feed_got)
    feed_got = along(feed, masks[1])
    flight_first, feed = stage(flight_first, feed)
    z2_leave = leaving([t[: 2 * half] for t in terms2[:2]] + [jnp.concatenate([flight_first, flight_first], axis=0)])
    z2 = along(z2_leave, masks[0])
    terms1, z2_leave = stage(terms1, z2_leave)
    z1_leave = leaving(terms1)
    terms1 = terms1 + [along(z1_leave, masks[1])]
    attn_got, z1_leave = stage(attn_got, z1_leave)
    attn = split(low_sum(staying, attn_got), masks[0])
    attn_got = along(attn[1], masks[0])
    z2, flight, attn_leave = stage(z2, flight, attn[1])
    terms2 = terms2 + [flight, z2]
    z2_leave = leaving(terms2)
    z2 = along(z2_leave, masks[1])
    feed_got, terms0, z2_leave = stage(feed_got, terms0, z2_leave)
    feed = join(feed, feed_got, masks[1])
    feed_got = along(feed, masks[0])
    early = settle(0, terms0)
    attn_got, feed, early = stage(attn_got, feed, early)
    attn = split(low_sum(attn[0], attn_got), masks[1])
    attn_got = along(attn[1], masks[1])
    terms1, attn_leave = stage(terms1, attn[1])
    early = jnp.concatenate([early, settle(1, terms1)], axis=0)
    early_x = paired(early)[1]
    result, early = stage(result, early)
    result_x = paired(result)[1]
    z2, early = stage(z2, early)
    last = settle(2, terms2 + [z2])
    last_x = paired(last)[1]
    attn_got, early_x, last = stage(attn_got, early_x, last)
    attn = low_sum(attn[0], attn_got)
    attn_got = along(attn, masks[1])
    early = whole(early.reshape(early_x.shape), early_x)
    last_x, attn_got, early, result_x = stage(last_x, attn_got, early, result_x)
    attn = join(attn, attn_got, masks[1])
    attn_got = along(attn, masks[0])
    last = whole(last.reshape(last_x.shape), last_x)
    feed_got, last = stage(feed_got, last)
    feed = join(feed, feed_got, masks[0])
    outputs = whole(result.reshape(result_x.shape), result_x)
    attn_got, outputs, last, feed = stage(attn_got, outputs, last, feed)
    attn = join(attn, attn_got, masks[0])
    input_grad = jnp.concatenate([early, last], axis=0)

    feed, attn = feed.astype(F32), attn.astype(F32)
    vector_sums = feed[depth : depth + 7]
    bias_sums = attn[4 * cols :].reshape(-1)[: 2 * cols]
    matrices = attn[: 4 * cols].reshape(4, cols, depth)
    return (
        outputs,
        input_grad,
        matrices[0].T,
        bias_sums[:cols],
        matrices[1].T,
        matrices[2].T,
        bias_sums[cols:],
        matrices[3],
        vector_sums[0],
        vector_sums[1],
        vector_sums[2],
        feed[:depth],
        vector_sums[6],
        feed[depth + SUMS :].T,
        vector_sums[3],
        vector_sums[4],
        vector_sums[5],
    )


def solution(mesh):
    shards = mesh.shape["shard"]
    contexts = mesh.shape["context"]
    rows = P("shard", "context", None)
    into = P("shard", "tensor")
    onto = P("tensor", "shard")
    heads = P("tensor")
    return jax.shard_map(
        functools.partial(on_device, shards, contexts),
        mesh=mesh,
        in_specs=(rows, into, heads, into, into, heads, onto, P(), P(), P(), into, heads, onto, P(), P(), P(), rows),
        out_specs=(rows, rows, into, heads, into, into, heads, onto, P(), P(), P(), into, heads, onto, P(), P(), P()),
        check_vma=False,
    )
```

```python
import functools

import jax
import jax.numpy as jnp
from jax import lax
from jax.experimental import pallas as pl
from jax.experimental.pallas import tpu as pltpu
from jax.sharding import PartitionSpec as P

HEAD_DIM = 64
EPSILON = 1e-05
F32 = jnp.float32
BF16 = jnp.bfloat16
VMEM_LIMIT = 53 << 20
EXTRA = 16
SUMS = 64
SMEM_SPEC = pl.BlockSpec(memory_space=pltpu.SMEM)
ANY_SPEC = pl.BlockSpec(memory_space=pl.ANY)


def nn(a, b):
    return jnp.dot(a, b, preferred_element_type=F32)


def nt(a, b):
    return lax.dot_general(a, b, (((1,), (1,)), ((), ())), preferred_element_type=F32)


def vmem(n):
    return [pl.BlockSpec(memory_space=pltpu.VMEM)] * n


def params():
    return pltpu.CompilerParams(vmem_limit_bytes=VMEM_LIMIT)


def head_lanes(shape, head):
    lane = lax.broadcasted_iota(jnp.int32, shape, len(shape) - 1)
    return (lane >= head * HEAD_DIM) & (lane < (head + 1) * HEAD_DIM)


def divisor(size, most):
    while size % most:
        most //= 2
    return most


def slot_rows(places, slot, size):
    return pl.ds(pl.multiple_of(places[slot] * size, size), size)


def forward_body(heads, index, places, inputs, near, cross, sib, w_four, b_query, b_value, query, key, value, attended, log_total, keep, send, q_heads, own, sem):
    fetch = pltpu.make_async_copy(inputs.at[index], own, sem)
    fetch.start()
    part, width = own.shape
    cols = heads * HEAD_DIM
    quarter = part // 4
    factor = HEAD_DIM**-0.5
    w_query, w_key, w_value, w_out = (w_four.at[i] for i in range(4))
    row = part
    for piece in (near, cross, sib, own):
        size = piece.shape[0]
        if piece is own:
            fetch.wait()
            query[...] = ((nt(own[...], w_query[...]) + b_query[...]).astype(BF16).astype(F32) * factor).astype(BF16)
            row = 0
        step = divisor(size, 512)

        def project(i, carry, piece=piece, row=row, step=step):
            rows = piece[pl.ds(i * step, step), :]
            out = pl.ds(row + i * step, step)
            key[out, :] = nt(rows, w_key[...]).astype(BF16)
            value[out, :] = (nt(rows, w_value[...]) + b_value[...]).astype(BF16)
            return carry

        lax.fori_loop(0, size // step, project, 0)
        row += size
    total = key.shape[0]
    block = divisor(total, 1024)
    for head in range(heads):
        mask = head_lanes((part, cols), head)
        q_heads[head] = jnp.where(mask, query[...].astype(F32), 0.0).astype(BF16)
    ones = jnp.ones((16, block), BF16)

    def attend(i, carry):
        rows = pl.ds(pl.multiple_of(i * block, block), block)
        keys = key[rows, :]
        turned = value[rows, :].T
        out = []
        for head in range(heads):
            top, mixed = carry[head]
            scores = nt(keys, q_heads[head])
            new_top = jnp.maximum(top, jnp.max(scores, axis=0, keepdims=True))
            powers = jnp.exp(scores - new_top).astype(BF16)
            values = jnp.concatenate([turned[head * HEAD_DIM : (head + 1) * HEAD_DIM, :], ones], axis=0)
            out.append((new_top, mixed * jnp.exp(top - new_top) + nn(values, powers)))
        return tuple(out)

    start = tuple((jnp.full((1, part), -jnp.inf, F32), jnp.zeros((HEAD_DIM + 16, part), F32)) for _ in range(heads))
    final = lax.fori_loop(0, total // block, attend, start)
    mixes = []
    logs = []
    for top, mixed in final:
        count = mixed[HEAD_DIM : HEAD_DIM + 1, :]
        mixes.append(mixed[:HEAD_DIM, :] / count)
        logs.append(top + jnp.log(count))
    attended[...] = jnp.concatenate(mixes, axis=0).T.astype(BF16)
    log_total[...] = jnp.concatenate(logs + [jnp.zeros((8 - heads, part), F32)], axis=0)
    for out, first in ((keep, 0), (send, 2)):
        for j in range(2):
            rows = attended[slot_rows(places, first + j, quarter), :]
            out[j * quarter : (j + 1) * quarter, :] = nn(rows, w_out[...]).astype(BF16)


def backward_body(heads, nears, index, places, g_own, g_cross, g_sib, w_four, query, key, value, attended, log_total,
                  d_query, d_key, d_value, keep, send, d_out, sums, grad, q_heads, g_heads, dq_turned):
    part, cols = query.shape
    total = key.shape[0]
    quarter = part // 4
    factor = HEAD_DIM**-0.5
    w_query, w_key, w_value, w_out = (w_four.at[i] for i in range(4))
    begin = index * quarter
    middle = g_own.shape[0]
    grad[slot_rows(places, 0, quarter), :] = g_own[begin : begin + quarter, :]
    grad[slot_rows(places, 1, quarter), :] = g_cross[begin : begin + quarter, :]
    grad[slot_rows(places, 2, quarter), :] = g_sib[begin : begin + quarter, :]
    grad[slot_rows(places, 3, quarter), :] = g_sib[middle + begin : middle + begin + quarter, :]
    grad_heads = nt(grad[...], w_out[...]).astype(BF16)
    att = attended[...]
    d_out[...] = nn(att.T, grad[...])
    product = grad_heads.astype(F32) * att.astype(F32)
    picks = jnp.concatenate(
        [jnp.where(head_lanes((1, cols), h), 1.0, 0.0) for h in range(heads)]
        + [jnp.zeros((8 - heads, cols), F32)], axis=0)
    weighted = lax.dot_general(picks, product, (((1,), (1,)), ((), ())), precision=lax.Precision.HIGHEST,
                               preferred_element_type=F32)
    for h in range(heads):
        mask = head_lanes((part, cols), h)
        q_heads[h] = jnp.where(mask, query[...].astype(F32), 0.0).astype(BF16)
        g_heads[h] = jnp.where(mask, grad_heads.astype(F32), 0.0).astype(BF16)
    dq_turned[...] = jnp.zeros_like(dq_turned)
    block = divisor(total, 1024)

    def chunk(i, carry):
        rows = pl.ds(pl.multiple_of(i * block, block), block)
        keys = key[rows, :]
        values = value[rows, :]
        keys_turned = keys.T
        dk = jnp.zeros((block, cols), F32)
        dv = jnp.zeros((block, cols), F32)
        for h in range(heads):
            scores = nt(keys, q_heads[h])
            probs = jnp.exp(scores - log_total[h : h + 1, :])
            d_probs = nt(values, g_heads[h])
            d_scores = (probs * (d_probs - weighted[h : h + 1, :])).astype(BF16)
            dv = dv + nn(probs.astype(BF16), g_heads[h])
            dk = dk + nn(d_scores, q_heads[h])
            own = slice(h * HEAD_DIM, (h + 1) * HEAD_DIM)
            dq_turned[own, :] += nn(keys_turned[own, :], d_scores)
        d_key[rows, :] = dk.astype(BF16)
        d_value[rows, :] = dv.astype(BF16)
        return carry + jnp.sum(dv.astype(BF16).astype(F32), axis=0, keepdims=True)

    sum_value = lax.fori_loop(0, total // block, chunk, jnp.zeros((1, cols), F32))
    dq = (dq_turned[...] * factor).T.astype(BF16)
    d_query[...] = dq
    sums[...] = jnp.concatenate(
        [jnp.sum(dq.astype(F32), axis=0, keepdims=True), sum_value, jnp.zeros((6, cols), F32)], axis=0)

    def back(rows):
        return nn(d_key[rows, :], w_key[...]) + nn(d_value[rows, :], w_value[...])

    row = part
    for out, first in ((keep, 0), (send, 2)):
        for j in range(2):
            mine = slot_rows(places, first + j, quarter)
            begin = j * (quarter + nears)
            out[begin : begin + quarter, :] = (back(mine) + nn(d_query[mine, :], w_query[...])).astype(BF16)
            out[begin + quarter : begin + quarter + nears, :] = back(pl.ds(row, nears)).astype(BF16)
            row += nears


def attention_forward(places, index, inputs, near, cross, sib, w_four, b_query, b_value):
    part, width = inputs.shape[1:]
    cols = w_four.shape[1]
    heads = cols // HEAD_DIM
    total = part + near.shape[0] + cross.shape[0] + sib.shape[0]
    shape = jax.ShapeDtypeStruct
    return pl.pallas_call(
        functools.partial(forward_body, heads, index),
        out_shape=(
            shape((part, cols), BF16),
            shape((total, cols), BF16),
            shape((total, cols), BF16),
            shape((part, cols), BF16),
            shape((8, part), F32),
            shape((part // 2, width), BF16),
            shape((part // 2, width), BF16),
        ),
        in_specs=[SMEM_SPEC, ANY_SPEC] + vmem(6),
        out_specs=vmem(7),
        scratch_shapes=[pltpu.VMEM((heads, part, cols), BF16), pltpu.VMEM((part, width), BF16), pltpu.SemaphoreType.DMA(())],
        compiler_params=params(),
        cost_estimate=pl.CostEstimate(
            flops=4 * total * width * cols + 16 * heads * part * total * HEAD_DIM,
            bytes_accessed=2 * (total * width + 3 * total * cols),
            transcendentals=heads * part * total,
        ),
        name="attention_forward",
    )(places, inputs, near, cross, sib, w_four, b_query, b_value)


def attention_backward(places, index, g_own, g_cross, g_sib, w_four, query, key, value, attended, log_total):
    part, cols = query.shape
    width = w_four.shape[2]
    heads = cols // HEAD_DIM
    total = key.shape[0]
    nears = (total - part) // 4
    shape = jax.ShapeDtypeStruct
    return pl.pallas_call(
        functools.partial(backward_body, heads, nears, index),
        out_shape=(
            shape((part, cols), BF16),
            shape((total, cols), BF16),
            shape((total, cols), BF16),
            shape((total // 2, width), BF16),
            shape((total // 2, width), BF16),
            shape((cols, width), F32),
            shape((8, cols), F32),
        ),
        in_specs=[SMEM_SPEC] + vmem(9),
        out_specs=vmem(7),
        scratch_shapes=[
            pltpu.VMEM((part, width), BF16),
            pltpu.VMEM((heads, part, cols), BF16),
            pltpu.VMEM((heads, part, cols), BF16),
            pltpu.VMEM((cols, part), F32),
        ],
        compiler_params=params(),
        cost_estimate=pl.CostEstimate(
            flops=4 * total * width * cols + 40 * heads * part * total * HEAD_DIM,
            bytes_accessed=2 * (total * width + 5 * total * cols),
            transcendentals=heads * part * total,
        ),
        name="attention_backward",
    )(places, g_own, g_cross, g_sib, w_four, query, key, value, attended, log_total)


def gradients_body(index, adds, last, *refs):
    inputs, near, cross, sib, d_query, d_key, d_value = refs[:7]
    previous, refs = refs[7 : 7 + adds], refs[7 + adds :]
    if last:
        order, biases, d_outs = refs[0], refs[1], refs[2:5]
        staying, leaving, out, own, sem = refs[5:]
    else:
        out, own, sem = refs
    fetch = pltpu.make_async_copy(inputs.at[index], own, sem)
    fetch.start()
    row = own.shape[0]
    for piece in (near, cross, sib, own):
        if piece is own:
            fetch.wait()
            row = 0
        rows = slice(row, row + piece.shape[0])
        for slot, grad in ((1, d_key), (2, d_value)):
            part = nn(grad[rows, :].T, piece[...])
            if piece is not near:
                out[slot] += part
            elif previous:
                out[slot] = previous[0][slot] + part
            else:
                out[slot] = part
        row += piece.shape[0]
    part = nn(d_query[...].T, own[...])
    out[0] = previous[0][0] + part if previous else part
    if not last:
        return
    cols, width = part.shape
    depth = width // 2
    swap = order[4] == 1
    for slot in range(4):
        total = out[slot] if slot < 3 else d_outs[0][...] + d_outs[1][...] + d_outs[2][...]
        left, right = total[:, :depth], total[:, depth:]
        spot = slice(slot * cols, (slot + 1) * cols)
        staying[spot, :] = jnp.where(swap, right, left).astype(BF16)
        leaving[spot, :] = jnp.where(swap, left, right).astype(BF16)
    staying[4 * cols :, :] = biases[...]
    leaving[4 * cols :, :] = biases[...]


def attention_gradients(index, inputs, near, cross, sib, d_query, d_key, d_value, previous=(), final=()):
    cols = d_query.shape[1]
    width = inputs.shape[2]
    total = d_key.shape[0]
    shape = jax.ShapeDtypeStruct
    sums = shape((3, cols, width), F32)
    half = shape((4 * cols + final[1].shape[0], width // 2), BF16) if final else None
    scratch = [pltpu.VMEM(inputs.shape[1:], BF16), pltpu.SemaphoreType.DMA(())]
    return pl.pallas_call(
        functools.partial(gradients_body, index, len(previous), bool(final)),
        out_shape=(half, half) if final else sums,
        in_specs=[ANY_SPEC] + vmem(6 + len(previous)) + ([SMEM_SPEC] + vmem(4) if final else []),
        out_specs=vmem(2) if final else vmem(1)[0],
        scratch_shapes=[pltpu.VMEM(sums.shape, F32)] + scratch if final else scratch,
        compiler_params=params(),
        cost_estimate=pl.CostEstimate(
            flops=4 * total * cols * width, bytes_accessed=2 * total * (width + 2 * cols), transcendentals=0
        ),
        name="attention_gradients",
    )(inputs, near, cross, sib, d_query, d_key, d_value, *previous, *final)


def rows_mean(a):
    return jnp.mean(a, axis=-1, keepdims=True)


def norm(values):
    centred = values - rows_mean(values)
    inverse = lax.rsqrt(rows_mean(centred * centred) + EPSILON)
    return centred * inverse, inverse


def norm_back(scaled, normed, inverse):
    return inverse * (scaled - rows_mean(scaled) - normed * rows_mean(scaled * normed))


def col_sum(a):
    return jnp.sum(a, axis=0, keepdims=True)


def feed_body(blocks, pieces, seqs, order, cotangents, *refs):
    count = blocks * pieces
    up_pieces, down_pieces, refs = refs[:count], refs[count : 2 * count], refs[2 * count :]
    shard = order[4]
    mine, keeps, gots, rests = (refs[i * seqs : (i + 1) * seqs] for i in range(4))
    vectors, result, grad_first_attn, grad_rest_attn = refs[4 * seqs : 4 * seqs + 4]
    (grad_low, act, d_inner, d_ffn, low, sums,
     up, down, bias, slope, cotangent, sems, cot_sems) = refs[4 * seqs + 4 :]
    rows, width = result.shape
    quarter = rows // seqs
    depth = width // pieces
    copies = []
    for b in range(blocks):
        for p in range(pieces):
            spot = pl.ds(pl.multiple_of(lax.rem(shard + p, pieces) * depth, depth), depth)
            source = up_pieces[b * pieces + p].at[pl.ds(0, depth), :]
            copies.append(pltpu.make_async_copy(source, up.at[b, spot, :], sems.at[b, p, 0]))
            copies.append(pltpu.make_async_copy(down_pieces[b * pieces + p], down.at[b, spot, :], sems.at[b, p, 1]))
        source = up_pieces[b * pieces].at[pl.ds(depth, EXTRA), :]
        copies.append(pltpu.make_async_copy(source, bias.at[b], sems.at[b, pieces, 0]))
    for i in range(seqs):
        source = cotangents.at[i, slot_rows(order, 0, quarter), :]
        copies.append(pltpu.make_async_copy(source, cotangent.at[pl.ds(i * quarter, quarter), :], cot_sems.at[i]))
    for copy in copies:
        copy.start()
    inputs = jnp.concatenate([r[...].astype(F32) for r in mine], axis=0)
    branch = jnp.concatenate(
        [keeps[i][:quarter, :].astype(F32) + gots[i][:quarter, :].astype(F32) + rests[i][...].astype(F32) for i in range(seqs)],
        axis=0)
    b_out, gain_one, bias_one, b_down, gain_two, bias_two = (vectors[i : i + 1, :] for i in range(6))
    pre = inputs + branch + b_out
    normed_one, inverse_one = norm(pre)
    first = normed_one * gain_one + bias_one
    first_low = first.astype(BF16)
    low[...] = first_low
    for copy in copies:
        copy.wait()

    def ahead(b, total):
        parts = bias[b].astype(F32)
        b_hidden = (parts[0:1, :] + parts[1:2, :]) + parts[2:3, :]
        inner = nn(first_low, up[b]) + b_hidden
        shape = 0.5 * (1.0 + lax.erf(inner * (0.5**0.5)))
        act_low = (inner * shape).astype(BF16)
        act[b] = act_low
        slope[b] = shape + inner * (jnp.exp(-0.5 * inner * inner) * 0.3989422804014327)
        return total + nt(act_low, down[b])

    ffn = lax.fori_loop(0, blocks, ahead, jnp.zeros((rows, width), F32))
    normed_two, inverse_two = norm(first + ffn + b_down)
    result[...] = (normed_two * gain_two + bias_two).astype(BF16)
    grad = cotangent[...].astype(F32)
    grad_second = norm_back(grad * gain_two, normed_two, inverse_two)
    grad_ffn = grad_second.astype(BF16)
    d_ffn[...] = grad_ffn

    def astern(b, total):
        grad_inner = (nn(grad_ffn, down[b]) * slope[b]).astype(BF16)
        d_inner[b] = grad_inner
        return total + nt(grad_inner, up[b])

    grad_first = lax.fori_loop(0, blocks, astern, grad_second)
    grad_pre = norm_back(grad_first * gain_one, normed_one, inverse_one)
    grad_low[...] = grad_pre
    grad_first_attn[...] = grad_pre[:quarter, :].astype(BF16)
    grad_rest_attn[...] = grad_pre[quarter:, :].astype(BF16)
    sums[...] = jnp.concatenate(
        [col_sum(grad_pre), col_sum(grad_first * normed_one), col_sum(grad_first), col_sum(grad_second),
         col_sum(grad * normed_two), col_sum(grad), jnp.zeros((2, width), F32)], axis=0)


def feed_forward(order, ups, downs, cotangents, mine, keeps, gots, rests, vectors):
    seqs = len(mine)
    blocks = len(ups)
    pieces = len(ups[0])
    flat = [w for block in ups for w in block] + [w for block in downs for w in block]
    quarter, width = mine[0].shape
    rows = quarter * seqs
    hidden = ups[0][0].shape[-1]
    shape = jax.ShapeDtypeStruct
    return pl.pallas_call(
        functools.partial(feed_body, blocks, pieces, seqs),
        out_shape=(
            shape((rows, width), BF16),
            shape((quarter, width), BF16),
            shape((rows - quarter, width), BF16),
            shape((rows, width), F32),
            shape((blocks, rows, hidden), BF16),
            shape((blocks, rows, hidden), BF16),
            shape((rows, width), BF16),
            shape((rows, width), BF16),
            shape((8, width), F32),
        ),
        in_specs=[SMEM_SPEC] + [ANY_SPEC] * (1 + len(flat)) + vmem(4 * seqs + 1),
        out_specs=vmem(9),
        scratch_shapes=[
            pltpu.VMEM((blocks, width, hidden), BF16),
            pltpu.VMEM((blocks, width, hidden), BF16),
            pltpu.VMEM((blocks, EXTRA, hidden), BF16),
            pltpu.VMEM((blocks, rows, hidden), F32),
            pltpu.VMEM((rows, width), BF16),
            pltpu.SemaphoreType.DMA((blocks, pieces + 1, 2)),
            pltpu.SemaphoreType.DMA((seqs,)),
        ],
        compiler_params=params(),
        cost_estimate=pl.CostEstimate(
            flops=8 * rows * width * hidden * blocks,
            bytes_accessed=6 * width * hidden * blocks,
            transcendentals=2 * rows * hidden * blocks,
        ),
        name="feed_forward",
    )(order, cotangents, *flat, *mine, *keeps, *gots, *rests, vectors)


def feed_gradients_body(pieces, order, act, d_inner, d_ffn, low, sums, ups, downs, low_turned, ffn_turned):
    depth = low.shape[1] // pieces
    hidden = act.shape[-1]
    shard = order[4]
    grad_inner = d_inner[0]

    @pl.when(pl.program_id(0) == 0)
    def _():
        low_turned[...] = low[...].T
        ffn_turned[...] = d_ffn[...].T

    up = nn(low_turned[...], grad_inner)
    down = nn(ffn_turned[...], act[0])
    extra = jnp.concatenate(
        [sums[:6, :], col_sum(grad_inner.astype(F32)), jnp.zeros((SUMS - 7, hidden), F32)], axis=0).astype(BF16)
    for p in range(pieces):
        spot = lax.rem(p - shard + pieces, pieces)
        ups[0, spot, :depth, :] = up[p * depth : (p + 1) * depth, :].astype(BF16)
        ups[0, spot, depth:, :] = extra
        downs[0, spot, :, :] = down[p * depth : (p + 1) * depth, :].astype(BF16)


def feed_gradients(pieces, first, order, act, d_inner, d_ffn, low, sums):
    blocks, rows, hidden = act.shape
    width = low.shape[1]
    depth = width // pieces
    shape = jax.ShapeDtypeStruct
    pick = pl.BlockSpec((1, rows, hidden), lambda i, order: (first + i, 0, 0))
    whole = pl.BlockSpec((rows, width), lambda i, order: (0, 0))
    return pl.pallas_call(
        functools.partial(feed_gradients_body, pieces),
        out_shape=(shape((2, pieces, depth + SUMS, hidden), BF16), shape((2, pieces, depth, hidden), BF16)),
        grid_spec=pltpu.PrefetchScalarGridSpec(
            num_scalar_prefetch=1,
            grid=(2,),
            in_specs=[pick, pick, whole, whole, pl.BlockSpec((8, width), lambda i, order: (0, 0))],
            out_specs=[
                pl.BlockSpec((1, pieces, depth + SUMS, hidden), lambda i, order: (i, 0, 0, 0)),
                pl.BlockSpec((1, pieces, depth, hidden), lambda i, order: (i, 0, 0, 0)),
            ],
            scratch_shapes=[pltpu.VMEM((width, rows), BF16), pltpu.VMEM((width, rows), BF16)],
        ),
        compiler_params=params(),
        cost_estimate=pl.CostEstimate(
            flops=8 * rows * width * hidden, bytes_accessed=8 * width * hidden, transcendentals=0
        ),
        name="feed_gradients",
    )(order, act, d_inner, d_ffn, low, sums)


def rotated(value, axis, count, shift):
    return lax.ppermute(value, axis, [(i, (i + shift) % count) for i in range(count)])


def across(value):
    return lax.ppermute(value, "tensor", [(i, i ^ 2) for i in range(4)])


def sibling(value):
    return lax.ppermute(value, "tensor", [(i, i ^ 1) for i in range(4)])


def stage(*values):
    return lax.optimization_barrier(values)


def added(*values):
    total = values[0].astype(F32)
    for value in values[1:]:
        total = total + value.astype(F32)
    return total


def rounded(value):
    return lax.reduce_precision(value, 8, 7)


def low_sum(*values):
    return added(*values).astype(BF16)


def thirds(value):
    high = value.astype(BF16)
    rest = value - high.astype(F32)
    middle = rest.astype(BF16)
    return high, middle, (rest - middle.astype(F32)).astype(BF16)


def on_device(shards, contexts, inputs, w_query, b_query, w_key, w_value, b_value, w_out, b_out,
              first_gain, first_bias, w_hidden, b_hidden, w_down, b_down, second_gain, second_bias, cotangent):
    seqs, part, width = inputs.shape
    cols = w_query.shape[1]
    quarter = part // 4
    depth = width // shards
    shard = lax.axis_index("shard")
    context = lax.axis_index("context")
    tensor = lax.axis_index("tensor")
    masks = [1 << i for i in range(contexts.bit_length() - 1)]
    hops = len(masks)
    places = jnp.stack([tensor ^ flip for flip in (0, 2, 1, 3)]).astype(jnp.int32)
    order = jnp.concatenate([places, shard[None].astype(jnp.int32)])

    def along(value, mask):
        return lax.ppermute(value, "context", [(i, i ^ mask) for i in range(contexts)])

    def from_shards(value):
        return [rotated(value, "shard", shards, -r) for r in range(1, shards)]

    def to_shards(parts):
        return [rotated(value, "shard", shards, r) for r, value in enumerate(parts, 1)]

    mine = [lax.dynamic_slice_in_dim(inputs[s], tensor * quarter, quarter, axis=0) for s in range(seqs)]
    nears = [[m] for m in mine]
    cross = [None] * seqs
    four = jnp.stack([w_query.T, w_key.T, w_value.T, w_out])
    line = lax.broadcasted_iota(jnp.int32, (EXTRA, w_hidden.shape[1]), 0)
    biases = jnp.zeros((EXTRA, w_hidden.shape[1]), BF16)
    for i, third in enumerate(thirds(b_hidden)):
        biases = jnp.where(line == i, third[None], biases)
    up_own = jnp.concatenate([w_hidden, lax.optimization_barrier(biases)], axis=0)
    down_own = w_down.T
    vectors = jnp.concatenate([b_out, first_gain, first_bias, b_down, second_gain, second_bias]).reshape(6, width)
    up_x = up_y = up_xy = down_x = down_y = down_xy = other = None
    up_beside, down_beside = {}, {}
    saved = [None] * seqs
    sibs = [None] * seqs
    joined = [None] * seqs
    held = [None] * seqs
    gots = []
    rests = []
    rest = None
    four_all = None
    for j in range(hops + 1 + seqs):
        flights = {}
        found = ()
        s = j - hops - 1
        if s >= 0:
            sibs[s] = sibling(jnp.concatenate([joined[s], cross[s]], axis=0))
            if s >= 1:
                gots.append(sibling(held[s - 1][1]))
                rest = low_sum(held[s - 1][0][quarter:], gots[-1][quarter:])
                sibs[s], rest = stage(sibs[s], rest)
            if s >= 2:
                flights["rest"] = [across(r) for r in rests + [rest]]
            query, key, value, attended, log_total, keep, send = attention_forward(
                places, s, inputs, joined[s], cross[s], sibs[s], four_all, b_query[None], b_value[None])
            saved[s] = (query, key, value, attended, log_total)
            found = (keep, send)
        for q in range(seqs):
            k = j - q
            if 0 <= k < hops:
                flights[f"z{q}"] = along(jnp.concatenate(nears[q], axis=0), masks[hops - 1 - k])
            if k == hops:
                joined[q] = jnp.concatenate(nears[q][1:], axis=0)
                flights[f"x{q}"] = across(joined[q])
        if j == hops - 1:
            flights["up_x"] = across(up_own)
            flights["four"] = from_shards(four)
        if j == hops:
            flights["up_y"] = from_shards(up_own)
            flights["four_all"] = four_all
        if j == hops + 1:
            flights["down_y"] = from_shards(down_own)
            flights["down_x1"] = across(stage(down_own[: depth // 2], sibs[0])[0])
        if j == hops + 2:
            flights["up_xy"] = from_shards(up_x)
            flights["up_c"] = sibling(up_own)
            flights["down_x2"] = across(stage(down_own[depth // 2 :], sibs[1])[0])
        if j == hops + 3:
            flights["down_xy"] = from_shards(down_x)
            flights["down_c"] = sibling(down_own)
        flights, found, four, up_own, down_own, vectors, nears, up_x, up_y, up_xy, down_x, down_y = stage(
            flights, found, four, up_own, down_own, vectors, nears, up_x, up_y, up_xy, down_x, down_y)
        for q in range(seqs):
            if f"z{q}" in flights:
                nears[q] = nears[q] + [flights[f"z{q}"]]
            if f"x{q}" in flights:
                cross[q] = flights[f"x{q}"]
        if s >= 0:
            held[s] = found
            if s >= 1:
                rests.append(rest)
            if s >= 2:
                rests = flights["rest"]
        if j == hops - 1:
            up_x, other = flights["up_x"], flights["four"]
            if shards == 2:
                left = jnp.where(shard == 0, four, other[0])
                right = jnp.where(shard == 0, other[0], four)
                four_all = jnp.concatenate([left, right], axis=2)
            else:
                four_all = lax.all_gather(four, "shard", axis=2, tiled=True)
        if j == hops:
            up_y, four_all = flights["up_y"], flights["four_all"]
        if j == hops + 1:
            down_x1, down_y = flights["down_x1"], flights["down_y"]
        if j == hops + 2:
            up_xy, up_c = flights["up_xy"], flights["up_c"]
            down_x = jnp.concatenate([down_x1, flights["down_x2"]], axis=0)
        if j == hops + 3:
            down_xy, down_c = flights["down_xy"], flights["down_c"]
    gots.append(sibling(held[seqs - 1][1]))
    rests.append(across(low_sum(held[seqs - 1][0][quarter:], gots[-1][quarter:])))
    ups = [[up_own] + up_y, [up_x] + up_xy, [up_c] + [sibling(w) for w in up_y], [sibling(w) for w in [up_x] + up_xy]]
    downs = [[down_own] + down_y, [down_x] + down_xy, [down_c] + [sibling(w) for w in down_y],
             [sibling(w) for w in [down_x] + down_xy]]
    result, g_first, g_rest, grad_low, act, d_inner, d_ffn, low, sums = feed_forward(
        order, ups, downs, cotangent, mine, [h[0] for h in held], gots, rests, vectors)

    up_send, down_send = feed_gradients(shards, 2, order, act, d_inner, d_ffn, low, sums)
    g_first_x, up_send, down_send, d_inner, g_rest = stage(across(g_first), up_send, down_send, d_inner, g_rest)
    up_keep, down_keep = feed_gradients(shards, 0, order, act, d_inner, d_ffn, low, sums)
    g_first_c, up_got, down_got, up_keep, down_keep, result = stage(
        sibling(jnp.concatenate([g_first, g_first_x], axis=0)), sibling(up_send), sibling(down_send),
        up_keep, down_keep, result)

    def up_pair(p):
        return rounded(added(up_keep[0, p], up_got[0, p]))

    def down_pair(slot):
        return rounded(added(down_keep[slot, 0], down_got[slot, 0]))

    def project(s, found, previous=(), final=()):
        return attention_gradients(s, inputs, joined[s], cross[s], sibs[s], *found[:3], previous, final)

    def leaving(terms):
        half = terms[-1].shape[0] // 2
        return low_sum(*[t[half : 2 * half] for t in terms])

    def settle(s, terms):
        return low_sum(grad_low[s * quarter : (s + 1) * quarter], *[t[:quarter] for t in terms])

    def paired(parts):
        own = parts.reshape(parts.shape[0] // quarter, quarter, width)
        return own, across(own)

    def whole(own, swapped):
        count = own.shape[0]
        beside = sibling(jnp.stack([own, swapped]))
        row, side = tensor // 2, tensor % 2
        blocks = []
        for r in range(2):
            for c in range(2):
                here = jnp.where(side == c, own, beside[0])
                there = jnp.where(side == c, swapped, beside[1])
                blocks.append(jnp.where(row == r, here, there))
        return jnp.stack(blocks, axis=1).reshape(count, part, width)

    def split(value, mask):
        half = value.shape[0] // 2
        bit = (context & mask) // mask
        stay = lax.dynamic_slice_in_dim(value, bit * half, half, axis=0)
        return stay, lax.dynamic_slice_in_dim(value, (1 - bit) * half, half, axis=0).astype(BF16)

    def join(value, got, mask):
        lower = (context & mask) == 0
        return jnp.concatenate([jnp.where(lower, value, got), jnp.where(lower, got, value)], axis=0)

    columns = []
    outs = []
    projections = []

    def work(s, *gradient):
        found = attention_backward(places, max(s - 1, 0), *gradient, four_all, *saved[s])
        columns.append(found[6])
        outs.append(found[5])
        return found

    up_leave = [low_sum(up_keep[1, p], up_got[1, p]) for p in range(1, shards)]
    down_leave = [low_sum(down_keep[1, p], down_got[1, p]) for p in range(1, shards)]
    g_first, g_rest, g_rest_x, up_leave, down_leave = stage(g_first, g_rest, across(g_rest), up_leave, down_leave)
    found0 = work(0, g_first, g_first_x, g_first_c)
    up_far, down_far, g_rest_c, found0 = stage(
        [across(u) for u in up_leave], to_shards(down_leave), sibling(jnp.concatenate([g_rest, g_rest_x], axis=0)), found0)
    got0 = sibling(found0[4])
    up_second = [low_sum(up_pair(p), up_far[p - 1]) for p in range(1, shards)]
    down_second = low_sum(down_pair(1), *down_far)
    up_leave = low_sum(up_keep[1, 0], up_got[1, 0])
    down_leave = [low_sum(down_keep[0, p], down_got[0, p]) for p in range(1, shards)]
    g_rest, up_second, down_second, up_leave, down_leave = stage(g_rest, up_second, down_second, up_leave, down_leave)
    found1 = work(1, g_rest, g_rest_x, g_rest_c)
    up_far, down_far, got0, found1 = stage(across(up_leave), to_shards(down_leave), got0, found1)
    terms0 = [found0[3], got0]
    leave = leaving(terms0)
    found0, leave, up_second, down_second, found1 = stage(found0, leave, up_second, down_second, found1)
    up_last = to_shards(up_second)
    down_last = across(down_second)
    flight0 = across(leave)
    projection = project(0, found0)
    got1, projection = stage(sibling(found1[4]), projection)
    terms1 = [found1[3], got1]
    leave = leaving(terms1)
    found1, leave = stage(found1, leave)
    flight1 = across(leave)
    projection = project(1, found1, [projection])
    up_last, down_last, projection = stage(up_last, down_last, projection)
    feed = jnp.concatenate(
        [low_sum(rounded(up_pair(0) + up_far.astype(F32)), *up_last),
         low_sum(rounded(added(down_pair(0), *down_far)), down_last)], axis=0)
    feed_stay, feed_leave = split(feed, masks[0])
    g_rest, feed_leave, feed_stay = stage(g_rest, feed_leave, feed_stay)
    found = work(2, g_rest, g_rest_x, g_rest_c)
    feed_got, flight0, found = stage(along(feed_leave, masks[0]), flight0, found)
    got = sibling(found[4])
    terms0 = terms0 + [flight0]
    z_leave = leaving(terms0)
    feed_stay, feed_leave = split(low_sum(feed_stay, feed_got), masks[1])
    found, z_leave, feed_leave = stage(found, z_leave, feed_leave)
    terms0 = terms0 + [along(z_leave, masks[0])]
    feed_got = along(feed_leave, masks[1])
    biases = added(*columns)[:2].reshape(-1)
    lines = EXTRA * contexts
    biases = jnp.pad(biases, (0, lines * depth - biases.shape[0])).reshape(lines, depth).astype(BF16)
    if shards == 2:
        staying, leave = project(2, found, [projection], (order, biases, *outs))
        got, staying, leave = stage(got, staying, leave)
        attn_got = rotated(leave, "shard", 2, 1)
    else:
        projected = jnp.concatenate([project(2, found, [projection]), added(*outs)[None]], axis=0)
        stacked = jnp.stack([
            jnp.concatenate([projected[..., r * depth : (r + 1) * depth].reshape(4 * cols, depth).astype(BF16), biases], axis=0)
            for r in range(shards)])
        staying = lax.psum_scatter(stacked, "shard", scatter_dimension=0)
        attn_got = jnp.zeros_like(staying)
        got, staying = stage(got, staying)
    terms2 = [found[3], got]
    leave = leaving(terms2)
    half = leave.shape[0] // 2
    flight_first = across(leave[half:])
    flight = across(leave[:half])
    flight1, leave = stage(flight1, leave)
    terms1 = terms1 + [flight1]
    z1_leave = leaving(terms1)
    terms1 = terms1 + [along(z1_leave, masks[0])]
    terms0, z1_leave = stage(terms0, z1_leave)
    z0_leave = leaving(terms0)
    terms0 = terms0 + [along(z0_leave, masks[1])]
    feed_got, z0_leave = stage(feed_got, z0_leave)
    feed = low_sum(feed_stay, feed_got)
    feed_got = along(feed, masks[1])
    flight_first, feed = stage(flight_first, feed)
    z2_leave = leaving([t[: 2 * half] for t in terms2[:2]] + [jnp.concatenate([flight_first, flight_first], axis=0)])
    z2 = along(z2_leave, masks[0])
    terms1, z2_leave = stage(terms1, z2_leave)
    z1_leave = leaving(terms1)
    terms1 = terms1 + [along(z1_leave, masks[1])]
    attn_got, z1_leave = stage(attn_got, z1_leave)
    attn = split(low_sum(staying, attn_got), masks[0])
    attn_got = along(attn[1], masks[0])
    z2, flight, attn_leave = stage(z2, flight, attn[1])
    terms2 = terms2 + [flight, z2]
    z2_leave = leaving(terms2)
    z2 = along(z2_leave, masks[1])
    feed_got, terms0, z2_leave = stage(feed_got, terms0, z2_leave)
    feed = join(feed, feed_got, masks[1])
    feed_got = along(feed, masks[0])
    early = settle(0, terms0)
    attn_got, feed, early = stage(attn_got, feed, early)
    attn = split(low_sum(attn[0], attn_got), masks[1])
    attn_got = along(attn[1], masks[1])
    terms1, attn_leave = stage(terms1, attn[1])
    early = jnp.concatenate([early, settle(1, terms1)], axis=0)
    early_x = paired(early)[1]
    result, early = stage(result, early)
    result_x = paired(result)[1]
    z2, early = stage(z2, early)
    last = settle(2, terms2 + [z2])
    last_x = paired(last)[1]
    attn_got, early_x, last = stage(attn_got, early_x, last)
    attn = low_sum(attn[0], attn_got)
    attn_got = along(attn, masks[1])
    early = whole(early.reshape(early_x.shape), early_x)
    last_x, attn_got, early, result_x = stage(last_x, attn_got, early, result_x)
    attn = join(attn, attn_got, masks[1])
    attn_got = along(attn, masks[0])
    last = whole(last.reshape(last_x.shape), last_x)
    feed_got, last = stage(feed_got, last)
    feed = join(feed, feed_got, masks[0])
    outputs = whole(result.reshape(result_x.shape), result_x)
    attn_got, outputs, last, feed = stage(attn_got, outputs, last, feed)
    attn = join(attn, attn_got, masks[0])
    input_grad = jnp.concatenate([early, last], axis=0)

    feed, attn = feed.astype(F32), attn.astype(F32)
    vector_sums = feed[depth : depth + 7]
    bias_sums = attn[4 * cols :].reshape(-1)[: 2 * cols]
    matrices = attn[: 4 * cols].reshape(4, cols, depth)
    return (
        outputs,
        input_grad,
        matrices[0].T,
        bias_sums[:cols],
        matrices[1].T,
        matrices[2].T,
        bias_sums[cols:],
        matrices[3],
        vector_sums[0],
        vector_sums[1],
        vector_sums[2],
        feed[:depth],
        vector_sums[6],
        feed[depth + SUMS :].T,
        vector_sums[3],
        vector_sums[4],
        vector_sums[5],
    )


def solution(mesh):
    shards = mesh.shape["shard"]
    contexts = mesh.shape["context"]
    rows = P("shard", "context", None)
    into = P("shard", "tensor")
    onto = P("tensor", "shard")
    heads = P("tensor")
    return jax.shard_map(
        functools.partial(on_device, shards, contexts),
        mesh=mesh,
        in_specs=(rows, into, heads, into, into, heads, onto, P(), P(), P(), into, heads, onto, P(), P(), P(), rows),
        out_specs=(rows, rows, into, heads, into, into, heads, onto, P(), P(), P(), into, heads, onto, P(), P(), P()),
        check_vma=False,
    )
```

```python
import functools

import jax
import jax.numpy as jnp
from jax import lax
from jax.experimental import pallas as pl
from jax.experimental.pallas import tpu as pltpu
from jax.sharding import PartitionSpec as P

HEAD_DIM = 64
EPSILON = 1e-05
F32 = jnp.float32
BF16 = jnp.bfloat16
VMEM_LIMIT = 53 << 20
EXTRA = 16
SUMS = 64
SMEM_SPEC = pl.BlockSpec(memory_space=pltpu.SMEM)
ANY_SPEC = pl.BlockSpec(memory_space=pl.ANY)


def nn(a, b):
    return jnp.dot(a, b, preferred_element_type=F32)


def nt(a, b):
    return lax.dot_general(a, b, (((1,), (1,)), ((), ())), preferred_element_type=F32)


def vmem(n):
    return [pl.BlockSpec(memory_space=pltpu.VMEM)] * n


def params():
    return pltpu.CompilerParams(vmem_limit_bytes=VMEM_LIMIT)


def head_lanes(shape, head):
    lane = lax.broadcasted_iota(jnp.int32, shape, len(shape) - 1)
    return (lane >= head * HEAD_DIM) & (lane < (head + 1) * HEAD_DIM)


def divisor(size, most):
    while size % most:
        most //= 2
    return most


def slot_rows(places, slot, size):
    return pl.ds(pl.multiple_of(places[slot] * size, size), size)


def forward_body(heads, index, places, inputs, near, cross, sib, w_four, b_query, b_value, query, key, value, attended, log_total, keep, send, q_heads, own, sem):
    fetch = pltpu.make_async_copy(inputs.at[index], own, sem)
    fetch.start()
    part, width = own.shape
    cols = heads * HEAD_DIM
    quarter = part // 4
    factor = HEAD_DIM**-0.5
    w_query, w_key, w_value, w_out = (w_four.at[i] for i in range(4))
    row = part
    for piece in (near, cross, sib, own):
        size = piece.shape[0]
        if piece is own:
            fetch.wait()
            query[...] = ((nt(own[...], w_query[...]) + b_query[...]).astype(BF16).astype(F32) * factor).astype(BF16)
            row = 0
        step = divisor(size, 512)

        def project(i, carry, piece=piece, row=row, step=step):
            rows = piece[pl.ds(i * step, step), :]
            out = pl.ds(row + i * step, step)
            key[out, :] = nt(rows, w_key[...]).astype(BF16)
            value[out, :] = (nt(rows, w_value[...]) + b_value[...]).astype(BF16)
            return carry

        lax.fori_loop(0, size // step, project, 0)
        row += size
    total = key.shape[0]
    block = divisor(total, 1024)
    for head in range(heads):
        mask = head_lanes((part, cols), head)
        q_heads[head] = jnp.where(mask, query[...].astype(F32), 0.0).astype(BF16)
    ones = jnp.ones((16, block), BF16)

    def attend(i, carry):
        rows = pl.ds(pl.multiple_of(i * block, block), block)
        keys = key[rows, :]
        turned = value[rows, :].T
        out = []
        for head in range(heads):
            top, mixed = carry[head]
            scores = nt(keys, q_heads[head])
            new_top = jnp.maximum(top, jnp.max(scores, axis=0, keepdims=True))
            powers = jnp.exp(scores - new_top).astype(BF16)
            values = jnp.concatenate([turned[head * HEAD_DIM : (head + 1) * HEAD_DIM, :], ones], axis=0)
            out.append((new_top, mixed * jnp.exp(top - new_top) + nn(values, powers)))
        return tuple(out)

    start = tuple((jnp.full((1, part), -jnp.inf, F32), jnp.zeros((HEAD_DIM + 16, part), F32)) for _ in range(heads))
    final = lax.fori_loop(0, total // block, attend, start)
    mixes = []
    logs = []
    for top, mixed in final:
        count = mixed[HEAD_DIM : HEAD_DIM + 1, :]
        mixes.append(mixed[:HEAD_DIM, :] / count)
        logs.append(top + jnp.log(count))
    attended[...] = jnp.concatenate(mixes, axis=0).T.astype(BF16)
    log_total[...] = jnp.concatenate(logs + [jnp.zeros((8 - heads, part), F32)], axis=0)
    for out, first in ((keep, 0), (send, 2)):
        for j in range(2):
            rows = attended[slot_rows(places, first + j, quarter), :]
            out[j * quarter : (j + 1) * quarter, :] = nn(rows, w_out[...]).astype(BF16)


def backward_body(heads, nears, index, places, g_own, g_cross, g_sib, w_four, query, key, value, attended, log_total,
                  d_query, d_key, d_value, keep, send, d_out, sums, grad, q_heads, g_heads, dq_turned):
    part, cols = query.shape
    total = key.shape[0]
    quarter = part // 4
    factor = HEAD_DIM**-0.5
    w_query, w_key, w_value, w_out = (w_four.at[i] for i in range(4))
    begin = index * quarter
    middle = g_own.shape[0]
    grad[slot_rows(places, 0, quarter), :] = g_own[begin : begin + quarter, :]
    grad[slot_rows(places, 1, quarter), :] = g_cross[begin : begin + quarter, :]
    grad[slot_rows(places, 2, quarter), :] = g_sib[begin : begin + quarter, :]
    grad[slot_rows(places, 3, quarter), :] = g_sib[middle + begin : middle + begin + quarter, :]
    grad_heads = nt(grad[...], w_out[...]).astype(BF16)
    att = attended[...]
    d_out[...] = nn(att.T, grad[...])
    product = grad_heads.astype(F32) * att.astype(F32)
    picks = jnp.concatenate(
        [jnp.where(head_lanes((1, cols), h), 1.0, 0.0) for h in range(heads)]
        + [jnp.zeros((8 - heads, cols), F32)], axis=0)
    weighted = lax.dot_general(picks, product, (((1,), (1,)), ((), ())), precision=lax.Precision.HIGHEST,
                               preferred_element_type=F32)
    for h in range(heads):
        mask = head_lanes((part, cols), h)
        q_heads[h] = jnp.where(mask, query[...].astype(F32), 0.0).astype(BF16)
        g_heads[h] = jnp.where(mask, grad_heads.astype(F32), 0.0).astype(BF16)
    dq_turned[...] = jnp.zeros_like(dq_turned)
    block = divisor(total, 1024)

    def chunk(i, carry):
        rows = pl.ds(pl.multiple_of(i * block, block), block)
        keys = key[rows, :]
        values = value[rows, :]
        keys_turned = keys.T
        dk = jnp.zeros((block, cols), F32)
        dv = jnp.zeros((block, cols), F32)
        for h in range(heads):
            scores = nt(keys, q_heads[h])
            probs = jnp.exp(scores - log_total[h : h + 1, :])
            d_probs = nt(values, g_heads[h])
            d_scores = (probs * (d_probs - weighted[h : h + 1, :])).astype(BF16)
            dv = dv + nn(probs.astype(BF16), g_heads[h])
            dk = dk + nn(d_scores, q_heads[h])
            own = slice(h * HEAD_DIM, (h + 1) * HEAD_DIM)
            dq_turned[own, :] += nn(keys_turned[own, :], d_scores)
        d_key[rows, :] = dk.astype(BF16)
        d_value[rows, :] = dv.astype(BF16)
        return carry + jnp.sum(dv.astype(BF16).astype(F32), axis=0, keepdims=True)

    sum_value = lax.fori_loop(0, total // block, chunk, jnp.zeros((1, cols), F32))
    dq = (dq_turned[...] * factor).T.astype(BF16)
    d_query[...] = dq
    sums[...] = jnp.concatenate(
        [jnp.sum(dq.astype(F32), axis=0, keepdims=True), sum_value, jnp.zeros((6, cols), F32)], axis=0)

    def back(rows):
        return nn(d_key[rows, :], w_key[...]) + nn(d_value[rows, :], w_value[...])

    row = part
    for out, first in ((keep, 0), (send, 2)):
        for j in range(2):
            mine = slot_rows(places, first + j, quarter)
            begin = j * (quarter + nears)
            out[begin : begin + quarter, :] = (back(mine) + nn(d_query[mine, :], w_query[...])).astype(BF16)
            out[begin + quarter : begin + quarter + nears, :] = back(pl.ds(row, nears)).astype(BF16)
            row += nears


def attention_forward(places, index, inputs, near, cross, sib, w_four, b_query, b_value):
    part, width = inputs.shape[1:]
    cols = w_four.shape[1]
    heads = cols // HEAD_DIM
    total = part + near.shape[0] + cross.shape[0] + sib.shape[0]
    shape = jax.ShapeDtypeStruct
    return pl.pallas_call(
        functools.partial(forward_body, heads, index),
        out_shape=(
            shape((part, cols), BF16),
            shape((total, cols), BF16),
            shape((total, cols), BF16),
            shape((part, cols), BF16),
            shape((8, part), F32),
            shape((part // 2, width), BF16),
            shape((part // 2, width), BF16),
        ),
        in_specs=[SMEM_SPEC, ANY_SPEC] + vmem(6),
        out_specs=vmem(7),
        scratch_shapes=[pltpu.VMEM((heads, part, cols), BF16), pltpu.VMEM((part, width), BF16), pltpu.SemaphoreType.DMA(())],
        compiler_params=params(),
        cost_estimate=pl.CostEstimate(
            flops=4 * total * width * cols + 16 * heads * part * total * HEAD_DIM,
            bytes_accessed=2 * (total * width + 3 * total * cols),
            transcendentals=heads * part * total,
        ),
        name="attention_forward",
    )(places, inputs, near, cross, sib, w_four, b_query, b_value)


def attention_backward(places, index, g_own, g_cross, g_sib, w_four, query, key, value, attended, log_total):
    part, cols = query.shape
    width = w_four.shape[2]
    heads = cols // HEAD_DIM
    total = key.shape[0]
    nears = (total - part) // 4
    shape = jax.ShapeDtypeStruct
    return pl.pallas_call(
        functools.partial(backward_body, heads, nears, index),
        out_shape=(
            shape((part, cols), BF16),
            shape((total, cols), BF16),
            shape((total, cols), BF16),
            shape((total // 2, width), BF16),
            shape((total // 2, width), BF16),
            shape((cols, width), F32),
            shape((8, cols), F32),
        ),
        in_specs=[SMEM_SPEC] + vmem(9),
        out_specs=vmem(7),
        scratch_shapes=[
            pltpu.VMEM((part, width), BF16),
            pltpu.VMEM((heads, part, cols), BF16),
            pltpu.VMEM((heads, part, cols), BF16),
            pltpu.VMEM((cols, part), F32),
        ],
        compiler_params=params(),
        cost_estimate=pl.CostEstimate(
            flops=4 * total * width * cols + 40 * heads * part * total * HEAD_DIM,
            bytes_accessed=2 * (total * width + 5 * total * cols),
            transcendentals=heads * part * total,
        ),
        name="attention_backward",
    )(places, g_own, g_cross, g_sib, w_four, query, key, value, attended, log_total)


def gradients_body(index, adds, last, *refs):
    inputs, near, cross, sib, d_query, d_key, d_value = refs[:7]
    previous, refs = refs[7 : 7 + adds], refs[7 + adds :]
    if last:
        order, biases, d_outs = refs[0], refs[1], refs[2:5]
        staying, leaving, out, own, sem = refs[5:]
    else:
        out, own, sem = refs
    fetch = pltpu.make_async_copy(inputs.at[index], own, sem)
    fetch.start()
    row = own.shape[0]
    for piece in (near, cross, sib, own):
        if piece is own:
            fetch.wait()
            row = 0
        rows = slice(row, row + piece.shape[0])
        for slot, grad in ((1, d_key), (2, d_value)):
            part = nn(grad[rows, :].T, piece[...])
            if piece is not near:
                out[slot] += part
            elif previous:
                out[slot] = previous[0][slot] + part
            else:
                out[slot] = part
        row += piece.shape[0]
    part = nn(d_query[...].T, own[...])
    out[0] = previous[0][0] + part if previous else part
    if not last:
        return
    cols, width = part.shape
    depth = width // 2
    swap = order[4] == 1
    for slot in range(4):
        total = out[slot] if slot < 3 else d_outs[0][...] + d_outs[1][...] + d_outs[2][...]
        left, right = total[:, :depth], total[:, depth:]
        spot = slice(slot * cols, (slot + 1) * cols)
        staying[spot, :] = jnp.where(swap, right, left).astype(BF16)
        leaving[spot, :] = jnp.where(swap, left, right).astype(BF16)
    staying[4 * cols :, :] = biases[...]
    leaving[4 * cols :, :] = biases[...]


def attention_gradients(index, inputs, near, cross, sib, d_query, d_key, d_value, previous=(), final=()):
    cols = d_query.shape[1]
    width = inputs.shape[2]
    total = d_key.shape[0]
    shape = jax.ShapeDtypeStruct
    sums = shape((3, cols, width), F32)
    half = shape((4 * cols + final[1].shape[0], width // 2), BF16) if final else None
    scratch = [pltpu.VMEM(inputs.shape[1:], BF16), pltpu.SemaphoreType.DMA(())]
    return pl.pallas_call(
        functools.partial(gradients_body, index, len(previous), bool(final)),
        out_shape=(half, half) if final else sums,
        in_specs=[ANY_SPEC] + vmem(6 + len(previous)) + ([SMEM_SPEC] + vmem(4) if final else []),
        out_specs=vmem(2) if final else vmem(1)[0],
        scratch_shapes=[pltpu.VMEM(sums.shape, F32)] + scratch if final else scratch,
        compiler_params=params(),
        cost_estimate=pl.CostEstimate(
            flops=4 * total * cols * width, bytes_accessed=2 * total * (width + 2 * cols), transcendentals=0
        ),
        name="attention_gradients",
    )(inputs, near, cross, sib, d_query, d_key, d_value, *previous, *final)


def rows_mean(a):
    return jnp.mean(a, axis=-1, keepdims=True)


def norm(values):
    centred = values - rows_mean(values)
    inverse = lax.rsqrt(rows_mean(centred * centred) + EPSILON)
    return centred * inverse, inverse


def norm_back(scaled, normed, inverse):
    return inverse * (scaled - rows_mean(scaled) - normed * rows_mean(scaled * normed))


def col_sum(a):
    return jnp.sum(a, axis=0, keepdims=True)


def feed_body(blocks, pieces, seqs, order, cotangents, *refs):
    count = blocks * pieces
    up_pieces, down_pieces, refs = refs[:count], refs[count : 2 * count], refs[2 * count :]
    shard = order[4]
    mine, keeps, gots, rests = (refs[i * seqs : (i + 1) * seqs] for i in range(4))
    vectors, result, grad_first_attn, grad_rest_attn = refs[4 * seqs : 4 * seqs + 4]
    (grad_low, act, d_inner, d_ffn, low, sums,
     up, down, bias, slope, cotangent, sems, cot_sems) = refs[4 * seqs + 4 :]
    rows, width = result.shape
    quarter = rows // seqs
    depth = width // pieces
    copies = []
    for b in range(blocks):
        for p in range(pieces):
            spot = pl.ds(pl.multiple_of(lax.rem(shard + p, pieces) * depth, depth), depth)
            source = up_pieces[b * pieces + p].at[pl.ds(0, depth), :]
            copies.append(pltpu.make_async_copy(source, up.at[b, spot, :], sems.at[b, p, 0]))
            copies.append(pltpu.make_async_copy(down_pieces[b * pieces + p], down.at[b, spot, :], sems.at[b, p, 1]))
        source = up_pieces[b * pieces].at[pl.ds(depth, EXTRA), :]
        copies.append(pltpu.make_async_copy(source, bias.at[b], sems.at[b, pieces, 0]))
    for i in range(seqs):
        source = cotangents.at[i, slot_rows(order, 0, quarter), :]
        copies.append(pltpu.make_async_copy(source, cotangent.at[pl.ds(i * quarter, quarter), :], cot_sems.at[i]))
    for copy in copies:
        copy.start()
    inputs = jnp.concatenate([r[...].astype(F32) for r in mine], axis=0)
    branch = jnp.concatenate(
        [keeps[i][:quarter, :].astype(F32) + gots[i][:quarter, :].astype(F32) + rests[i][...].astype(F32) for i in range(seqs)],
        axis=0)
    b_out, gain_one, bias_one, b_down, gain_two, bias_two = (vectors[i : i + 1, :] for i in range(6))
    pre = inputs + branch + b_out
    normed_one, inverse_one = norm(pre)
    first = normed_one * gain_one + bias_one
    first_low = first.astype(BF16)
    low[...] = first_low
    for copy in copies:
        copy.wait()

    def ahead(b, total):
        parts = bias[b].astype(F32)
        b_hidden = (parts[0:1, :] + parts[1:2, :]) + parts[2:3, :]
        inner = nn(first_low, up[b]) + b_hidden
        shape = 0.5 * (1.0 + lax.erf(inner * (0.5**0.5)))
        act_low = (inner * shape).astype(BF16)
        act[b] = act_low
        slope[b] = shape + inner * (jnp.exp(-0.5 * inner * inner) * 0.3989422804014327)
        return total + nt(act_low, down[b])

    ffn = lax.fori_loop(0, blocks, ahead, jnp.zeros((rows, width), F32))
    normed_two, inverse_two = norm(first + ffn + b_down)
    result[...] = (normed_two * gain_two + bias_two).astype(BF16)
    grad = cotangent[...].astype(F32)
    grad_second = norm_back(grad * gain_two, normed_two, inverse_two)
    grad_ffn = grad_second.astype(BF16)
    d_ffn[...] = grad_ffn

    def astern(b, total):
        grad_inner = (nn(grad_ffn, down[b]) * slope[b]).astype(BF16)
        d_inner[b] = grad_inner
        return total + nt(grad_inner, up[b])

    grad_first = lax.fori_loop(0, blocks, astern, grad_second)
    grad_pre = norm_back(grad_first * gain_one, normed_one, inverse_one)
    grad_low[...] = grad_pre
    grad_first_attn[...] = grad_pre[:quarter, :].astype(BF16)
    grad_rest_attn[...] = grad_pre[quarter:, :].astype(BF16)
    sums[...] = jnp.concatenate(
        [col_sum(grad_pre), col_sum(grad_first * normed_one), col_sum(grad_first), col_sum(grad_second),
         col_sum(grad * normed_two), col_sum(grad), jnp.zeros((2, width), F32)], axis=0)


def feed_forward(order, ups, downs, cotangents, mine, keeps, gots, rests, vectors):
    seqs = len(mine)
    blocks = len(ups)
    pieces = len(ups[0])
    flat = [w for block in ups for w in block] + [w for block in downs for w in block]
    quarter, width = mine[0].shape
    rows = quarter * seqs
    hidden = ups[0][0].shape[-1]
    shape = jax.ShapeDtypeStruct
    return pl.pallas_call(
        functools.partial(feed_body, blocks, pieces, seqs),
        out_shape=(
            shape((rows, width), BF16),
            shape((quarter, width), BF16),
            shape((rows - quarter, width), BF16),
            shape((rows, width), F32),
            shape((blocks, rows, hidden), BF16),
            shape((blocks, rows, hidden), BF16),
            shape((rows, width), BF16),
            shape((rows, width), BF16),
            shape((8, width), F32),
        ),
        in_specs=[SMEM_SPEC] + [ANY_SPEC] * (1 + len(flat)) + vmem(4 * seqs + 1),
        out_specs=vmem(9),
        scratch_shapes=[
            pltpu.VMEM((blocks, width, hidden), BF16),
            pltpu.VMEM((blocks, width, hidden), BF16),
            pltpu.VMEM((blocks, EXTRA, hidden), BF16),
            pltpu.VMEM((blocks, rows, hidden), F32),
            pltpu.VMEM((rows, width), BF16),
            pltpu.SemaphoreType.DMA((blocks, pieces + 1, 2)),
            pltpu.SemaphoreType.DMA((seqs,)),
        ],
        compiler_params=params(),
        cost_estimate=pl.CostEstimate(
            flops=8 * rows * width * hidden * blocks,
            bytes_accessed=6 * width * hidden * blocks,
            transcendentals=2 * rows * hidden * blocks,
        ),
        name="feed_forward",
    )(order, cotangents, *flat, *mine, *keeps, *gots, *rests, vectors)


def feed_gradients_body(pieces, order, act, d_inner, d_ffn, low, sums, ups, downs, low_turned, ffn_turned):
    depth = low.shape[1] // pieces
    hidden = act.shape[-1]
    shard = order[4]
    grad_inner = d_inner[0]

    @pl.when(pl.program_id(0) == 0)
    def _():
        low_turned[...] = low[...].T
        ffn_turned[...] = d_ffn[...].T

    up = nn(low_turned[...], grad_inner)
    down = nn(ffn_turned[...], act[0])
    extra = jnp.concatenate(
        [sums[:6, :], col_sum(grad_inner.astype(F32)), jnp.zeros((SUMS - 7, hidden), F32)], axis=0).astype(BF16)
    for p in range(pieces):
        spot = lax.rem(p - shard + pieces, pieces)
        ups[0, spot, :depth, :] = up[p * depth : (p + 1) * depth, :].astype(BF16)
        ups[0, spot, depth:, :] = extra
        downs[0, spot, :, :] = down[p * depth : (p + 1) * depth, :].astype(BF16)


def feed_gradients(pieces, first, order, act, d_inner, d_ffn, low, sums):
    blocks, rows, hidden = act.shape
    width = low.shape[1]
    depth = width // pieces
    shape = jax.ShapeDtypeStruct
    pick = pl.BlockSpec((1, rows, hidden), lambda i, order: (first + i, 0, 0))
    whole = pl.BlockSpec((rows, width), lambda i, order: (0, 0))
    return pl.pallas_call(
        functools.partial(feed_gradients_body, pieces),
        out_shape=(shape((2, pieces, depth + SUMS, hidden), BF16), shape((2, pieces, depth, hidden), BF16)),
        grid_spec=pltpu.PrefetchScalarGridSpec(
            num_scalar_prefetch=1,
            grid=(2,),
            in_specs=[pick, pick, whole, whole, pl.BlockSpec((8, width), lambda i, order: (0, 0))],
            out_specs=[
                pl.BlockSpec((1, pieces, depth + SUMS, hidden), lambda i, order: (i, 0, 0, 0)),
                pl.BlockSpec((1, pieces, depth, hidden), lambda i, order: (i, 0, 0, 0)),
            ],
            scratch_shapes=[pltpu.VMEM((width, rows), BF16), pltpu.VMEM((width, rows), BF16)],
        ),
        compiler_params=params(),
        cost_estimate=pl.CostEstimate(
            flops=8 * rows * width * hidden, bytes_accessed=8 * width * hidden, transcendentals=0
        ),
        name="feed_gradients",
    )(order, act, d_inner, d_ffn, low, sums)


def rotated(value, axis, count, shift):
    return lax.ppermute(value, axis, [(i, (i + shift) % count) for i in range(count)])


def across(value):
    return lax.ppermute(value, "tensor", [(i, i ^ 2) for i in range(4)])


def sibling(value):
    return lax.ppermute(value, "tensor", [(i, i ^ 1) for i in range(4)])


def stage(*values):
    return lax.optimization_barrier(values)


def added(*values):
    total = values[0].astype(F32)
    for value in values[1:]:
        total = total + value.astype(F32)
    return total


def rounded(value):
    return lax.reduce_precision(value, 8, 7)


def low_sum(*values):
    return added(*values).astype(BF16)


def thirds(value):
    high = value.astype(BF16)
    rest = value - high.astype(F32)
    middle = rest.astype(BF16)
    return high, middle, (rest - middle.astype(F32)).astype(BF16)


def on_device(shards, contexts, inputs, w_query, b_query, w_key, w_value, b_value, w_out, b_out,
              first_gain, first_bias, w_hidden, b_hidden, w_down, b_down, second_gain, second_bias, cotangent):
    seqs, part, width = inputs.shape
    cols = w_query.shape[1]
    quarter = part // 4
    depth = width // shards
    shard = lax.axis_index("shard")
    context = lax.axis_index("context")
    tensor = lax.axis_index("tensor")
    masks = [1 << i for i in range(contexts.bit_length() - 1)]
    hops = len(masks)
    places = jnp.stack([tensor ^ flip for flip in (0, 2, 1, 3)]).astype(jnp.int32)
    order = jnp.concatenate([places, shard[None].astype(jnp.int32)])

    def along(value, mask):
        return lax.ppermute(value, "context", [(i, i ^ mask) for i in range(contexts)])

    def from_shards(value):
        return [rotated(value, "shard", shards, -r) for r in range(1, shards)]

    def to_shards(parts):
        return [rotated(value, "shard", shards, r) for r, value in enumerate(parts, 1)]

    mine = [lax.dynamic_slice_in_dim(inputs[s], tensor * quarter, quarter, axis=0) for s in range(seqs)]
    nears = [[m] for m in mine]
    cross = [None] * seqs
    four = jnp.stack([w_query.T, w_key.T, w_value.T, w_out])
    line = lax.broadcasted_iota(jnp.int32, (EXTRA, w_hidden.shape[1]), 0)
    biases = jnp.zeros((EXTRA, w_hidden.shape[1]), BF16)
    for i, third in enumerate(thirds(b_hidden)):
        biases = jnp.where(line == i, third[None], biases)
    up_own = jnp.concatenate([w_hidden, lax.optimization_barrier(biases)], axis=0)
    down_own = w_down.T
    vectors = jnp.concatenate([b_out, first_gain, first_bias, b_down, second_gain, second_bias]).reshape(6, width)
    up_x = up_y = up_xy = down_x = down_y = down_xy = other = None
    up_beside, down_beside = {}, {}
    saved = [None] * seqs
    sibs = [None] * seqs
    joined = [None] * seqs
    held = [None] * seqs
    gots = []
    rests = []
    rest = None
    four_all = None
    for j in range(hops + 1 + seqs):
        flights = {}
        found = ()
        s = j - hops - 1
        if s >= 0:
            sibs[s] = sibling(jnp.concatenate([joined[s], cross[s]], axis=0))
            if s >= 1:
                gots.append(sibling(held[s - 1][1]))
                rest = low_sum(held[s - 1][0][quarter:], gots[-1][quarter:])
                sibs[s], rest = stage(sibs[s], rest)
            if s >= 2:
                flights["rest"] = [across(r) for r in rests + [rest]]
            query, key, value, attended, log_total, keep, send = attention_forward(
                places, s, inputs, joined[s], cross[s], sibs[s], four_all, b_query[None], b_value[None])
            saved[s] = (query, key, value, attended, log_total)
            found = (keep, send)
        for q in range(seqs):
            k = j - q
            if 0 <= k < hops:
                flights[f"z{q}"] = along(jnp.concatenate(nears[q], axis=0), masks[hops - 1 - k])
            if k == hops:
                joined[q] = jnp.concatenate(nears[q][1:], axis=0)
                flights[f"x{q}"] = across(joined[q])
        if j == hops - 1:
            flights["up_x"] = across(up_own)
            flights["four"] = from_shards(four)
        if j == hops:
            flights["up_y"] = from_shards(up_own)
            flights["four_all"] = four_all
        if j == hops + 1:
            flights["down_y"] = from_shards(down_own)
            flights["down_x1"] = across(stage(down_own[: depth // 2], sibs[0])[0])
        if j == hops + 2:
            flights["up_xy"] = from_shards(up_x)
            flights["up_c"] = sibling(up_own)
            flights["down_x2"] = across(stage(down_own[depth // 2 :], sibs[1])[0])
        if j == hops + 3:
            flights["down_xy"] = from_shards(down_x)
            flights["down_c"] = sibling(down_own)
        flights, found, four, up_own, down_own, vectors, nears, up_x, up_y, up_xy, down_x, down_y = stage(
            flights, found, four, up_own, down_own, vectors, nears, up_x, up_y, up_xy, down_x, down_y)
        for q in range(seqs):
            if f"z{q}" in flights:
                nears[q] = nears[q] + [flights[f"z{q}"]]
            if f"x{q}" in flights:
                cross[q] = flights[f"x{q}"]
        if s >= 0:
            held[s] = found
            if s >= 1:
                rests.append(rest)
            if s >= 2:
                rests = flights["rest"]
        if j == hops - 1:
            up_x, other = flights["up_x"], flights["four"]
            if shards == 2:
                left = jnp.where(shard == 0, four, other[0])
                right = jnp.where(shard == 0, other[0], four)
                four_all = jnp.concatenate([left, right], axis=2)
            else:
                four_all = lax.all_gather(four, "shard", axis=2, tiled=True)
        if j == hops:
            up_y, four_all = flights["up_y"], flights["four_all"]
        if j == hops + 1:
            down_x1, down_y = flights["down_x1"], flights["down_y"]
        if j == hops + 2:
            up_xy, up_c = flights["up_xy"], flights["up_c"]
            down_x = jnp.concatenate([down_x1, flights["down_x2"]], axis=0)
        if j == hops + 3:
            down_xy, down_c = flights["down_xy"], flights["down_c"]
    gots.append(sibling(held[seqs - 1][1]))
    rests.append(across(low_sum(held[seqs - 1][0][quarter:], gots[-1][quarter:])))
    ups = [[up_own] + up_y, [up_x] + up_xy, [up_c] + [sibling(w) for w in up_y], [sibling(w) for w in [up_x] + up_xy]]
    downs = [[down_own] + down_y, [down_x] + down_xy, [down_c] + [sibling(w) for w in down_y],
             [sibling(w) for w in [down_x] + down_xy]]
    result, g_first, g_rest, grad_low, act, d_inner, d_ffn, low, sums = feed_forward(
        order, ups, downs, cotangent, mine, [h[0] for h in held], gots, rests, vectors)

    up_send, down_send = feed_gradients(shards, 2, order, act, d_inner, d_ffn, low, sums)
    g_first_x, up_send, down_send, d_inner, g_rest = stage(across(g_first), up_send, down_send, d_inner, g_rest)
    up_keep, down_keep = feed_gradients(shards, 0, order, act, d_inner, d_ffn, low, sums)
    g_first_c, up_got, down_got, up_keep, down_keep, result = stage(
        sibling(jnp.concatenate([g_first, g_first_x], axis=0)), sibling(up_send), sibling(down_send),
        up_keep, down_keep, result)

    def up_pair(p):
        return rounded(added(up_keep[0, p], up_got[0, p]))

    def down_pair(slot):
        return rounded(added(down_keep[slot, 0], down_got[slot, 0]))

    def project(s, found, previous=(), final=()):
        return attention_gradients(s, inputs, joined[s], cross[s], sibs[s], *found[:3], previous, final)

    def leaving(terms):
        half = terms[-1].shape[0] // 2
        return low_sum(*[t[half : 2 * half] for t in terms])

    def settle(s, terms):
        return low_sum(grad_low[s * quarter : (s + 1) * quarter], *[t[:quarter] for t in terms])

    def paired(parts):
        own = parts.reshape(parts.shape[0] // quarter, quarter, width)
        return own, across(own)

    def whole(own, swapped):
        count = own.shape[0]
        beside = sibling(jnp.stack([own, swapped]))
        row, side = tensor // 2, tensor % 2
        blocks = []
        for r in range(2):
            for c in range(2):
                here = jnp.where(side == c, own, beside[0])
                there = jnp.where(side == c, swapped, beside[1])
                blocks.append(jnp.where(row == r, here, there))
        return jnp.stack(blocks, axis=1).reshape(count, part, width)

    def split(value, mask):
        half = value.shape[0] // 2
        bit = (context & mask) // mask
        stay = lax.dynamic_slice_in_dim(value, bit * half, half, axis=0)
        return stay, lax.dynamic_slice_in_dim(value, (1 - bit) * half, half, axis=0).astype(BF16)

    def join(value, got, mask):
        lower = (context & mask) == 0
        return jnp.concatenate([jnp.where(lower, value, got), jnp.where(lower, got, value)], axis=0)

    columns = []
    outs = []
    projections = []

    def work(s, *gradient):
        found = attention_backward(places, max(s - 1, 0), *gradient, four_all, *saved[s])
        columns.append(found[6])
        outs.append(found[5])
        return found

    up_leave = [low_sum(up_keep[1, p], up_got[1, p]) for p in range(1, shards)]
    down_leave = [low_sum(down_keep[1, p], down_got[1, p]) for p in range(1, shards)]
    g_first, g_rest, g_rest_x, up_leave, down_leave = stage(g_first, g_rest, across(g_rest), up_leave, down_leave)
    found0 = work(0, g_first, g_first_x, g_first_c)
    up_far, down_far, g_rest_c, found0 = stage(
        [across(u) for u in up_leave], to_shards(down_leave), sibling(jnp.concatenate([g_rest, g_rest_x], axis=0)), found0)
    got0 = sibling(found0[4])
    up_second = [low_sum(up_pair(p), up_far[p - 1]) for p in range(1, shards)]
    down_second = low_sum(down_pair(1), *down_far)
    up_leave = low_sum(up_keep[1, 0], up_got[1, 0])
    down_leave = [low_sum(down_keep[0, p], down_got[0, p]) for p in range(1, shards)]
    g_rest, up_second, down_second, up_leave, down_leave = stage(g_rest, up_second, down_second, up_leave, down_leave)
    found1 = work(1, g_rest, g_rest_x, g_rest_c)
    up_far, down_far, got0, found1 = stage(across(up_leave), to_shards(down_leave), got0, found1)
    terms0 = [found0[3], got0]
    leave = leaving(terms0)
    found0, leave, up_second, down_second, found1 = stage(found0, leave, up_second, down_second, found1)
    up_last = to_shards(up_second)
    down_last = across(down_second)
    flight0 = across(leave)
    projection = project(0, found0)
    got1, projection = stage(sibling(found1[4]), projection)
    terms1 = [found1[3], got1]
    leave = leaving(terms1)
    found1, leave = stage(found1, leave)
    flight1 = across(leave)
    projection = project(1, found1, [projection])
    up_last, down_last, projection = stage(up_last, down_last, projection)
    feed = jnp.concatenate(
        [low_sum(rounded(up_pair(0) + up_far.astype(F32)), *up_last),
         low_sum(rounded(added(down_pair(0), *down_far)), down_last)], axis=0)
    feed_stay, feed_leave = split(feed, masks[0])
    g_rest, feed_leave, feed_stay = stage(g_rest, feed_leave, feed_stay)
    found = work(2, g_rest, g_rest_x, g_rest_c)
    feed_got, flight0, found = stage(along(feed_leave, masks[0]), flight0, found)
    got = sibling(found[4])
    terms0 = terms0 + [flight0]
    z_leave = leaving(terms0)
    feed_stay, feed_leave = split(low_sum(feed_stay, feed_got), masks[1])
    found, z_leave, feed_leave = stage(found, z_leave, feed_leave)
    terms0 = terms0 + [along(z_leave, masks[0])]
    feed_got = along(feed_leave, masks[1])
    biases = added(*columns)[:2].reshape(-1)
    lines = EXTRA * contexts
    biases = jnp.pad(biases, (0, lines * depth - biases.shape[0])).reshape(lines, depth).astype(BF16)
    if shards == 2:
        staying, leave = project(2, found, [projection], (order, biases, *outs))
        got, staying, leave = stage(got, staying, leave)
        attn_got = rotated(leave, "shard", 2, 1)
    else:
        projected = jnp.concatenate([project(2, found, [projection]), added(*outs)[None]], axis=0)
        stacked = jnp.stack([
            jnp.concatenate([projected[..., r * depth : (r + 1) * depth].reshape(4 * cols, depth).astype(BF16), biases], axis=0)
            for r in range(shards)])
        staying = lax.psum_scatter(stacked, "shard", scatter_dimension=0)
        attn_got = jnp.zeros_like(staying)
        got, staying = stage(got, staying)
    terms2 = [found[3], got]
    leave = leaving(terms2)
    half = leave.shape[0] // 2
    flight_first = across(leave[half:])
    flight = across(leave[:half])
    flight1, leave = stage(flight1, leave)
    terms1 = terms1 + [flight1]
    z1_leave = leaving(terms1)
    terms1 = terms1 + [along(z1_leave, masks[0])]
    terms0, z1_leave = stage(terms0, z1_leave)
    z0_leave = leaving(terms0)
    terms0 = terms0 + [along(z0_leave, masks[1])]
    feed_got, z0_leave = stage(feed_got, z0_leave)
    feed = low_sum(feed_stay, feed_got)
    feed_got = along(feed, masks[1])
    flight_first, feed = stage(flight_first, feed)
    z2_leave = leaving([t[: 2 * half] for t in terms2[:2]] + [jnp.concatenate([flight_first, flight_first], axis=0)])
    z2 = along(z2_leave, masks[0])
    terms1, z2_leave = stage(terms1, z2_leave)
    z1_leave = leaving(terms1)
    terms1 = terms1 + [along(z1_leave, masks[1])]
    attn_got, z1_leave = stage(attn_got, z1_leave)
    attn = split(low_sum(staying, attn_got), masks[0])
    attn_got = along(attn[1], masks[0])
    z2, flight, attn_leave = stage(z2, flight, attn[1])
    terms2 = terms2 + [flight, z2]
    z2_leave = leaving(terms2)
    z2 = along(z2_leave, masks[1])
    feed_got, terms0, z2_leave = stage(feed_got, terms0, z2_leave)
    feed = join(feed, feed_got, masks[1])
    feed_got = along(feed, masks[0])
    early = settle(0, terms0)
    attn_got, feed, early = stage(attn_got, feed, early)
    attn = split(low_sum(attn[0], attn_got), masks[1])
    attn_got = along(attn[1], masks[1])
    terms1, attn_leave = stage(terms1, attn[1])
    early = jnp.concatenate([early, settle(1, terms1)], axis=0)
    early_x = paired(early)[1]
    result, early = stage(result, early)
    result_x = paired(result)[1]
    z2, early = stage(z2, early)
    last = settle(2, terms2 + [z2])
    last_x = paired(last)[1]
    attn_got, early_x, last = stage(attn_got, early_x, last)
    attn = low_sum(attn[0], attn_got)
    attn_got = along(attn, masks[1])
    early = whole(early.reshape(early_x.shape), early_x)
    last_x, attn_got, early, result_x = stage(last_x, attn_got, early, result_x)
    attn = join(attn, attn_got, masks[1])
    attn_got = along(attn, masks[0])
    last = whole(last.reshape(last_x.shape), last_x)
    feed_got, last = stage(feed_got, last)
    feed = join(feed, feed_got, masks[0])
    outputs = whole(result.reshape(result_x.shape), result_x)
    input_grad = jnp.concatenate([early, last], axis=0)
    feed = feed.astype(F32)
    vector_sums = feed[depth : depth + 7]
    up_grad = feed[:depth]
    down_grad = feed[depth + SUMS :].T
    attn_got, outputs, input_grad, vector_sums, up_grad, down_grad = stage(
        attn_got, outputs, input_grad, vector_sums, up_grad, down_grad)
    attn = join(attn, attn_got, masks[0])

    attn = attn.astype(F32)
    bias_sums = attn[4 * cols :].reshape(-1)[: 2 * cols]
    matrices = attn[: 4 * cols].reshape(4, cols, depth)
    return (
        outputs,
        input_grad,
        matrices[0].T,
        bias_sums[:cols],
        matrices[1].T,
        matrices[2].T,
        bias_sums[cols:],
        matrices[3],
        vector_sums[0],
        vector_sums[1],
        vector_sums[2],
        up_grad,
        vector_sums[6],
        down_grad,
        vector_sums[3],
        vector_sums[4],
        vector_sums[5],
    )


def solution(mesh):
    shards = mesh.shape["shard"]
    contexts = mesh.shape["context"]
    rows = P("shard", "context", None)
    into = P("shard", "tensor")
    onto = P("tensor", "shard")
    heads = P("tensor")
    return jax.shard_map(
        functools.partial(on_device, shards, contexts),
        mesh=mesh,
        in_specs=(rows, into, heads, into, into, heads, onto, P(), P(), P(), into, heads, onto, P(), P(), P(), rows),
        out_specs=(rows, rows, into, heads, into, into, heads, onto, P(), P(), P(), into, heads, onto, P(), P(), P()),
        check_vma=False,
    )
```
